32 devices in a mesh: user: 4 (over y, core), pool: 8 (over z, x).
Axes of the slice: x: 2, y: 2, z: 4, core: 2. Of those that a mesh axis runs over, the one named last changes fastest.
Arguments:
- item_feats: bfloat16 [16384, 512], P(('user', 'pool')), may hold values from -6 to 6
- w_in: bfloat16 [512, 2048], replicated, may hold values from -0.25 to 0.25
- bias_in: float32 [2048], replicated, may hold values from -3 to 3
- w_out: bfloat16 [2048, 512], replicated, may hold values from -0.125 to 0.125
- bilinear: bfloat16 [512, 512], replicated, may hold values from -0.25 to 0.25
- fetch_table: int32 [32, 32, 16], P(None, ('user', 'pool')), may hold values from 0 to 511, as said below
- hist_index: int32 [1024, 256], P(('user', 'pool')), may hold values from 0 to 511
- hist_len: int32 [1024], P(('user', 'pool')), may hold values from 32 to 256
- route_init: float32 [1024, 4, 256], P(('user', 'pool')), may hold values from -6 to 6
- label_index: int32 [1024], P(('user', 'pool')), may hold values from 0 to 511
- label_ids: int32 [1024], P(('user', 'pool')), may hold values from 0 to 1048575
- label_counts: int32 [1024], P(('user', 'pool')), may hold values from 1 to 15
- neg_feats: bfloat16 [4096, 512], P(('user', 'pool')), may hold values from -6 to 6
- neg_ids: int32 [4096], P(('user', 'pool')), may hold values from 0 to 1048575
- neg_counts: int32 [4096], P(('user', 'pool')), may hold values from 1 to 15
Outputs:
- interests: float32 [1024, 2048], P(('user', 'pool'))
- user_loss: float32 [1024], P(('user', 'pool'))
The draws below stay inside these ranges and needn't reach their ends.
Inputs may be any that keep to these rules, and one draw needn't show every extreme that they name: fetch_table[b, s, :] names 16 different rows of item block s.
All inputs are finite; a program needn't handle non-finite values.
Results may differ from the reference program's by a relative error of at most 0.0011.
Values may be sent and summed in bfloat16 or wider, within the bound.
No kernel may reach another device: no remote copies, remote signals or barrier semaphores. Data moves between devices by JAX's collectives and lax.ppermute only.
A program may use at most 192 MiB of HBM per device.

```python
import math
import jax
import jax.numpy as jnp
import numpy as np
from jax import lax

D = 512
FF = 2048
INTERESTS = 4
HIST = 256
ITERS = 3
VOCAB = 1048576
ITEMS_DEV = 512
CAP = 16
USERS_DEV = 32
ITEMS = 16384
USERS = 1024
NEG = 4096
SLOTS = 512
DEVICES = 32


def spread_counts(seed_key, shape):
    power_key, rest_key = jax.random.split(seed_key)
    exponent = jax.random.randint(power_key, shape, 0, 4)
    power_base = jnp.left_shift(jnp.ones(shape, jnp.int32), exponent)
    return power_base + jax.random.randint(rest_key, shape, 0, power_base)


def draw_label_counts(key, part):
    return spread_counts(jax.random.fold_in(key, 12), (USERS,)).astype(jnp.int32)


def draw_neg_counts(key, part):
    return spread_counts(jax.random.fold_in(key, 11), (NEG,)).astype(jnp.int32)


def draw_fetch_table(key, part):
    scores = jax.random.randint(jax.random.fold_in(key, 13), (DEVICES, DEVICES, ITEMS_DEV), 0, 262144)
    scores = scores * ITEMS_DEV + lax.broadcasted_iota(jnp.int32, (DEVICES, DEVICES, ITEMS_DEV), 2)
    chosen = lax.top_k(scores, CAP)[1]
    return chosen.astype(jnp.int32)


def place_ends(array, own_key, smallest, largest):
    place = [jax.random.randint(jax.random.fold_in(own_key, axis), (), 0, length) for axis, length in enumerate(array.shape)]
    longest = array.shape.index(max(array.shape))
    beside = place[:longest] + [(place[longest] + 1) % array.shape[longest]] + place[longest + 1:]
    return array.at[tuple(place)].set(smallest).at[tuple(beside)].set(largest)


def levels(own_key, extent, cuts, low, high):
    def one(axis_at, shards_of):
        steps = jax.random.uniform(jax.random.fold_in(jax.random.fold_in(own_key, 6), axis_at), (shards_of,), jnp.float32, low / len(cuts), high / len(cuts))
        return jnp.repeat(jnp.exp(steps), extent[axis_at] // shards_of).reshape((-1,) + (1,) * (len(extent) - axis_at - 1))

    factor_of = one(*cuts[0])
    for cut in cuts[1:]:
        factor_of = factor_of * one(*cut)
    return factor_of


def ranked_wide(own_key, extent, amount, skew):
    loads = [min(1 << octave, amount + 1 - (1 << octave)) * (1 << 20) // math.isqrt((1 << octave) ** skew) + 1 for octave in range((amount + 1).bit_length()) if 1 << octave <= amount]
    width = 1 + sum(loads) // (1 << 30)
    listing = np.cumsum(np.array([max(1, weight // width) for weight in loads]))
    lot = jax.random.randint(jax.random.fold_in(own_key, 1), extent, 0, int(listing[len(loads) - 1]))
    start = jnp.left_shift(1, jnp.searchsorted(jnp.asarray(listing, jnp.int32), lot, side="right").astype(jnp.int32))
    rank = start - 1 + jax.random.randint(jax.random.fold_in(own_key, 4), extent, 0, 1 << 30) % jnp.minimum(start, amount + 1 - start)
    return jax.random.permutation(jax.random.fold_in(own_key, 2), amount)[rank].astype(jnp.int32)


def centred(key, dims, width, limit, cuts=(), kind=jnp.bfloat16):
    values = width * jax.random.normal(key, dims, jnp.float32)
    if cuts:
        values = values * levels(key, dims, cuts, -0.22, 0.18)
    return jnp.clip(values, -limit, limit).astype(kind)


def setup_inputs(seed: int = 0) -> dict:
    arg_keys = jax.random.split(jax.random.key(seed), 16)
    return {
        "item_feats": centred(arg_keys[0], (ITEMS, D), 1.0, 6.0, ((0, 32),)),
        "w_in": centred(arg_keys[1], (D, FF), D ** -0.5, 0.25),
        "bias_in": centred(arg_keys[2], (FF,), 0.5, 3.0, (), jnp.float32),
        "w_out": centred(arg_keys[3], (FF, D), FF ** -0.5, 0.125),
        "bilinear": centred(arg_keys[4], (D, D), D ** -0.5, 0.25),
        "fetch_table": draw_fetch_table(jax.random.fold_in(arg_keys[15], 71), 0),
        "hist_index": place_ends(jax.random.randint(arg_keys[6], (USERS, HIST), 0, SLOTS), jax.random.fold_in(arg_keys[6], 1), 0, SLOTS - 1).astype(jnp.int32),
        "hist_len": place_ends(jax.random.randint(arg_keys[7], (USERS,), HIST // 8, HIST + 1), jax.random.fold_in(arg_keys[7], 1), HIST // 8, HIST).astype(jnp.int32),
        "route_init": centred(arg_keys[8], (USERS, INTERESTS, HIST), 1.0, 6.0, ((0, 32),), jnp.float32),
        "label_index": place_ends(jax.random.randint(arg_keys[9], (USERS,), 0, SLOTS), jax.random.fold_in(arg_keys[9], 1), 0, SLOTS - 1).astype(jnp.int32),
        "label_ids": place_ends(ranked_wide(arg_keys[10], (USERS,), VOCAB, 2), jax.random.fold_in(arg_keys[10], 3), 0, VOCAB - 1).astype(jnp.int32),
        "label_counts": draw_label_counts(jax.random.fold_in(arg_keys[15], 71), 0),
        "neg_feats": centred(arg_keys[12], (NEG, D), 1.0, 6.0, ((0, 32),)),
        "neg_ids": place_ends(ranked_wide(arg_keys[13], (NEG,), VOCAB, 2), jax.random.fold_in(arg_keys[13], 3), 0, VOCAB - 1).astype(jnp.int32),
        "neg_counts": draw_neg_counts(jax.random.fold_in(arg_keys[15], 71), 0),
    }


norm_epsilon = 1e-06
attend_scale = 8.0
logit_scale = 20.0

def item_tower(features, w_in, bias_in, w_out):
    hidden = jnp.dot(features, w_in, preferred_element_type=jnp.float32) + bias_in
    hidden = jnp.maximum(hidden, 0.0).astype(jnp.bfloat16)
    embedding = jnp.dot(hidden, w_out, preferred_element_type=jnp.float32)
    inverse_norm = lax.rsqrt(lax.optimization_barrier(jnp.sum(embedding * embedding, axis=-1, keepdims=True)) + norm_epsilon)
    return (embedding * inverse_norm).astype(jnp.bfloat16)

def dynamic_route(mapped, hist_index, hist_len, route_init):
    history = jnp.take(mapped, hist_index, axis=0).astype(jnp.float32)
    live_mask = (lax.broadcasted_iota(jnp.int32, hist_index.shape, 1) < hist_len[:, None]).astype(jnp.float32)
    route_logits = route_init.astype(jnp.float32)
    capsules = jnp.zeros((hist_index.shape[0], INTERESTS, D), jnp.float32)
    for iteration in range(ITERS):
        raised = jnp.exp(route_logits)
        weights = (raised / lax.optimization_barrier(jnp.sum(raised, axis=1, keepdims=True)) * live_mask[:, None, :]).astype(jnp.bfloat16)
        weights = lax.optimization_barrier(weights).astype(jnp.float32)
        capsule_sums = jnp.einsum('ukl,uld->ukd', weights, history, precision=lax.Precision.HIGHEST)
        norm_sq = lax.optimization_barrier(jnp.sum(capsule_sums * capsule_sums, axis=-1, keepdims=True))
        capsules = capsule_sums * jnp.sqrt(norm_sq) / (1.0 + norm_sq)
        if iteration + 1 < ITERS:
            capsule_half = lax.optimization_barrier(capsules.astype(jnp.bfloat16)).astype(jnp.float32)
            agreement = jnp.einsum('ukd,uld->ukl', capsule_half, history, precision=lax.Precision.HIGHEST)
            route_logits = route_logits + agreement
    return capsules

def label_attention(capsules, label_rows, label_counts):
    scores = attend_scale * lax.optimization_barrier(jnp.sum(capsules * label_rows[:, None, :], axis=-1))
    raised = jnp.exp(scores)
    attention = raised / lax.optimization_barrier(jnp.sum(raised, axis=1, keepdims=True))
    user_vec = lax.optimization_barrier(jnp.sum(attention[:, :, None] * capsules, axis=1)).astype(jnp.bfloat16)
    user_wide = lax.optimization_barrier(user_vec).astype(jnp.float32)
    positive = logit_scale * lax.optimization_barrier(jnp.sum(user_wide * label_rows, axis=-1)) - jnp.log(label_counts.astype(jnp.float32))
    return (user_vec, positive)

def exp_terms(user_vec, label_ids, neg_unit, neg_ids, neg_counts):
    logits = logit_scale * jnp.einsum('ud,nd->un', user_vec.astype(jnp.float32), neg_unit.astype(jnp.float32), precision=lax.Precision.HIGHEST)
    logits = logits - jnp.log(neg_counts.astype(jnp.float32))[None, :]
    keep_mask = neg_ids[None, :] != label_ids[:, None]
    return lax.optimization_barrier(jnp.sum(jnp.where(keep_mask, jnp.exp(logits), 0.0), axis=1))

def reference(item_feats, w_in, bias_in, w_out, bilinear, fetch_table, hist_index, hist_len, route_init, label_index, label_ids, label_counts, neg_feats, neg_ids, neg_counts):
    item_blocks = item_feats.reshape(DEVICES, ITEMS_DEV, D)
    unit = lax.map(lambda block_rows: item_tower(block_rows, w_in, bias_in, w_out), item_blocks)
    neg_unit = item_tower(neg_feats, w_in, bias_in, w_out)

    def per_block(inputs):
        fetch_rows, index_rows, length_rows, init_rows, label_at, label_id, label_count = inputs
        received = jnp.take_along_axis(unit, fetch_rows.astype(jnp.int32)[:, :, None], axis=1).reshape(DEVICES * CAP, D)
        mapped = jnp.dot(received, bilinear, preferred_element_type=jnp.float32).astype(jnp.bfloat16)
        capsules = dynamic_route(mapped, index_rows, length_rows, init_rows)
        label_rows = jnp.take(received, label_at, axis=0).astype(jnp.float32)
        user_vec, positive = label_attention(capsules, label_rows, label_count)
        negative_sum = exp_terms(user_vec, label_id, neg_unit, neg_ids, neg_counts)
        partition = jnp.exp(positive) + negative_sum
        return (capsules.reshape(USERS_DEV, INTERESTS * D), jnp.log(partition) - positive)
    results = lax.map(per_block, (fetch_table, hist_index.reshape(DEVICES, USERS_DEV, HIST), hist_len.reshape(DEVICES, USERS_DEV), route_init.reshape(DEVICES, USERS_DEV, INTERESTS, HIST), label_index.reshape(DEVICES, USERS_DEV), label_ids.reshape(DEVICES, USERS_DEV), label_counts.reshape(DEVICES, USERS_DEV)))
    return (results[0].reshape(USERS, INTERESTS * D), results[1].reshape(USERS))
```

```python
import functools

import jax
import jax.numpy as jnp
from jax import lax
from jax.experimental import pallas as pl
from jax.experimental.pallas import tpu as pltpu
from jax.sharding import PartitionSpec as P

INTERESTS = 4
ITERS = 3
LANES = 128
SUB = 8
GROUP_USERS = 8

norm_epsilon = 1e-06
attend_scale = 8.0
logit_scale = 20.0

f32 = jnp.float32
bf16 = jnp.bfloat16
i32 = jnp.int32


def mm(a, b):
    return jnp.dot(a, b, preferred_element_type=f32)


def mm_nt(a, b):
    return lax.dot_general(a, b, (((1,), (1,)), ((), ())), preferred_element_type=f32)


def iota(shape, axis):
    return lax.broadcasted_iota(i32, shape, axis)


def to_column(row):
    n = row.shape[1]
    eye = iota((n, n), 0) == iota((n, n), 1)
    return jnp.sum(jnp.where(eye, row, 0.0), axis=1, keepdims=True)


def to_row(column):
    n = column.shape[0]
    eye = iota((n, n), 0) == iota((n, n), 1)
    return jnp.sum(jnp.where(eye, column, 0.0), axis=0, keepdims=True)


def id_digits(ids_row):
    low = to_column((ids_row & 255).astype(f32))
    mid = to_column(((ids_row >> 8) & 255).astype(f32))
    high = to_column((ids_row >> 16).astype(f32))
    return low, mid, high


def lane_columns(columns, rows):
    lane = iota((rows, LANES), 1)
    out = jnp.zeros((rows, LANES), f32)
    for at, column in enumerate(columns):
        out = jnp.where(lane == at, column, out)
    return out


def select_kernel(fetch_ref, rows_ref, out_ref):
    blocks, _, cap = fetch_ref.shape
    count = blocks * cap
    fetch = fetch_ref[:, 0, :]
    row = iota((count, blocks), 0)
    block = iota((count, blocks), 1)
    pick = jnp.where((row >= block * cap) & (row < block * cap + cap), 1.0, 0.0).astype(bf16)
    high = mm(pick, (fetch >> 7).astype(f32).astype(bf16))
    low = mm(pick, (fetch & 127).astype(f32).astype(bf16))
    place = iota((count, cap), 1) == lax.rem(iota((count, cap), 0), jnp.int32(cap))
    column = jnp.sum(jnp.where(place, high * 128.0 + low, 0.0), axis=1, keepdims=True)
    item = iota((count, rows_ref.shape[0]), 1).astype(f32)
    chosen = jnp.where(item == column, 1.0, 0.0).astype(bf16)
    out_ref[...] = mm(chosen, rows_ref[...]).astype(bf16)


def select_rows(fetch, rows):
    blocks, _, cap = fetch.shape
    return pl.pallas_call(
        select_kernel,
        out_shape=jax.ShapeDtypeStruct((blocks * cap, rows.shape[1]), bf16),
        name="select_rows",
    )(fetch, rows)


def tower_step(rows_ref, w_in_ref, bias_ref, w_out_ref, acc_ref):
    hidden = mm(rows_ref[...], w_in_ref[...]) + bias_ref[...]
    hidden = jnp.maximum(hidden, 0.0).astype(bf16)
    part = mm(hidden, w_out_ref[...])

    @pl.when(pl.program_id(0) == 0)
    def _():
        acc_ref[...] = part

    @pl.when(pl.program_id(0) > 0)
    def _():
        acc_ref[...] += part


def unit_of(acc_ref):
    embedding = acc_ref[...]
    total = jnp.sum(embedding * embedding, axis=1, keepdims=True)
    return (embedding * lax.rsqrt(total + norm_epsilon)).astype(bf16)


def item_kernel(rows_ref, w_in_ref, bias_ref, w_out_ref, bilinear_ref, unit_ref, mapped_ref, acc_ref):
    tower_step(rows_ref, w_in_ref, bias_ref, w_out_ref, acc_ref)

    @pl.when(pl.program_id(0) == pl.num_programs(0) - 1)
    def _():
        unit = unit_of(acc_ref)
        unit_ref[...] = unit
        mapped_ref[...] = mm(unit, bilinear_ref[...]).astype(bf16)


def neg_kernel(rows_ref, w_in_ref, bias_ref, w_out_ref, ids_ref, counts_ref, out_ref, acc_ref):
    tower_step(rows_ref, w_in_ref, bias_ref, w_out_ref, acc_ref)

    @pl.when(pl.program_id(0) == pl.num_programs(0) - 1)
    def _():
        width = acc_ref.shape[1]
        out_ref[:, :width] = unit_of(acc_ref)
        columns = id_digits(ids_ref[...]) + (to_column(counts_ref[...].astype(f32)),)
        out_ref[:, width:] = lane_columns(columns, acc_ref.shape[0]).astype(bf16)


def chunk_of(hidden_units):
    return 512 if hidden_units % 512 == 0 else hidden_units


def tower_specs(rows, w_in, w_out):
    chunk = chunk_of(w_in.shape[1])
    return chunk, [
        pl.BlockSpec(rows.shape, lambda i: (0, 0)),
        pl.BlockSpec((w_in.shape[0], chunk), lambda i: (0, i)),
        pl.BlockSpec((1, chunk), lambda i: (0, i)),
        pl.BlockSpec((chunk, w_out.shape[1]), lambda i: (i, 0)),
    ]


def whole(shape):
    return pl.BlockSpec(shape, lambda i: (0,) * len(shape))


def item_tower(rows, w_in, bias, w_out, bilinear):
    chunk, specs = tower_specs(rows, w_in, w_out)
    shape = (rows.shape[0], w_out.shape[1])
    return pl.pallas_call(
        item_kernel,
        grid=(w_in.shape[1] // chunk,),
        in_specs=specs + [whole(bilinear.shape)],
        out_specs=[whole(shape), whole((shape[0], bilinear.shape[1]))],
        out_shape=[
            jax.ShapeDtypeStruct(shape, bf16),
            jax.ShapeDtypeStruct((shape[0], bilinear.shape[1]), bf16),
        ],
        scratch_shapes=[pltpu.VMEM(shape, f32)],
        name="item_tower",
    )(rows, w_in, bias, w_out, bilinear)


def neg_tower(rows, w_in, bias, w_out, ids, counts):
    chunk, specs = tower_specs(rows, w_in, w_out)
    shape = (rows.shape[0], w_out.shape[1])
    return pl.pallas_call(
        neg_kernel,
        grid=(w_in.shape[1] // chunk,),
        in_specs=specs + [whole(ids.shape), whole(counts.shape)],
        out_specs=whole((shape[0], shape[1] + LANES)),
        out_shape=jax.ShapeDtypeStruct((shape[0], shape[1] + LANES), bf16),
        scratch_shapes=[pltpu.VMEM(shape, f32)],
        name="neg_tower",
    )(rows, w_in, bias, w_out, ids, counts)


def event_weights(logits, live):
    raised = [jnp.exp(one) for one in logits]
    total = functools.reduce(jnp.add, raised)
    return [(one / total * live).astype(bf16).astype(f32) for one in raised]


def scatter_weights(weights, upper, onehot_ref, slot_ref):
    users = weights[0].shape[0]
    pages = slot_ref.shape[1] // LANES
    count = pages * INTERESTS * SUB
    for group in range(users // GROUP_USERS):
        at = slice(group * GROUP_USERS, (group + 1) * GROUP_USERS)
        base = jnp.concatenate(
            [
                jnp.where(upper[at] == page, weights[k][at], 0.0)
                for page in range(pages)
                for k in range(INTERESTS)
            ],
            axis=0,
        )
        user = iota((count, 1), 0) & (GROUP_USERS - 1)
        left = jnp.concatenate(
            [
                jnp.where((user >> 1) == pair, base, 0.0).astype(bf16)
                for pair in range(GROUP_USERS // 2)
            ],
            axis=1,
        )
        both = mm_nt(left, onehot_ref[group])
        own = jnp.where((user & 1) == 0, both[:, :LANES], both[:, LANES:])
        for page in range(pages):
            for k in range(INTERESTS):
                source = (page * INTERESTS + k) * SUB
                target = k * users + group * GROUP_USERS
                slot_ref[target : target + SUB, page * LANES : (page + 1) * LANES] = own[
                    source : source + SUB
                ]


def live_mask(length_ref, shape):
    length = to_column(length_ref[...].astype(f32))
    return jnp.where(iota(shape, 1).astype(f32) < length, 1.0, 0.0)


def prepare_kernel(index_ref, length_ref, init_ref, onehot_ref, slot_ref):
    users, events = index_ref.shape
    index = index_ref[...]
    upper = index >> 7
    lower = index & (LANES - 1)
    lane_id = iota((LANES, events), 0)
    for user in range(users):
        group, within = divmod(user, GROUP_USERS)
        pair, side = divmod(within, 2)
        hit = jnp.where(lane_id == lower[user : user + 1], 1.0, 0.0).astype(bf16)
        onehot_ref[
            group, side * LANES : (side + 1) * LANES, pair * events : (pair + 1) * events
        ] = hit
    live = live_mask(length_ref, index.shape)
    weights = event_weights([init_ref[:, k, :] for k in range(INTERESTS)], live)
    scatter_weights(weights, upper, onehot_ref, slot_ref)


def prepare(index, length, init, slots):
    users, events = index.shape
    return pl.pallas_call(
        prepare_kernel,
        out_shape=[
            jax.ShapeDtypeStruct(
                (users // GROUP_USERS, 2 * LANES, GROUP_USERS // 2 * events), bf16
            ),
            jax.ShapeDtypeStruct((INTERESTS * users, slots), f32),
        ],
        name="prepare",
    )(index, length, init)


def route_kernel(
    unit_ref,
    mapped_ref,
    onehot_ref,
    first_ref,
    index_ref,
    length_ref,
    init_ref,
    label_ref,
    ids_ref,
    counts_ref,
    interests_ref,
    vec_ref,
    positive_ref,
    slot_ref,
):
    users, events = index_ref.shape
    slots, width = mapped_ref.shape
    index = index_ref[...]
    upper = index >> 7
    lower = index & (LANES - 1)
    live = live_mask(length_ref, index.shape)
    mapped = mapped_ref[...]
    logits = [init_ref[:, k, :] for k in range(INTERESTS)]
    capsules = None
    for iteration in range(ITERS):
        if iteration:
            scatter_weights(event_weights(logits, live), upper, onehot_ref, slot_ref)
        slot_weights = first_ref[...] if iteration == 0 else slot_ref[...]
        coarse = slot_weights.astype(bf16)
        rest = (slot_weights - coarse.astype(f32)).astype(bf16)
        sums = mm(coarse, mapped) + mm(rest, mapped)
        norm_sq = jnp.sum(sums * sums, axis=1, keepdims=True)
        capsules = sums * (jnp.sqrt(norm_sq) / (1.0 + norm_sq))
        if iteration + 1 < ITERS:
            scores = mm_nt(capsules.astype(bf16), mapped)
            for k in range(INTERESTS):
                chunks = []
                for at in range(0, events, LANES):
                    low = lower[:, at : at + LANES]
                    high = upper[:, at : at + LANES]
                    found = jnp.zeros((users, LANES), f32)
                    for page in range(slots // LANES):
                        piece = scores[
                            k * users : (k + 1) * users, page * LANES : (page + 1) * LANES
                        ]
                        taken = jnp.take_along_axis(
                            piece, low, axis=1, mode="promise_in_bounds"
                        )
                        found = jnp.where(high == page, taken, found)
                    chunks.append(found)
                logits[k] = logits[k] + jnp.concatenate(chunks, axis=1)
    each = [capsules[k * users : (k + 1) * users] for k in range(INTERESTS)]
    for k in range(INTERESTS):
        interests_ref[:, k * width : (k + 1) * width] = each[k]
    label = to_column(label_ref[...].astype(f32))
    chosen = jnp.where(iota((users, slots), 1).astype(f32) == label, 1.0, 0.0).astype(bf16)
    label_rows = mm(chosen, unit_ref[...])
    raised = [
        jnp.exp(attend_scale * jnp.sum(one * label_rows, axis=1, keepdims=True)) for one in each
    ]
    total = functools.reduce(jnp.add, raised)
    user_vec = functools.reduce(jnp.add, [(r / total) * one for r, one in zip(raised, each)])
    user_vec = user_vec.astype(bf16)
    vec_ref[:, :width] = user_vec
    vec_ref[:, width:] = lane_columns(id_digits(ids_ref[...]), users).astype(bf16)
    match = jnp.sum(user_vec.astype(f32) * label_rows, axis=1, keepdims=True)
    positive_ref[...] = logit_scale * to_row(match) - jnp.log(counts_ref[...].astype(f32))


def route(unit, mapped, onehot, first, index, length, init, label, ids, counts):
    users = index.shape[0]
    width = mapped.shape[1]
    return pl.pallas_call(
        route_kernel,
        out_shape=[
            jax.ShapeDtypeStruct((users, INTERESTS * width), f32),
            jax.ShapeDtypeStruct((users, width + LANES), bf16),
            jax.ShapeDtypeStruct((1, users), f32),
        ],
        scratch_shapes=[pltpu.VMEM(first.shape, f32)],
        name="route",
    )(unit, mapped, onehot, first, index, length, init, label, ids, counts)


def sums_kernel(parts, pieces, *refs):
    vec_refs = refs[:parts]
    neg_refs = refs[parts : parts + pieces]
    out_refs = refs[parts + pieces :]
    vec = jnp.concatenate([ref[...] for ref in vec_refs], axis=0)
    users = vec_refs[0].shape[0]
    width = vec.shape[1] - LANES
    place = iota((SUB, LANES), 1)
    scale = jnp.where(
        place == 0, 1.0, jnp.where(place == 1, 256.0, jnp.where(place == 2, 65536.0, 0.0))
    ).astype(bf16)
    label_ids = mm_nt(scale, vec[:, width:])[:1]
    row = iota((LANES, LANES), 0)
    to_id = jnp.where(
        row == 0, 1.0, jnp.where(row == 1, 256.0, jnp.where(row == 2, 65536.0, 0.0))
    ).astype(bf16)
    to_count = jnp.where(row == 3, 1.0, 0.0).astype(bf16)
    total = jnp.zeros((1, vec.shape[0]), f32)
    for ref in neg_refs:
        extra = ref[:, width:]
        ids = mm(extra, to_id)[:, :1]
        counts = mm(extra, to_count)[:, :1]
        dots = mm_nt(ref[:, :width], vec[:, :width])
        terms = jnp.exp(logit_scale * dots) * (1.0 / counts)
        total += jnp.sum(jnp.where(ids != label_ids, terms, 0.0), axis=0, keepdims=True)
    for part, ref in enumerate(out_refs):
        ref[...] = total[:, part * users : (part + 1) * users]


def negative_sums(vecs, negs):
    users = vecs[0].shape[0]
    return pl.pallas_call(
        functools.partial(sums_kernel, len(vecs), len(negs)),
        out_shape=[jax.ShapeDtypeStruct((1, users), f32) for _ in vecs],
        name="negative_sums",
    )(*vecs, *negs)


def swap(array, axis, size, bit):
    return lax.ppermute(array, axis, [(at, at ^ bit) for at in range(size)])


def rotate(array, axis, size, step):
    return lax.ppermute(array, axis, [(at, (at + step) % size) for at in range(size)])


def on_device(
    user_size,
    pool_size,
    item_feats,
    w_in,
    bias_in,
    w_out,
    bilinear,
    fetch_table,
    hist_index,
    hist_len,
    route_init,
    label_index,
    label_ids,
    label_counts,
    neg_feats,
    neg_ids,
    neg_counts,
):
    bias = bias_in.reshape(1, -1)
    outgoing = select_rows(fetch_table, item_feats)
    arrived = lax.all_to_all(
        outgoing.reshape(fetch_table.shape[0], fetch_table.shape[2], -1),
        ("user", "pool"),
        split_axis=0,
        concat_axis=0,
        tiled=True,
    )
    arrived = arrived.reshape(outgoing.shape)

    own_neg = neg_tower(
        neg_feats, w_in, bias, w_out, neg_ids.reshape(1, -1), neg_counts.reshape(1, -1)
    )
    length = hist_len.reshape(1, -1)
    onehot, first = prepare(hist_index, length, route_init, outgoing.shape[0])

    bits = [1 << at for at in range(pool_size.bit_length() - 1)]
    negs = [own_neg]
    for bit in bits[1:] + bits[:1]:
        held = negs[0] if len(negs) == 1 else jnp.concatenate(negs, axis=0)
        negs.append(swap(held, "pool", pool_size, bit))

    unit, mapped = item_tower(arrived, w_in, bias, w_out, bilinear)
    interests, vec, positive = route(
        unit,
        mapped,
        onehot,
        first,
        hist_index,
        length,
        route_init,
        label_index.reshape(1, -1),
        label_ids.reshape(1, -1),
        label_counts.reshape(1, -1),
    )
    vecs = [vec] + [rotate(vec, "user", user_size, step) for step in range(1, user_size)]
    sums = negative_sums(vecs, negs)
    partition = jnp.exp(positive) + sums[0]
    for step in range(1, user_size):
        partition += rotate(sums[step], "user", user_size, user_size - step)
    user_loss = jnp.log(partition) - positive
    return (interests, user_loss.reshape(-1))


def solution(mesh):
    both = ("user", "pool")
    in_specs = (
        P(both, None),
        P(),
        P(),
        P(),
        P(),
        P(None, both, None),
        P(both, None),
        P(both),
        P(both, None, None),
        P(both),
        P(both),
        P(both),
        P(both, None),
        P(both),
        P(both),
    )
    out_specs = (P(both, None), P(both))
    body = functools.partial(on_device, mesh.shape["user"], mesh.shape["pool"])
    return jax.shard_map(
        body, mesh=mesh, in_specs=in_specs, out_specs=out_specs, check_vma=False
    )
```

```python
import functools

import jax
import jax.numpy as jnp
from jax import lax
from jax.experimental import pallas as pl
from jax.experimental.pallas import tpu as pltpu
from jax.sharding import PartitionSpec as P


INTERESTS = 4
ITERS = 3
LANES = 128
SUB = 8
EXTRA = 16
GROUP_USERS = 8

norm_epsilon = 1e-06
attend_scale = 8.0
logit_scale = 20.0

f32 = jnp.float32
bf16 = jnp.bfloat16
i32 = jnp.int32


def mm(a, b):
    return jnp.dot(a, b, preferred_element_type=f32)


def mm_nt(a, b):
    return lax.dot_general(a, b, (((1,), (1,)), ((), ())), preferred_element_type=f32)


def iota(shape, axis):
    return lax.broadcasted_iota(i32, shape, axis)


def to_column(row):
    n = row.shape[1]
    eye = iota((n, n), 0) == iota((n, n), 1)
    return jnp.sum(jnp.where(eye, row, 0.0), axis=1, keepdims=True)


def to_row(column):
    n = column.shape[0]
    eye = iota((n, n), 0) == iota((n, n), 1)
    return jnp.sum(jnp.where(eye, column, 0.0), axis=0, keepdims=True)


def id_digits(ids_row):
    low = (ids_row & 255).astype(f32)
    mid = ((ids_row >> 8) & 255).astype(f32)
    high = (ids_row >> 16).astype(f32)
    return low, mid, high


def lane_columns(columns, rows):
    lane = iota((rows, LANES), 1)
    out = jnp.zeros((rows, LANES), f32)
    for at, column in enumerate(columns):
        out = jnp.where(lane == at, column, out)
    return out


def select_kernel(fetch_ref, rows_ref, out_ref):
    _, cap, blocks = fetch_ref.shape
    count = blocks * cap
    fetch = fetch_ref[0]
    row = iota((count, blocks), 0)
    block = iota((count, blocks), 1)
    pick = jnp.where((row >= block * cap) & (row < block * cap + cap), 1.0, 0.0).astype(bf16)
    high = mm_nt(pick, (fetch >> 7).astype(f32).astype(bf16))
    low = mm_nt(pick, (fetch & 127).astype(f32).astype(bf16))
    place = iota((count, cap), 1) == lax.rem(iota((count, cap), 0), jnp.int32(cap))
    column = jnp.sum(jnp.where(place, high * 128.0 + low, 0.0), axis=1, keepdims=True)
    item = iota((count, rows_ref.shape[0]), 1).astype(f32)
    chosen = jnp.where(item == column, 1.0, 0.0).astype(bf16)
    out_ref[...] = mm(chosen, rows_ref[...]).astype(bf16)


def select_rows(fetch, rows):
    blocks, _, cap = fetch.shape
    return pl.pallas_call(
        select_kernel,
        out_shape=pltpu.VMEM((blocks * cap, rows.shape[1]), bf16),
        name="select_rows",
    )(fetch.transpose(1, 2, 0), rows)


def tower_step(rows_ref, w_in_ref, bias_ref, w_out_ref, acc_ref):
    hidden = mm(rows_ref[...], w_in_ref[...]) + bias_ref[...]
    hidden = jnp.maximum(hidden, 0.0).astype(bf16)
    part = mm(hidden, w_out_ref[...])

    @pl.when(pl.program_id(0) == 0)
    def _():
        acc_ref[...] = part

    @pl.when(pl.program_id(0) > 0)
    def _():
        acc_ref[...] += part


def unit_of(acc_ref, kind):
    embedding = acc_ref[...]
    total = jnp.sum(embedding * embedding, axis=1, keepdims=True)
    return (embedding * lax.rsqrt(total + norm_epsilon)).astype(kind)


def item_kernel(rows_ref, w_in_ref, bias_ref, w_out_ref, bilinear_ref, unit_ref, mapped_ref, acc_ref):
    tower_step(rows_ref, w_in_ref, bias_ref, w_out_ref, acc_ref)

    @pl.when(pl.program_id(0) == pl.num_programs(0) - 1)
    def _():
        unit = unit_of(acc_ref, bf16)
        unit_ref[...] = unit
        mapped_ref[...] = mm(unit, bilinear_ref[...]).astype(bf16)


def neg_kernel(rows_ref, w_in_ref, bias_ref, w_out_ref, ids_ref, counts_ref, out_ref, acc_ref):
    tower_step(rows_ref, w_in_ref, bias_ref, w_out_ref, acc_ref)

    @pl.when(pl.program_id(0) == pl.num_programs(0) - 1)
    def _():
        count, width = acc_ref.shape
        out_ref[:width, :] = unit_of(acc_ref, f32).T.astype(bf16)
        rows = id_digits(ids_ref[...]) + (counts_ref[...].astype(f32),)
        at = iota((EXTRA, count), 0)
        extra = jnp.zeros((EXTRA, count), f32)
        for place, row in enumerate(rows):
            extra = jnp.where(at == place, row, extra)
        out_ref[width:, :] = extra.astype(bf16)


def chunk_of(hidden_units):
    return 512 if hidden_units % 512 == 0 else hidden_units


def tower_specs(rows, w_in, w_out):
    chunk = chunk_of(w_in.shape[1])
    return chunk, [
        pl.BlockSpec(rows.shape, lambda i: (0, 0)),
        pl.BlockSpec((w_in.shape[0], chunk), lambda i: (0, i)),
        pl.BlockSpec((1, chunk), lambda i: (0, i)),
        pl.BlockSpec((chunk, w_out.shape[1]), lambda i: (i, 0)),
    ]


def whole(shape):
    return pl.BlockSpec(shape, lambda i: (0,) * len(shape))


def item_tower(rows, w_in, bias, w_out, bilinear):
    chunk, specs = tower_specs(rows, w_in, w_out)
    shape = (rows.shape[0], w_out.shape[1])
    return pl.pallas_call(
        item_kernel,
        grid=(w_in.shape[1] // chunk,),
        in_specs=specs + [whole(bilinear.shape)],
        out_specs=[whole(shape), whole((shape[0], bilinear.shape[1]))],
        out_shape=[
            jax.ShapeDtypeStruct(shape, bf16),
            jax.ShapeDtypeStruct((shape[0], bilinear.shape[1]), bf16),
        ],
        scratch_shapes=[pltpu.VMEM(shape, f32)],
        name="item_tower",
    )(rows, w_in, bias, w_out, bilinear)


def neg_tower(rows, w_in, bias, w_out, ids, counts):
    chunk, specs = tower_specs(rows, w_in, w_out)
    shape = (rows.shape[0], w_out.shape[1])
    return pl.pallas_call(
        neg_kernel,
        grid=(w_in.shape[1] // chunk,),
        in_specs=specs + [whole(ids.shape), whole(counts.shape)],
        out_specs=whole((shape[1] + EXTRA, shape[0])),
        out_shape=jax.ShapeDtypeStruct((shape[1] + EXTRA, shape[0]), bf16),
        scratch_shapes=[pltpu.VMEM(shape, f32)],
        name="neg_tower",
    )(rows, w_in, bias, w_out, ids, counts)


def event_weights(logits, live):
    raised = [jnp.exp(one) for one in logits]
    total = functools.reduce(jnp.add, raised)
    return [(one / total * live).astype(bf16).astype(f32) for one in raised]


def scatter_weights(weights, upper, onehot_ref, slot_ref):
    users = weights[0].shape[0]
    pages = slot_ref.shape[1] // LANES
    count = pages * INTERESTS * SUB
    for group in range(users // GROUP_USERS):
        at = slice(group * GROUP_USERS, (group + 1) * GROUP_USERS)
        base = jnp.concatenate(
            [
                jnp.where(upper[at] == page, weights[k][at], 0.0)
                for page in range(pages)
                for k in range(INTERESTS)
            ],
            axis=0,
        )
        user = iota((count, 1), 0) & (GROUP_USERS - 1)
        left = jnp.concatenate(
            [
                jnp.where((user >> 1) == pair, base, 0.0).astype(bf16)
                for pair in range(GROUP_USERS // 2)
            ],
            axis=1,
        )
        both = mm_nt(left, onehot_ref[group])
        own = jnp.where((user & 1) == 0, both[:, :LANES], both[:, LANES:])
        for page in range(pages):
            for k in range(INTERESTS):
                source = (page * INTERESTS + k) * SUB
                target = k * users + group * GROUP_USERS
                slot_ref[target : target + SUB, page * LANES : (page + 1) * LANES] = own[
                    source : source + SUB
                ]


def live_mask(length_ref, shape):
    length = to_column(length_ref[...].astype(f32))
    return jnp.where(iota(shape, 1).astype(f32) < length, 1.0, 0.0)


def prepare_kernel(index_ref, length_ref, init_ref, onehot_ref, slot_ref):
    users, events = index_ref.shape
    index = index_ref[...]
    upper = index >> 7
    lower = index & (LANES - 1)
    lane_id = iota((LANES, events), 0)
    for user in range(users):
        group, within = divmod(user, GROUP_USERS)
        pair, side = divmod(within, 2)
        hit = jnp.where(lane_id == lower[user : user + 1], 1.0, 0.0).astype(bf16)
        onehot_ref[
            group, side * LANES : (side + 1) * LANES, pair * events : (pair + 1) * events
        ] = hit
    live = live_mask(length_ref, index.shape)
    weights = event_weights([init_ref[:, k, :] for k in range(INTERESTS)], live)
    scatter_weights(weights, upper, onehot_ref, slot_ref)


def prepare(index, length, init, slots):
    users, events = index.shape
    return pl.pallas_call(
        prepare_kernel,
        out_shape=[
            jax.ShapeDtypeStruct(
                (users // GROUP_USERS, 2 * LANES, GROUP_USERS // 2 * events), bf16
            ),
            jax.ShapeDtypeStruct((INTERESTS * users, slots), f32),
        ],
        name="prepare",
    )(index, length, init)


def route_kernel(
    unit_ref,
    mapped_ref,
    onehot_ref,
    first_ref,
    index_ref,
    length_ref,
    init_ref,
    label_ref,
    ids_ref,
    counts_ref,
    interests_ref,
    vec_ref,
    positive_ref,
    slot_ref,
):
    users, events = index_ref.shape
    slots, width = mapped_ref.shape
    index = index_ref[...]
    upper = index >> 7
    lower = index & (LANES - 1)
    live = live_mask(length_ref, index.shape)
    mapped = mapped_ref[...]
    logits = [init_ref[:, k, :] for k in range(INTERESTS)]
    capsules = None
    for iteration in range(ITERS):
        if iteration:
            scatter_weights(event_weights(logits, live), upper, onehot_ref, slot_ref)
        slot_weights = first_ref[...] if iteration == 0 else slot_ref[...]
        coarse = slot_weights.astype(bf16)
        rest = (slot_weights - coarse.astype(f32)).astype(bf16)
        sums = mm(coarse, mapped) + mm(rest, mapped)
        norm_sq = jnp.sum(sums * sums, axis=1, keepdims=True)
        capsules = sums * (jnp.sqrt(norm_sq) / (1.0 + norm_sq))
        if iteration + 1 < ITERS:
            scores = mm_nt(capsules.astype(bf16), mapped)
            for k in range(INTERESTS):
                chunks = []
                for at in range(0, events, LANES):
                    low = lower[:, at : at + LANES]
                    high = upper[:, at : at + LANES]
                    found = jnp.zeros((users, LANES), f32)
                    for page in range(slots // LANES):
                        piece = scores[
                            k * users : (k + 1) * users, page * LANES : (page + 1) * LANES
                        ]
                        taken = jnp.take_along_axis(
                            piece, low, axis=1, mode="promise_in_bounds"
                        )
                        found = jnp.where(high == page, taken, found)
                    chunks.append(found)
                logits[k] = logits[k] + jnp.concatenate(chunks, axis=1)
    each = [capsules[k * users : (k + 1) * users] for k in range(INTERESTS)]
    for k in range(INTERESTS):
        interests_ref[:, k * width : (k + 1) * width] = each[k]
    label = to_column(label_ref[...].astype(f32))
    chosen = jnp.where(iota((users, slots), 1).astype(f32) == label, 1.0, 0.0).astype(bf16)
    label_rows = mm(chosen, unit_ref[...])
    raised = [
        jnp.exp(attend_scale * jnp.sum(one * label_rows, axis=1, keepdims=True)) for one in each
    ]
    total = functools.reduce(jnp.add, raised)
    user_vec = functools.reduce(jnp.add, [(r / total) * one for r, one in zip(raised, each)])
    user_vec = user_vec.astype(bf16)
    vec_ref[:, :width] = user_vec
    vec_ref[:, width:] = lane_columns([to_column(one) for one in id_digits(ids_ref[...])], users).astype(bf16)
    match = jnp.sum(user_vec.astype(f32) * label_rows, axis=1, keepdims=True)
    positive_ref[...] = logit_scale * to_row(match) - jnp.log(counts_ref[...].astype(f32))


def route(unit, mapped, onehot, first, index, length, init, label, ids, counts):
    users = index.shape[0]
    width = mapped.shape[1]
    return pl.pallas_call(
        route_kernel,
        out_shape=[
            jax.ShapeDtypeStruct((users, INTERESTS * width), f32),
            jax.ShapeDtypeStruct((users, width + LANES), bf16),
            jax.ShapeDtypeStruct((1, users), f32),
        ],
        scratch_shapes=[pltpu.VMEM(first.shape, f32)],
        name="route",
    )(unit, mapped, onehot, first, index, length, init, label, ids, counts)


def sums_kernel(parts, pieces, *refs):
    vec_refs = refs[:parts]
    neg_refs = refs[parts : parts + pieces]
    out_refs = refs[parts + pieces :]
    vec = jnp.concatenate([ref[...] for ref in vec_refs], axis=0)
    users = vec_refs[0].shape[0]
    width = vec.shape[1] - LANES
    digits = vec[:, width:].astype(f32)
    label_ids = digits[:, 0:1] + 256.0 * digits[:, 1:2] + 65536.0 * digits[:, 2:3]
    vec = vec[:, :width]
    total = None
    for ref in neg_refs:
        extra = ref[width:, :].astype(f32)
        ids = extra[0:1] + 256.0 * extra[1:2] + 65536.0 * extra[2:3]
        terms = jnp.exp(logit_scale * mm(vec, ref[:width, :])) * (1.0 / extra[3:4])
        terms = jnp.where(ids != label_ids, terms, 0.0)
        total = terms if total is None else total + terms
    total = to_row(jnp.sum(total, axis=1, keepdims=True))
    for part, ref in enumerate(out_refs):
        ref[...] = total[:, part * users : (part + 1) * users]


def negative_sums(vecs, negs):
    users = vecs[0].shape[0]
    return pl.pallas_call(
        functools.partial(sums_kernel, len(vecs), len(negs)),
        out_shape=[jax.ShapeDtypeStruct((1, users), f32) for _ in vecs],
        name="negative_sums",
    )(*vecs, *negs)


def gather_pool(own, size):
    pieces = {0: own}
    for mask in range(1, size):
        bit = 1 << (mask.bit_length() - 1) if mask < 4 else mask & -mask
        pieces[mask] = lax.ppermute(
            pieces[mask ^ bit], "pool", [(at, at ^ bit) for at in range(size)]
        )
    return list(pieces.values())


def rotate(array, axis, size, step):
    return lax.ppermute(array, axis, [(at, (at + step) % size) for at in range(size)])


def on_device(
    user_size,
    pool_size,
    item_feats,
    w_in,
    bias_in,
    w_out,
    bilinear,
    fetch_table,
    hist_index,
    hist_len,
    route_init,
    label_index,
    label_ids,
    label_counts,
    neg_feats,
    neg_ids,
    neg_counts,
):
    bias = bias_in.reshape(1, -1)
    outgoing = select_rows(fetch_table, item_feats)
    arrived = lax.all_to_all(
        outgoing.reshape(fetch_table.shape[0], fetch_table.shape[2], -1),
        ("user", "pool"),
        split_axis=0,
        concat_axis=0,
        tiled=True,
    )
    arrived = arrived.reshape(outgoing.shape)

    own_neg = neg_tower(
        neg_feats, w_in, bias, w_out, neg_ids.reshape(1, -1), neg_counts.reshape(1, -1)
    )
    length = hist_len.reshape(1, -1)
    onehot, first = prepare(hist_index, length, route_init, outgoing.shape[0])
    negs = gather_pool(own_neg, pool_size)

    unit, mapped = item_tower(arrived, w_in, bias, w_out, bilinear)
    interests, vec, positive = route(
        unit,
        mapped,
        onehot,
        first,
        hist_index,
        length,
        route_init,
        label_index.reshape(1, -1),
        label_ids.reshape(1, -1),
        label_counts.reshape(1, -1),
    )
    vecs = [vec]
    for step in range(1, user_size):
        vecs.append(rotate(vec, "user", user_size, step))
    sums = negative_sums(vecs, negs)
    partition = jnp.exp(positive) + sums[0]
    for step in range(1, user_size):
        partition += rotate(sums[step], "user", user_size, user_size - step)
    user_loss = jnp.log(partition) - positive
    return (interests, user_loss.reshape(-1))


def solution(mesh):
    both = ("user", "pool")
    in_specs = (
        P(both, None),
        P(),
        P(),
        P(),
        P(),
        P(None, both, None),
        P(both, None),
        P(both),
        P(both, None, None),
        P(both),
        P(both),
        P(both),
        P(both, None),
        P(both),
        P(both),
    )
    out_specs = (P(both, None), P(both))

    def body(*args):
        return on_device(mesh.shape["user"], mesh.shape["pool"], *args)

    return jax.shard_map(body, mesh=mesh, in_specs=in_specs, out_specs=out_specs, check_vma=False)
```

```python
import functools

import jax
import jax.numpy as jnp
from jax import lax
from jax.experimental import pallas as pl
from jax.experimental.pallas import tpu as pltpu
from jax.sharding import PartitionSpec as P


INTERESTS = 4
ITERS = 3
LANES = 128
SUB = 8
EXTRA = 16
GROUP_USERS = 8

norm_epsilon = 1e-06
attend_scale = 8.0
logit_scale = 20.0

f32 = jnp.float32
bf16 = jnp.bfloat16
i32 = jnp.int32


INSIDE = pl.BlockSpec(memory_space=pltpu.VMEM)
OUTSIDE = pl.BlockSpec(memory_space=pltpu.HBM)
PARAMS = pltpu.CompilerParams(vmem_limit_bytes=20 << 20)


def near(array):
    return pltpu.with_memory_space_constraint(array, pltpu.VMEM)


def far(array):
    return pltpu.with_memory_space_constraint(array, pltpu.HBM)


def mm(a, b):
    return jnp.dot(a, b, preferred_element_type=f32)


def mm_nt(a, b):
    return lax.dot_general(a, b, (((1,), (1,)), ((), ())), preferred_element_type=f32)


def iota(shape, axis):
    return lax.broadcasted_iota(i32, shape, axis)


def to_column(row):
    n = row.shape[1]
    eye = iota((n, n), 0) == iota((n, n), 1)
    return jnp.sum(jnp.where(eye, row, 0.0), axis=1, keepdims=True)


def to_row(column):
    n = column.shape[0]
    eye = iota((n, n), 0) == iota((n, n), 1)
    return jnp.sum(jnp.where(eye, column, 0.0), axis=0, keepdims=True)


def id_digits(ids_row):
    low = (ids_row & 255).astype(f32)
    mid = ((ids_row >> 8) & 255).astype(f32)
    high = (ids_row >> 16).astype(f32)
    return low, mid, high


def lane_columns(columns, rows):
    lane = iota((rows, LANES), 1)
    out = jnp.zeros((rows, LANES), f32)
    for at, column in enumerate(columns):
        out = jnp.where(lane == at, column, out)
    return out


def select_kernel(fetch_ref, rows, out_ref, rows_ref, sem):
    copy = pltpu.make_async_copy(rows, rows_ref, sem)
    copy.start()
    _, cap, blocks = fetch_ref.shape
    count = blocks * cap
    fetch = fetch_ref[0]
    row = iota((count, blocks), 0)
    block = iota((count, blocks), 1)
    pick = jnp.where((row >= block * cap) & (row < block * cap + cap), 1.0, 0.0).astype(bf16)
    high = mm_nt(pick, (fetch >> 7).astype(f32).astype(bf16))
    low = mm_nt(pick, (fetch & 127).astype(f32).astype(bf16))
    place = iota((count, cap), 1) == lax.rem(iota((count, cap), 0), jnp.int32(cap))
    column = jnp.sum(jnp.where(place, high * 128.0 + low, 0.0), axis=1, keepdims=True)
    item = iota((count, rows_ref.shape[0]), 1).astype(f32)
    chosen = jnp.where(item == column, 1.0, 0.0).astype(bf16)
    copy.wait()
    out_ref[...] = mm(chosen, rows_ref[...]).astype(bf16)


def select_rows(fetch, rows):
    blocks, _, cap = fetch.shape
    return pl.pallas_call(
        select_kernel,
        in_specs=[INSIDE, OUTSIDE],
        out_shape=pltpu.VMEM((blocks * cap, rows.shape[1]), bf16),
        scratch_shapes=[pltpu.VMEM(rows.shape, bf16), pltpu.SemaphoreType.DMA(())],
        compiler_params=PARAMS,
        name="select_rows",
    )(fetch.transpose(1, 2, 0), far(rows))


def tower(rows_ref, w_in_ref, bias, w_out, bias_ref, out_ref, sems):
    small = pltpu.make_async_copy(bias, bias_ref, sems.at[0])
    small.start()
    large = pltpu.make_async_copy(w_out, out_ref, sems.at[1])
    large.start()
    hidden = mm(rows_ref[...], w_in_ref[...])
    small.wait()
    hidden = jnp.maximum(hidden + bias_ref[...], 0.0).astype(bf16)
    large.wait()
    embedding = mm(hidden, out_ref[...])
    total = jnp.sum(embedding * embedding, axis=1, keepdims=True)
    return embedding * lax.rsqrt(total + norm_epsilon)


def item_kernel(
    rows_ref, w_in_ref, bias, w_out, bilinear, unit_ref, mapped_ref, bias_ref, out_ref, map_ref, sems
):
    fetch = pltpu.make_async_copy(bilinear, map_ref, sems.at[2])
    fetch.start()
    unit = tower(rows_ref, w_in_ref, bias, w_out, bias_ref, out_ref, sems).astype(bf16)
    unit_ref[...] = unit
    fetch.wait()
    mapped_ref[...] = mm(unit, map_ref[...]).astype(bf16)


def neg_kernel(
    rows_ref, w_in_ref, bias, w_out, ids_ref, counts_ref, out_ref, bias_ref, w_out_ref, sems
):
    unit = tower(rows_ref, w_in_ref, bias, w_out, bias_ref, w_out_ref, sems)
    count, width = unit.shape
    out_ref[:width, :] = unit.T.astype(bf16)
    rows = id_digits(ids_ref[...]) + (counts_ref[...].astype(f32),)
    at = iota((EXTRA, count), 0)
    extra = jnp.zeros((EXTRA, count), f32)
    for place, row in enumerate(rows):
        extra = jnp.where(at == place, row, extra)
    out_ref[width:, :] = extra.astype(bf16)


def item_tower(rows, weights, bilinear):
    shape = (rows.shape[0], bilinear.shape[1])
    return pl.pallas_call(
        item_kernel,
        in_specs=[INSIDE, INSIDE, OUTSIDE, OUTSIDE, OUTSIDE],
        out_shape=[pltpu.VMEM(rows.shape, bf16), pltpu.VMEM(shape, bf16)],
        scratch_shapes=[
            pltpu.VMEM(weights[1].shape, f32),
            pltpu.VMEM(weights[2].shape, bf16),
            pltpu.VMEM(bilinear.shape, bf16),
            pltpu.SemaphoreType.DMA((3,)),
        ],
        compiler_params=PARAMS,
        name="item_tower",
    )(near(rows), *weights, far(bilinear))


def neg_tower(rows, weights, ids, counts):
    return pl.pallas_call(
        neg_kernel,
        in_specs=[INSIDE, INSIDE, OUTSIDE, OUTSIDE, INSIDE, INSIDE],
        out_shape=pltpu.VMEM((rows.shape[1] + EXTRA, rows.shape[0]), bf16),
        scratch_shapes=[
            pltpu.VMEM(weights[1].shape, f32),
            pltpu.VMEM(weights[2].shape, bf16),
            pltpu.SemaphoreType.DMA((2,)),
        ],
        compiler_params=PARAMS,
        name="neg_tower",
    )(near(rows), *weights, ids, counts)


def event_weights(logits, live):
    raised = [jnp.exp(one) for one in logits]
    total = functools.reduce(jnp.add, raised)
    return [(one / total * live).astype(bf16).astype(f32) for one in raised]


def scatter_weights(weights, upper, onehot_ref, slot_ref):
    users = weights[0].shape[0]
    pages = slot_ref.shape[1] // LANES
    count = pages * INTERESTS * SUB
    for group in range(users // GROUP_USERS):
        at = slice(group * GROUP_USERS, (group + 1) * GROUP_USERS)
        base = jnp.concatenate(
            [
                jnp.where(upper[at] == page, weights[k][at], 0.0)
                for page in range(pages)
                for k in range(INTERESTS)
            ],
            axis=0,
        )
        user = iota((count, 1), 0) & (GROUP_USERS - 1)
        left = jnp.concatenate(
            [
                jnp.where((user >> 1) == pair, base, 0.0).astype(bf16)
                for pair in range(GROUP_USERS // 2)
            ],
            axis=1,
        )
        both = mm_nt(left, onehot_ref[group])
        own = jnp.where((user & 1) == 0, both[:, :LANES], both[:, LANES:])
        for page in range(pages):
            for k in range(INTERESTS):
                source = (page * INTERESTS + k) * SUB
                target = k * users + group * GROUP_USERS
                slot_ref[target : target + SUB, page * LANES : (page + 1) * LANES] = own[
                    source : source + SUB
                ]


def live_mask(length_ref, shape):
    length = to_column(length_ref[...].astype(f32))
    return jnp.where(iota(shape, 1).astype(f32) < length, 1.0, 0.0)


def prepare_kernel(index_ref, length_ref, init_ref, onehot_ref, slot_ref):
    users, events = index_ref.shape
    index = index_ref[...]
    upper = index >> 7
    lower = index & (LANES - 1)
    lane_id = iota((LANES, events), 0)
    for user in range(users):
        group, within = divmod(user, GROUP_USERS)
        pair, side = divmod(within, 2)
        hit = jnp.where(lane_id == lower[user : user + 1], 1.0, 0.0).astype(bf16)
        onehot_ref[
            group, side * LANES : (side + 1) * LANES, pair * events : (pair + 1) * events
        ] = hit
    live = live_mask(length_ref, index.shape)
    weights = event_weights([init_ref[:, k, :] for k in range(INTERESTS)], live)
    scatter_weights(weights, upper, onehot_ref, slot_ref)


def prepare(index, length, init, slots):
    users, events = index.shape
    return pl.pallas_call(
        prepare_kernel,
        out_shape=[
            pltpu.VMEM((users // GROUP_USERS, 2 * LANES, GROUP_USERS // 2 * events), bf16),
            pltpu.VMEM((INTERESTS * users, slots), f32),
        ],
        compiler_params=PARAMS,
        name="prepare",
    )(near(index), length, near(init))


def route_kernel(
    unit_ref,
    mapped_ref,
    onehot_ref,
    first_ref,
    index_ref,
    length_ref,
    init_ref,
    label_ref,
    ids_ref,
    counts_ref,
    interests_ref,
    vec_ref,
    positive_ref,
    slot_ref,
):
    users, events = index_ref.shape
    slots, width = mapped_ref.shape
    index = index_ref[...]
    upper = index >> 7
    lower = index & (LANES - 1)
    live = live_mask(length_ref, index.shape)
    mapped = mapped_ref[...]
    logits = [init_ref[:, k, :] for k in range(INTERESTS)]
    capsules = None
    for iteration in range(ITERS):
        if iteration:
            scatter_weights(event_weights(logits, live), upper, onehot_ref, slot_ref)
        slot_weights = first_ref[...] if iteration == 0 else slot_ref[...]
        coarse = slot_weights.astype(bf16)
        rest = (slot_weights - coarse.astype(f32)).astype(bf16)
        sums = mm(coarse, mapped) + mm(rest, mapped)
        norm_sq = jnp.sum(sums * sums, axis=1, keepdims=True)
        capsules = sums * (jnp.sqrt(norm_sq) / (1.0 + norm_sq))
        if iteration + 1 < ITERS:
            scores = mm_nt(capsules.astype(bf16), mapped)
            for k in range(INTERESTS):
                chunks = []
                for at in range(0, events, LANES):
                    low = lower[:, at : at + LANES]
                    high = upper[:, at : at + LANES]
                    found = jnp.zeros((users, LANES), f32)
                    for page in range(slots // LANES):
                        piece = scores[
                            k * users : (k + 1) * users, page * LANES : (page + 1) * LANES
                        ]
                        taken = jnp.take_along_axis(
                            piece, low, axis=1, mode="promise_in_bounds"
                        )
                        found = jnp.where(high == page, taken, found)
                    chunks.append(found)
                logits[k] = logits[k] + jnp.concatenate(chunks, axis=1)
    each = [capsules[k * users : (k + 1) * users] for k in range(INTERESTS)]
    for k in range(INTERESTS):
        interests_ref[:, k * width : (k + 1) * width] = each[k]
    label = to_column(label_ref[...].astype(f32))
    chosen = jnp.where(iota((users, slots), 1).astype(f32) == label, 1.0, 0.0).astype(bf16)
    label_rows = mm(chosen, unit_ref[...])
    raised = [
        jnp.exp(attend_scale * jnp.sum(one * label_rows, axis=1, keepdims=True)) for one in each
    ]
    total = functools.reduce(jnp.add, raised)
    user_vec = functools.reduce(jnp.add, [(r / total) * one for r, one in zip(raised, each)])
    user_vec = user_vec.astype(bf16)
    vec_ref[:, :width] = user_vec
    vec_ref[:, width:] = lane_columns([to_column(one) for one in id_digits(ids_ref[...])], users).astype(bf16)
    match = jnp.sum(user_vec.astype(f32) * label_rows, axis=1, keepdims=True)
    positive_ref[...] = logit_scale * to_row(match) - jnp.log(counts_ref[...].astype(f32))


def route(unit, mapped, onehot, first, index, length, init, label, ids, counts):
    users = index.shape[0]
    width = mapped.shape[1]
    return pl.pallas_call(
        route_kernel,
        out_shape=[
            jax.ShapeDtypeStruct((users, INTERESTS * width), f32),
            pltpu.VMEM((users, width + LANES), bf16),
            pltpu.VMEM((1, users), f32),
        ],
        scratch_shapes=[pltpu.VMEM(first.shape, f32)],
        compiler_params=PARAMS,
        name="route",
    )(
        near(unit),
        near(mapped),
        near(onehot),
        near(first),
        near(index),
        length,
        near(init),
        label,
        ids,
        counts,
    )


def sums_kernel(parts, pieces, *refs):
    vec_refs = refs[:parts]
    neg_refs = refs[parts : parts + pieces]
    out_refs = refs[parts + pieces :]
    vec = jnp.concatenate([ref[...] for ref in vec_refs], axis=0)
    users = vec_refs[0].shape[0]
    width = vec.shape[1] - LANES
    digits = vec[:, width:].astype(f32)
    label_ids = digits[:, 0:1] + 256.0 * digits[:, 1:2] + 65536.0 * digits[:, 2:3]
    vec = vec[:, :width]
    total = None
    for ref in neg_refs:
        extra = ref[width:, :].astype(f32)
        ids = extra[0:1] + 256.0 * extra[1:2] + 65536.0 * extra[2:3]
        terms = jnp.exp(logit_scale * mm(vec, ref[:width, :])) * (1.0 / extra[3:4])
        terms = jnp.where(ids != label_ids, terms, 0.0)
        total = terms if total is None else total + terms
    total = to_row(jnp.sum(total, axis=1, keepdims=True))
    for part, ref in enumerate(out_refs):
        ref[...] = total[:, part * users : (part + 1) * users]


def negative_sums(vecs, negs):
    users = vecs[0].shape[0]
    return pl.pallas_call(
        functools.partial(sums_kernel, len(vecs), len(negs)),
        out_shape=[pltpu.VMEM((1, users), f32) for _ in vecs],
        compiler_params=PARAMS,
        name="negative_sums",
    )(*[near(one) for one in [*vecs, *negs]])


def gather_pool(own, size):
    pieces = {0: own}
    for mask in range(1, size):
        bit = 1 << (mask.bit_length() - 1) if mask < 4 else mask & -mask
        pieces[mask] = lax.ppermute(
            pieces[mask ^ bit], "pool", [(at, at ^ bit) for at in range(size)]
        )
    return list(pieces.values())


def rotate(array, axis, size, step):
    return lax.ppermute(array, axis, [(at, (at + step) % size) for at in range(size)])


def on_device(
    user_size,
    pool_size,
    item_feats,
    w_in,
    bias_in,
    w_out,
    bilinear,
    fetch_table,
    hist_index,
    hist_len,
    route_init,
    label_index,
    label_ids,
    label_counts,
    neg_feats,
    neg_ids,
    neg_counts,
):
    weights = (near(w_in), far(bias_in.reshape(1, -1)), far(w_out))
    outgoing = select_rows(fetch_table, item_feats)
    arrived = lax.all_to_all(
        outgoing.reshape(fetch_table.shape[0], fetch_table.shape[2], -1),
        ("user", "pool"),
        split_axis=0,
        concat_axis=0,
        tiled=True,
    )
    arrived = arrived.reshape(outgoing.shape)

    own_neg = neg_tower(
        neg_feats, weights, neg_ids.reshape(1, -1), neg_counts.reshape(1, -1)
    )
    length = hist_len.reshape(1, -1)
    onehot, first = prepare(hist_index, length, route_init, outgoing.shape[0])
    negs = gather_pool(own_neg, pool_size)

    unit, mapped = item_tower(arrived, weights, bilinear)
    interests, vec, positive = route(
        unit,
        mapped,
        onehot,
        first,
        hist_index,
        length,
        route_init,
        label_index.reshape(1, -1),
        label_ids.reshape(1, -1),
        label_counts.reshape(1, -1),
    )
    vecs = [vec]
    for step in range(1, user_size):
        vecs.append(rotate(vec, "user", user_size, step))
    sums = negative_sums(vecs, negs)
    partition = jnp.exp(positive) + sums[0]
    for step in range(1, user_size):
        partition += rotate(sums[step], "user", user_size, user_size - step)
    user_loss = jnp.log(partition) - positive
    return (interests, user_loss.reshape(-1))


def solution(mesh):
    both = ("user", "pool")
    in_specs = (
        P(both, None),
        P(),
        P(),
        P(),
        P(),
        P(None, both, None),
        P(both, None),
        P(both),
        P(both, None, None),
        P(both),
        P(both),
        P(both),
        P(both, None),
        P(both),
        P(both),
    )
    out_specs = (P(both, None), P(both))

    def body(*args):
        return on_device(mesh.shape["user"], mesh.shape["pool"], *args)

    return jax.shard_map(body, mesh=mesh, in_specs=in_specs, out_specs=out_specs, check_vma=False)
```

```python
import functools

import jax
import jax.numpy as jnp
from jax import lax
from jax.experimental import pallas as pl
from jax.experimental.pallas import tpu as pltpu
from jax.sharding import PartitionSpec as P


INTERESTS = 4
ITERS = 3
LANES = 128
SUB = 8
EXTRA = 16
GROUP_USERS = 8

norm_epsilon = 1e-06
attend_scale = 8.0
logit_scale = 20.0

f32 = jnp.float32
bf16 = jnp.bfloat16
i32 = jnp.int32


INSIDE = pl.BlockSpec(memory_space=pltpu.VMEM)
OUTSIDE = pl.BlockSpec(memory_space=pltpu.HBM)
PARAMS = pltpu.CompilerParams(vmem_limit_bytes=20 << 20)


def near(array):
    return pltpu.with_memory_space_constraint(array, pltpu.VMEM)


def far(array):
    return pltpu.with_memory_space_constraint(array, pltpu.HBM)


def mm(a, b):
    return jnp.dot(a, b, preferred_element_type=f32)


def mm_nt(a, b):
    return lax.dot_general(a, b, (((1,), (1,)), ((), ())), preferred_element_type=f32)


def iota(shape, axis):
    return lax.broadcasted_iota(i32, shape, axis)


def to_column(row):
    n = row.shape[1]
    eye = iota((n, n), 0) == iota((n, n), 1)
    return jnp.sum(jnp.where(eye, row, 0.0), axis=1, keepdims=True)


def to_row(column):
    n = column.shape[0]
    eye = iota((n, n), 0) == iota((n, n), 1)
    return jnp.sum(jnp.where(eye, column, 0.0), axis=0, keepdims=True)


def id_digits(ids_row):
    low = (ids_row & 255).astype(f32)
    mid = ((ids_row >> 8) & 255).astype(f32)
    high = (ids_row >> 16).astype(f32)
    return low, mid, high


def lane_columns(columns, rows):
    lane = iota((rows, LANES), 1)
    out = jnp.zeros((rows, LANES), f32)
    for at, column in enumerate(columns):
        out = jnp.where(lane == at, column, out)
    return out


def select_kernel(fetch, rows, out_ref, fetch_ref, rows_ref, sems):
    table = pltpu.make_async_copy(fetch, fetch_ref, sems.at[0])
    table.start()
    copy = pltpu.make_async_copy(rows, rows_ref, sems.at[1])
    copy.start()
    _, cap, blocks = fetch_ref.shape
    count = blocks * cap
    row = iota((count, blocks), 0)
    block = iota((count, blocks), 1)
    pick = jnp.where((row >= block * cap) & (row < block * cap + cap), 1.0, 0.0).astype(bf16)
    table.wait()
    picked = fetch_ref[0]
    high = mm_nt(pick, (picked >> 7).astype(f32).astype(bf16))
    low = mm_nt(pick, (picked & 127).astype(f32).astype(bf16))
    place = iota((count, cap), 1) == lax.rem(iota((count, cap), 0), jnp.int32(cap))
    column = jnp.sum(jnp.where(place, high * 128.0 + low, 0.0), axis=1, keepdims=True)
    item = iota((count, rows_ref.shape[0]), 1).astype(f32)
    chosen = jnp.where(item == column, 1.0, 0.0).astype(bf16)
    copy.wait()
    out_ref[...] = mm(chosen, rows_ref[...]).astype(bf16)


def select_rows(fetch, rows):
    blocks, _, cap = fetch.shape
    return pl.pallas_call(
        select_kernel,
        in_specs=[OUTSIDE, OUTSIDE],
        out_shape=pltpu.VMEM((blocks * cap, rows.shape[1]), bf16),
        scratch_shapes=[
            pltpu.VMEM((1, cap, blocks), i32),
            pltpu.VMEM(rows.shape, bf16),
            pltpu.SemaphoreType.DMA((2,)),
        ],
        compiler_params=PARAMS,
        name="select_rows",
    )(far(fetch.transpose(1, 2, 0)), far(rows))


def tower(rows_ref, w_in_ref, bias, w_out, bias_ref, out_ref, sems):
    small = pltpu.make_async_copy(bias, bias_ref, sems.at[0])
    small.start()
    large = pltpu.make_async_copy(w_out, out_ref, sems.at[1])
    large.start()
    hidden = mm(rows_ref[...], w_in_ref[...])
    small.wait()
    hidden = jnp.maximum(hidden + bias_ref[...], 0.0).astype(bf16)
    large.wait()
    embedding = mm(hidden, out_ref[...])
    total = jnp.sum(embedding * embedding, axis=1, keepdims=True)
    return embedding * lax.rsqrt(total + norm_epsilon)


def item_kernel(
    rows_ref, w_in_ref, bias, w_out, bilinear, unit_ref, mapped_ref, bias_ref, out_ref, map_ref, sems
):
    fetch = pltpu.make_async_copy(bilinear, map_ref, sems.at[2])
    fetch.start()
    unit = tower(rows_ref, w_in_ref, bias, w_out, bias_ref, out_ref, sems).astype(bf16)
    unit_ref[...] = unit
    fetch.wait()
    mapped_ref[...] = mm(unit, map_ref[...]).astype(bf16)


def neg_kernel(
    rows_ref, w_in_ref, bias, w_out, ids_ref, counts_ref, out_ref, bias_ref, w_out_ref, sems
):
    unit = tower(rows_ref, w_in_ref, bias, w_out, bias_ref, w_out_ref, sems)
    count, width = unit.shape
    out_ref[:width, :] = unit.T.astype(bf16)
    rows = id_digits(ids_ref[...]) + (counts_ref[...].astype(f32),)
    at = iota((EXTRA, count), 0)
    extra = jnp.zeros((EXTRA, count), f32)
    for place, row in enumerate(rows):
        extra = jnp.where(at == place, row, extra)
    out_ref[width:, :] = extra.astype(bf16)


def item_tower(rows, weights, bilinear):
    shape = (rows.shape[0], bilinear.shape[1])
    return pl.pallas_call(
        item_kernel,
        in_specs=[INSIDE, INSIDE, OUTSIDE, OUTSIDE, OUTSIDE],
        out_shape=[pltpu.VMEM(rows.shape, bf16), pltpu.VMEM(shape, bf16)],
        scratch_shapes=[
            pltpu.VMEM(weights[1].shape, f32),
            pltpu.VMEM(weights[2].shape, bf16),
            pltpu.VMEM(bilinear.shape, bf16),
            pltpu.SemaphoreType.DMA((3,)),
        ],
        compiler_params=PARAMS,
        name="item_tower",
    )(near(rows), *weights, far(bilinear))


def neg_tower(rows, weights, ids, counts):
    return pl.pallas_call(
        neg_kernel,
        in_specs=[INSIDE, INSIDE, OUTSIDE, OUTSIDE, INSIDE, INSIDE],
        out_shape=pltpu.VMEM((rows.shape[1] + EXTRA, rows.shape[0]), bf16),
        scratch_shapes=[
            pltpu.VMEM(weights[1].shape, f32),
            pltpu.VMEM(weights[2].shape, bf16),
            pltpu.SemaphoreType.DMA((2,)),
        ],
        compiler_params=PARAMS,
        name="neg_tower",
    )(near(rows), *weights, ids, counts)


def event_weights(logits, live):
    raised = [jnp.exp(one) for one in logits]
    total = functools.reduce(jnp.add, raised)
    return [(one / total * live).astype(bf16).astype(f32) for one in raised]


def scatter_weights(weights, upper, onehot_ref, slot_ref):
    users = weights[0].shape[0]
    pages = slot_ref.shape[1] // LANES
    count = pages * INTERESTS * SUB
    for group in range(users // GROUP_USERS):
        at = slice(group * GROUP_USERS, (group + 1) * GROUP_USERS)
        base = jnp.concatenate(
            [
                jnp.where(upper[at] == page, weights[k][at], 0.0)
                for page in range(pages)
                for k in range(INTERESTS)
            ],
            axis=0,
        )
        user = iota((count, 1), 0) & (GROUP_USERS - 1)
        left = jnp.concatenate(
            [
                jnp.where((user >> 1) == pair, base, 0.0).astype(bf16)
                for pair in range(GROUP_USERS // 2)
            ],
            axis=1,
        )
        both = mm_nt(left, onehot_ref[group])
        own = jnp.where((user & 1) == 0, both[:, :LANES], both[:, LANES:])
        for page in range(pages):
            for k in range(INTERESTS):
                source = (page * INTERESTS + k) * SUB
                target = k * users + group * GROUP_USERS
                slot_ref[target : target + SUB, page * LANES : (page + 1) * LANES] = own[
                    source : source + SUB
                ]


def live_mask(length_ref, shape):
    length = to_column(length_ref[...].astype(f32))
    return jnp.where(iota(shape, 1).astype(f32) < length, 1.0, 0.0)


def prepare_kernel(index_ref, length_ref, init_ref, onehot_ref, slot_ref):
    users, events = index_ref.shape
    index = index_ref[...]
    upper = index >> 7
    lower = index & (LANES - 1)
    lane_id = iota((LANES, events), 0)
    for user in range(users):
        group, within = divmod(user, GROUP_USERS)
        pair, side = divmod(within, 2)
        hit = jnp.where(lane_id == lower[user : user + 1], 1.0, 0.0).astype(bf16)
        onehot_ref[
            group, side * LANES : (side + 1) * LANES, pair * events : (pair + 1) * events
        ] = hit
    live = live_mask(length_ref, index.shape)
    weights = event_weights([init_ref[:, k, :] for k in range(INTERESTS)], live)
    scatter_weights(weights, upper, onehot_ref, slot_ref)


def prepare(index, length, init, slots):
    users, events = index.shape
    return pl.pallas_call(
        prepare_kernel,
        out_shape=[
            jax.ShapeDtypeStruct(
                (users // GROUP_USERS, 2 * LANES, GROUP_USERS // 2 * events), bf16
            ),
            pltpu.VMEM((INTERESTS * users, slots), f32),
        ],
        compiler_params=PARAMS,
        name="prepare",
    )(near(index), length, near(init))


def route_kernel(
    unit_ref,
    mapped_ref,
    onehot,
    first_ref,
    index_ref,
    length_ref,
    init_ref,
    label_ref,
    ids_ref,
    counts_ref,
    interests_ref,
    vec_ref,
    positive_ref,
    slot_ref,
    onehot_ref,
    sem,
):
    fetch = pltpu.make_async_copy(onehot, onehot_ref, sem)
    fetch.start()
    users, events = index_ref.shape
    slots, width = mapped_ref.shape
    index = index_ref[...]
    upper = index >> 7
    lower = index & (LANES - 1)
    live = live_mask(length_ref, index.shape)
    mapped = mapped_ref[...]
    logits = [init_ref[:, k, :] for k in range(INTERESTS)]
    capsules = None
    for iteration in range(ITERS):
        if iteration == 1:
            fetch.wait()
        if iteration:
            scatter_weights(event_weights(logits, live), upper, onehot_ref, slot_ref)
        slot_weights = first_ref[...] if iteration == 0 else slot_ref[...]
        coarse = slot_weights.astype(bf16)
        rest = (slot_weights - coarse.astype(f32)).astype(bf16)
        sums = mm(coarse, mapped) + mm(rest, mapped)
        norm_sq = jnp.sum(sums * sums, axis=1, keepdims=True)
        capsules = sums * (jnp.sqrt(norm_sq) / (1.0 + norm_sq))
        if iteration + 1 < ITERS:
            scores = mm_nt(capsules.astype(bf16), mapped)
            for k in range(INTERESTS):
                chunks = []
                for at in range(0, events, LANES):
                    low = lower[:, at : at + LANES]
                    high = upper[:, at : at + LANES]
                    found = jnp.zeros((users, LANES), f32)
                    for page in range(slots // LANES):
                        piece = scores[
                            k * users : (k + 1) * users, page * LANES : (page + 1) * LANES
                        ]
                        taken = jnp.take_along_axis(
                            piece, low, axis=1, mode="promise_in_bounds"
                        )
                        found = jnp.where(high == page, taken, found)
                    chunks.append(found)
                logits[k] = logits[k] + jnp.concatenate(chunks, axis=1)
    each = [capsules[k * users : (k + 1) * users] for k in range(INTERESTS)]
    for k in range(INTERESTS):
        interests_ref[:, k * width : (k + 1) * width] = each[k]
    label = to_column(label_ref[...].astype(f32))
    chosen = jnp.where(iota((users, slots), 1).astype(f32) == label, 1.0, 0.0).astype(bf16)
    label_rows = mm(chosen, unit_ref[...])
    raised = [
        jnp.exp(attend_scale * jnp.sum(one * label_rows, axis=1, keepdims=True)) for one in each
    ]
    total = functools.reduce(jnp.add, raised)
    user_vec = functools.reduce(jnp.add, [(r / total) * one for r, one in zip(raised, each)])
    user_vec = user_vec.astype(bf16)
    vec_ref[:, :width] = user_vec
    vec_ref[:, width:] = lane_columns([to_column(one) for one in id_digits(ids_ref[...])], users).astype(bf16)
    match = jnp.sum(user_vec.astype(f32) * label_rows, axis=1, keepdims=True)
    positive_ref[...] = logit_scale * to_row(match) - jnp.log(counts_ref[...].astype(f32))


def route(unit, mapped, onehot, first, index, length, init, label, ids, counts):
    users = index.shape[0]
    width = mapped.shape[1]
    return pl.pallas_call(
        route_kernel,
        out_shape=[
            jax.ShapeDtypeStruct((users, INTERESTS * width), f32),
            pltpu.VMEM((users, width + LANES), bf16),
            pltpu.VMEM((1, users), f32),
        ],
        in_specs=[INSIDE, INSIDE, OUTSIDE] + [INSIDE] * 7,
        scratch_shapes=[
            pltpu.VMEM(first.shape, f32),
            pltpu.VMEM(onehot.shape, bf16),
            pltpu.SemaphoreType.DMA(()),
        ],
        compiler_params=PARAMS,
        name="route",
    )(
        near(unit),
        near(mapped),
        far(onehot),
        near(first),
        near(index),
        length,
        near(init),
        label,
        ids,
        counts,
    )


def sums_kernel(parts, pieces, *refs):
    vec_refs = refs[:parts]
    neg_refs = refs[parts : parts + pieces]
    out_refs = refs[parts + pieces :]
    vec = jnp.concatenate([ref[...] for ref in vec_refs], axis=0)
    users = vec_refs[0].shape[0]
    width = vec.shape[1] - LANES
    digits = vec[:, width:].astype(f32)
    label_ids = digits[:, 0:1] + 256.0 * digits[:, 1:2] + 65536.0 * digits[:, 2:3]
    vec = vec[:, :width]
    total = None
    for ref in neg_refs:
        extra = ref[width:, :].astype(f32)
        ids = extra[0:1] + 256.0 * extra[1:2] + 65536.0 * extra[2:3]
        terms = jnp.exp(logit_scale * mm(vec, ref[:width, :])) * (1.0 / extra[3:4])
        terms = jnp.where(ids != label_ids, terms, 0.0)
        total = terms if total is None else total + terms
    total = to_row(jnp.sum(total, axis=1, keepdims=True))
    for part, ref in enumerate(out_refs):
        ref[...] = total[:, part * users : (part + 1) * users]


def negative_sums(vecs, negs):
    users = vecs[0].shape[0]
    return pl.pallas_call(
        functools.partial(sums_kernel, len(vecs), len(negs)),
        out_shape=[pltpu.VMEM((1, users), f32) for _ in vecs],
        compiler_params=PARAMS,
        name="negative_sums",
    )(*[near(one) for one in [*vecs, *negs]])


def swap_pool(array, size):
    return lax.ppermute(array, "pool", [(at, at ^ 1) for at in range(size)])


def rotate_user(array, size, step):
    return lax.ppermute(array, "user", [(at, (at + step) % size) for at in range(size)])


def rotate_pool(array, size, step):
    return lax.ppermute(array, "pool", [(at, (at + 2 * step) % size) for at in range(size)])


def gather_negatives(own, user_size, pool_size):
    pair = swap_pool(own, pool_size)
    pieces = [own, pair]
    for step in range(1, user_size):
        pieces.append(rotate_user(own, user_size, step))
    for step in range(1, user_size):
        pieces.append(rotate_user(pair, user_size, step))
    return pieces


def on_device(
    user_size,
    pool_size,
    item_feats,
    w_in,
    bias_in,
    w_out,
    bilinear,
    fetch_table,
    hist_index,
    hist_len,
    route_init,
    label_index,
    label_ids,
    label_counts,
    neg_feats,
    neg_ids,
    neg_counts,
):
    weights = (near(w_in), far(bias_in.reshape(1, -1)), far(w_out))
    outgoing = select_rows(fetch_table, item_feats)
    arrived = lax.all_to_all(
        outgoing.reshape(fetch_table.shape[0], fetch_table.shape[2], -1),
        ("user", "pool"),
        split_axis=0,
        concat_axis=0,
        tiled=True,
    )
    arrived = arrived.reshape(outgoing.shape)

    own_neg = neg_tower(
        neg_feats, weights, neg_ids.reshape(1, -1), neg_counts.reshape(1, -1)
    )
    length = hist_len.reshape(1, -1)
    onehot, first = prepare(hist_index, length, route_init, outgoing.shape[0])
    negs = gather_negatives(own_neg, user_size, pool_size)

    unit, mapped = item_tower(arrived, weights, bilinear)
    interests, vec, positive = route(
        unit,
        mapped,
        onehot,
        first,
        hist_index,
        length,
        route_init,
        label_index.reshape(1, -1),
        label_ids.reshape(1, -1),
        label_counts.reshape(1, -1),
    )
    late = pool_size // 2
    vecs = [vec] + [rotate_pool(vec, pool_size, step) for step in range(1, late)]
    sums = negative_sums(vecs, negs)
    partition = jnp.exp(positive) + sums[0]
    for step in range(1, late):
        partition += rotate_pool(sums[step], pool_size, late - step)
    user_loss = jnp.log(partition) - positive
    return (interests, user_loss.reshape(-1))


def solution(mesh):
    both = ("user", "pool")
    in_specs = (
        P(both, None),
        P(),
        P(),
        P(),
        P(),
        P(None, both, None),
        P(both, None),
        P(both),
        P(both, None, None),
        P(both),
        P(both),
        P(both),
        P(both, None),
        P(both),
        P(both),
    )
    out_specs = (P(both, None), P(both))

    def body(*args):
        return on_device(mesh.shape["user"], mesh.shape["pool"], *args)

    return jax.shard_map(body, mesh=mesh, in_specs=in_specs, out_specs=out_specs, check_vma=False)
```

```python
import functools

import jax
import jax.numpy as jnp
from jax import lax
from jax.experimental import pallas as pl
from jax.experimental.pallas import tpu as pltpu
from jax.sharding import PartitionSpec as P


INTERESTS = 4
ITERS = 3
LANES = 128
SUB = 8
EXTRA = 16
SPLIT = 4
GROUP_USERS = 8

norm_epsilon = 1e-06
attend_scale = 8.0
logit_scale = 20.0

f32 = jnp.float32
bf16 = jnp.bfloat16
i32 = jnp.int32


INSIDE = pl.BlockSpec(memory_space=pltpu.VMEM)
OUTSIDE = pl.BlockSpec(memory_space=pltpu.HBM)
PARAMS = pltpu.CompilerParams(vmem_limit_bytes=20 << 20)


def near(array):
    return pltpu.with_memory_space_constraint(array, pltpu.VMEM)


def far(array):
    return pltpu.with_memory_space_constraint(array, pltpu.HBM)


def mm(a, b):
    return jnp.dot(a, b, preferred_element_type=f32)


def mm_nt(a, b):
    return lax.dot_general(a, b, (((1,), (1,)), ((), ())), preferred_element_type=f32)


def iota(shape, axis):
    return lax.broadcasted_iota(i32, shape, axis)


def to_column(row):
    n = row.shape[1]
    eye = iota((n, n), 0) == iota((n, n), 1)
    return jnp.sum(jnp.where(eye, row, 0.0), axis=1, keepdims=True)


def to_row(column):
    n = column.shape[0]
    eye = iota((n, n), 0) == iota((n, n), 1)
    return jnp.sum(jnp.where(eye, column, 0.0), axis=0, keepdims=True)


def id_digits(ids_row):
    low = (ids_row & 255).astype(f32)
    mid = ((ids_row >> 8) & 255).astype(f32)
    high = (ids_row >> 16).astype(f32)
    return low, mid, high


def lane_columns(columns, rows):
    lane = iota((rows, LANES), 1)
    out = jnp.zeros((rows, LANES), f32)
    for at, column in enumerate(columns):
        out = jnp.where(lane == at, column, out)
    return out


class Copies:
    def __init__(self, source, target, sems, first, count):
        size = source.shape[0] // count
        self.copies = [
            pltpu.make_async_copy(
                source.at[pl.ds(at * size, size)],
                target.at[pl.ds(at * size, size)],
                sems.at[first + at],
            )
            for at in range(count)
        ]
        for copy in self.copies:
            copy.start()

    def wait(self):
        for copy in self.copies:
            copy.wait()


def select_kernel(fetch, rows, out_ref, fetch_ref, rows_ref, sems):
    table = pltpu.make_async_copy(fetch, fetch_ref, sems.at[0])
    table.start()
    copy = pltpu.make_async_copy(rows, rows_ref, sems.at[1])
    copy.start()
    _, cap, blocks = fetch_ref.shape
    count = blocks * cap
    row = iota((count, blocks), 0)
    block = iota((count, blocks), 1)
    pick = jnp.where((row >= block * cap) & (row < block * cap + cap), 1.0, 0.0).astype(bf16)
    table.wait()
    picked = fetch_ref[0]
    high = mm_nt(pick, (picked >> 7).astype(f32).astype(bf16))
    low = mm_nt(pick, (picked & 127).astype(f32).astype(bf16))
    place = iota((count, cap), 1) == lax.rem(iota((count, cap), 0), jnp.int32(cap))
    column = jnp.sum(jnp.where(place, high * 128.0 + low, 0.0), axis=1, keepdims=True)
    item = iota((count, rows_ref.shape[0]), 1).astype(f32)
    chosen = jnp.where(item == column, 1.0, 0.0).astype(bf16)
    copy.wait()
    out_ref[...] = mm(chosen, rows_ref[...]).astype(bf16)


def select_rows(fetch, rows):
    blocks, _, cap = fetch.shape
    return pl.pallas_call(
        select_kernel,
        in_specs=[OUTSIDE, OUTSIDE],
        out_shape=pltpu.VMEM((blocks * cap, rows.shape[1]), bf16),
        scratch_shapes=[
            pltpu.VMEM((1, cap, blocks), i32),
            pltpu.VMEM(rows.shape, bf16),
            pltpu.SemaphoreType.DMA((2,)),
        ],
        compiler_params=PARAMS,
        name="select_rows",
    )(far(fetch.transpose(1, 2, 0)), far(rows))


def tower(rows_ref, w_in_ref, bias, w_out, bias_ref, out_ref, sems):
    small = Copies(bias, bias_ref, sems, 0, 1)
    large = Copies(w_out, out_ref, sems, 1, SPLIT)
    hidden = mm(rows_ref[...], w_in_ref[...])
    small.wait()
    hidden = jnp.maximum(hidden + bias_ref[...], 0.0).astype(bf16)
    large.wait()
    embedding = mm(hidden, out_ref[...])
    total = jnp.sum(embedding * embedding, axis=1, keepdims=True)
    return embedding * lax.rsqrt(total + norm_epsilon)


def neg_kernel(
    own_ref,
    apart_ref,
    w_in_ref,
    bias,
    w_out,
    numbers_ref,
    numbers_apart_ref,
    out_ref,
    rows_ref,
    bias_ref,
    w_out_ref,
    sems,
):
    count = own_ref.shape[0]
    rows_ref[:count, :] = own_ref[...]
    rows_ref[count:, :] = apart_ref[...]
    unit = tower(rows_ref, w_in_ref, bias, w_out, bias_ref, w_out_ref, sems)
    width = unit.shape[1]
    out_ref[:width, :] = unit.T.astype(bf16)
    for start, ref in ((0, numbers_ref), (count, numbers_apart_ref)):
        rows = id_digits(ref[0:1, :]) + (ref[1:2, :].astype(f32),)
        at = iota((EXTRA, count), 0)
        extra = jnp.zeros((EXTRA, count), f32)
        for place, row in enumerate(rows):
            extra = jnp.where(at == place, row, extra)
        out_ref[width:, start : start + count] = extra.astype(bf16)


def neg_tower(own, apart, weights, numbers, numbers_apart):
    count, width = own.shape
    return pl.pallas_call(
        neg_kernel,
        in_specs=[INSIDE, INSIDE, INSIDE, OUTSIDE, OUTSIDE, INSIDE, INSIDE],
        out_shape=pltpu.VMEM((width + EXTRA, 2 * count), bf16),
        scratch_shapes=[
            pltpu.VMEM((2 * count, width), bf16),
            pltpu.VMEM(weights[1].shape, f32),
            pltpu.VMEM(weights[2].shape, bf16),
            pltpu.SemaphoreType.DMA((1 + SPLIT,)),
        ],
        compiler_params=PARAMS,
        name="neg_tower",
    )(near(own), near(apart), *weights, near(numbers), near(numbers_apart))


def event_weights(logits, live):
    raised = [jnp.exp(one) for one in logits]
    total = functools.reduce(jnp.add, raised)
    return [(one / total * live).astype(bf16).astype(f32) for one in raised]


def scatter_weights(weights, upper, onehot_ref, slot_ref):
    users = weights[0].shape[0]
    pages = slot_ref.shape[1] // LANES
    count = pages * INTERESTS * SUB
    for group in range(users // GROUP_USERS):
        at = slice(group * GROUP_USERS, (group + 1) * GROUP_USERS)
        base = jnp.concatenate(
            [
                jnp.where(upper[at] == page, weights[k][at], 0.0)
                for page in range(pages)
                for k in range(INTERESTS)
            ],
            axis=0,
        )
        user = iota((count, 1), 0) & (GROUP_USERS - 1)
        left = jnp.concatenate(
            [
                jnp.where((user >> 1) == pair, base, 0.0).astype(bf16)
                for pair in range(GROUP_USERS // 2)
            ],
            axis=1,
        )
        both = mm_nt(left, onehot_ref[group])
        own = jnp.where((user & 1) == 0, both[:, :LANES], both[:, LANES:])
        for page in range(pages):
            for k in range(INTERESTS):
                source = (page * INTERESTS + k) * SUB
                target = k * users + group * GROUP_USERS
                slot_ref[target : target + SUB, page * LANES : (page + 1) * LANES] = own[
                    source : source + SUB
                ]


def live_mask(length_ref, shape):
    length = to_column(length_ref[...].astype(f32))
    return jnp.where(iota(shape, 1).astype(f32) < length, 1.0, 0.0)


def prepare_kernel(index_ref, length_ref, init_ref, onehot_ref, slot_ref):
    users, events = index_ref.shape
    index = index_ref[...]
    upper = index >> 7
    lower = index & (LANES - 1)
    lane_id = iota((LANES, events), 0)
    for user in range(users):
        group, within = divmod(user, GROUP_USERS)
        pair, side = divmod(within, 2)
        hit = jnp.where(lane_id == lower[user : user + 1], 1.0, 0.0).astype(bf16)
        onehot_ref[
            group, side * LANES : (side + 1) * LANES, pair * events : (pair + 1) * events
        ] = hit
    live = live_mask(length_ref, index.shape)
    weights = event_weights([init_ref[:, k, :] for k in range(INTERESTS)], live)
    scatter_weights(weights, upper, onehot_ref, slot_ref)


def prepare(index, length, init, slots):
    users, events = index.shape
    return pl.pallas_call(
        prepare_kernel,
        out_shape=[
            jax.ShapeDtypeStruct(
                (users // GROUP_USERS, 2 * LANES, GROUP_USERS // 2 * events), bf16
            ),
            pltpu.VMEM((INTERESTS * users, slots), f32),
        ],
        compiler_params=PARAMS,
        name="prepare",
    )(near(index), length, near(init))


def route_kernel(
    rows_ref,
    w_in_ref,
    first_ref,
    bias,
    w_out,
    bilinear,
    onehot,
    index,
    length,
    init,
    label,
    ids,
    counts,
    interests_ref,
    vec_ref,
    positive_ref,
    bias_ref,
    out_ref,
    map_ref,
    onehot_ref,
    index_ref,
    length_ref,
    init_ref,
    label_ref,
    ids_ref,
    counts_ref,
    slot_ref,
    sems,
):
    pairs = (
        (bilinear, map_ref),
        (index, index_ref),
        (length, length_ref),
        (init, init_ref),
        (label, label_ref),
        (ids, ids_ref),
        (counts, counts_ref),
    )
    start = 1 + SPLIT
    others = [Copies(*pair, sems, start + at, 1) for at, pair in enumerate(pairs)]
    unit = tower(rows_ref, w_in_ref, bias, w_out, bias_ref, out_ref, sems).astype(bf16)
    fetch = Copies(onehot, onehot_ref, sems, start + len(pairs), onehot.shape[0])
    for other in others:
        other.wait()
    mapped = mm(unit, map_ref[...]).astype(bf16)
    users, events = index_ref.shape
    slots, width = mapped.shape
    index = index_ref[...]
    upper = index >> 7
    lower = index & (LANES - 1)
    live = live_mask(length_ref, index.shape)
    logits = [init_ref[:, k, :] for k in range(INTERESTS)]
    capsules = None
    for iteration in range(ITERS):
        if iteration == 1:
            fetch.wait()
        if iteration:
            scatter_weights(event_weights(logits, live), upper, onehot_ref, slot_ref)
        slot_weights = first_ref[...] if iteration == 0 else slot_ref[...]
        coarse = slot_weights.astype(bf16)
        rest = (slot_weights - coarse.astype(f32)).astype(bf16)
        sums = mm(coarse, mapped) + mm(rest, mapped)
        norm_sq = jnp.sum(sums * sums, axis=1, keepdims=True)
        capsules = sums * (jnp.sqrt(norm_sq) / (1.0 + norm_sq))
        if iteration + 1 < ITERS:
            scores = mm_nt(capsules.astype(bf16), mapped)
            for k in range(INTERESTS):
                chunks = []
                for at in range(0, events, LANES):
                    low = lower[:, at : at + LANES]
                    high = upper[:, at : at + LANES]
                    found = jnp.zeros((users, LANES), f32)
                    for page in range(slots // LANES):
                        piece = scores[
                            k * users : (k + 1) * users, page * LANES : (page + 1) * LANES
                        ]
                        taken = jnp.take_along_axis(
                            piece, low, axis=1, mode="promise_in_bounds"
                        )
                        found = jnp.where(high == page, taken, found)
                    chunks.append(found)
                logits[k] = logits[k] + jnp.concatenate(chunks, axis=1)
    each = [capsules[k * users : (k + 1) * users] for k in range(INTERESTS)]
    for k in range(INTERESTS):
        interests_ref[:, k * width : (k + 1) * width] = each[k]
    label = to_column(label_ref[...].astype(f32))
    chosen = jnp.where(iota((users, slots), 1).astype(f32) == label, 1.0, 0.0).astype(bf16)
    label_rows = mm(chosen, unit)
    raised = [
        jnp.exp(attend_scale * jnp.sum(one * label_rows, axis=1, keepdims=True)) for one in each
    ]
    total = functools.reduce(jnp.add, raised)
    user_vec = functools.reduce(jnp.add, [(r / total) * one for r, one in zip(raised, each)])
    user_vec = user_vec.astype(bf16)
    vec_ref[:, :width] = user_vec
    vec_ref[:, width:] = lane_columns([to_column(one) for one in id_digits(ids_ref[...])], users).astype(bf16)
    match = jnp.sum(user_vec.astype(f32) * label_rows, axis=1, keepdims=True)
    positive_ref[...] = logit_scale * to_row(match) - jnp.log(counts_ref[...].astype(f32))


def route(rows, w_in, first, *others):
    _, _, bilinear, onehot, index, _, _, _, _, _ = others
    users = index.shape[0]
    width = bilinear.shape[1]
    return pl.pallas_call(
        route_kernel,
        in_specs=[INSIDE] * 3 + [OUTSIDE] * len(others),
        out_shape=[
            jax.ShapeDtypeStruct((users, INTERESTS * width), f32),
            pltpu.VMEM((users, width + LANES), bf16),
            pltpu.VMEM((1, users), f32),
        ],
        scratch_shapes=[pltpu.VMEM(one.shape, one.dtype) for one in others]
        + [
            pltpu.VMEM(first.shape, f32),
            pltpu.SemaphoreType.DMA((SPLIT + len(others) - 1 + onehot.shape[0],)),
        ],
        compiler_params=PARAMS,
        name="route",
    )(near(rows), near(w_in), near(first), *[far(one) for one in others])


def sums_kernel(parts, pieces, *refs):
    vec_refs = refs[:parts]
    neg_refs = refs[parts : parts + pieces]
    out_refs = refs[parts + pieces :]
    vec = jnp.concatenate([ref[...] for ref in vec_refs], axis=0)
    users = vec_refs[0].shape[0]
    width = vec.shape[1] - LANES
    digits = vec[:, width:].astype(f32)
    label_ids = digits[:, 0:1] + 256.0 * digits[:, 1:2] + 65536.0 * digits[:, 2:3]
    vec = vec[:, :width]
    total = None
    for ref in neg_refs:
        extra = ref[width:, :].astype(f32)
        ids = extra[0:1] + 256.0 * extra[1:2] + 65536.0 * extra[2:3]
        terms = jnp.exp(logit_scale * mm(vec, ref[:width, :])) * (1.0 / extra[3:4])
        terms = jnp.where(ids != label_ids, terms, 0.0)
        total = terms if total is None else total + terms
    total = to_row(jnp.sum(total, axis=1, keepdims=True))
    for part, ref in enumerate(out_refs):
        ref[...] = total[:, part * users : (part + 1) * users]


def negative_sums(vecs, negs):
    users = vecs[0].shape[0]
    return pl.pallas_call(
        functools.partial(sums_kernel, len(vecs), len(negs)),
        out_shape=[pltpu.VMEM((1, users), f32) for _ in vecs],
        compiler_params=PARAMS,
        name="negative_sums",
    )(*[near(one) for one in [*vecs, *negs]])


def swap_pool(array, size, bit):
    return lax.ppermute(array, "pool", [(at, at ^ bit) for at in range(size)])


def rotate_user(array, size, step):
    return lax.ppermute(array, "user", [(at, (at + step) % size) for at in range(size)])


def gather_negatives(own, bits, size):
    pieces = {0: own}
    for mask in range(1, 1 << len(bits)):
        last = mask.bit_length() - 1
        pieces[mask] = swap_pool(pieces[mask ^ (1 << last)], size, bits[last])
    return list(pieces.values())


def on_device(
    user_size,
    pool_size,
    item_feats,
    w_in,
    bias_in,
    w_out,
    bilinear,
    fetch_table,
    hist_index,
    hist_len,
    route_init,
    label_index,
    label_ids,
    label_counts,
    neg_feats,
    neg_ids,
    neg_counts,
):
    weights = (near(w_in), far(bias_in.reshape(1, -1)), far(w_out))
    apart = swap_pool(neg_feats, pool_size, pool_size // 2)
    outgoing = select_rows(fetch_table, item_feats)
    arrived = lax.all_to_all(
        outgoing.reshape(fetch_table.shape[0], fetch_table.shape[2], -1),
        ("user", "pool"),
        split_axis=0,
        concat_axis=0,
        tiled=True,
    )
    arrived = arrived.reshape(outgoing.shape)

    numbers = jnp.stack([neg_ids, neg_counts])
    numbers_apart = swap_pool(numbers, pool_size, pool_size // 2)
    own_neg = neg_tower(neg_feats, apart, weights, numbers, numbers_apart)
    length = hist_len.reshape(1, -1)
    onehot, first = prepare(hist_index, length, route_init, outgoing.shape[0])
    bits = [1 << at for at in range(pool_size.bit_length() - 2)]
    negs = gather_negatives(own_neg, bits[1:] + bits[:1], pool_size)

    interests, vec, positive = route(
        arrived,
        w_in,
        first,
        bias_in.reshape(1, -1),
        w_out,
        bilinear,
        onehot,
        hist_index,
        length,
        route_init,
        label_index.reshape(1, -1),
        label_ids.reshape(1, -1),
        label_counts.reshape(1, -1),
    )
    vecs = [vec] + [rotate_user(vec, user_size, step) for step in range(1, user_size)]
    sums = negative_sums(vecs, negs)
    partition = jnp.exp(positive) + sums[0]
    for step in range(1, user_size):
        partition += rotate_user(sums[step], user_size, user_size - step)
    user_loss = jnp.log(partition) - positive
    return (interests, user_loss.reshape(-1))


def solution(mesh):
    both = ("user", "pool")
    in_specs = (
        P(both, None),
        P(),
        P(),
        P(),
        P(),
        P(None, both, None),
        P(both, None),
        P(both),
        P(both, None, None),
        P(both),
        P(both),
        P(both),
        P(both, None),
        P(both),
        P(both),
    )
    out_specs = (P(both, None), P(both))

    def body(*args):
        return on_device(mesh.shape["user"], mesh.shape["pool"], *args)

    return jax.shard_map(body, mesh=mesh, in_specs=in_specs, out_specs=out_specs, check_vma=False)
```

```python
import functools

import jax
import jax.numpy as jnp
from jax import lax
from jax.experimental import pallas as pl
from jax.experimental.pallas import tpu as pltpu
from jax.sharding import PartitionSpec as P


INTERESTS = 4
ITERS = 3
LANES = 128
SUB = 8
EXTRA = 16
SPLIT = 4
GROUP_USERS = 8

norm_epsilon = 1e-06
attend_scale = 8.0
logit_scale = 20.0

f32 = jnp.float32
bf16 = jnp.bfloat16
i32 = jnp.int32


INSIDE = pl.BlockSpec(memory_space=pltpu.VMEM)
OUTSIDE = pl.BlockSpec(memory_space=pltpu.HBM)
PARAMS = pltpu.CompilerParams(vmem_limit_bytes=20 << 20)


def near(array):
    return pltpu.with_memory_space_constraint(array, pltpu.VMEM)


def far(array):
    return pltpu.with_memory_space_constraint(array, pltpu.HBM)


def mm(a, b):
    return jnp.dot(a, b, preferred_element_type=f32)


def mm_nt(a, b):
    return lax.dot_general(a, b, (((1,), (1,)), ((), ())), preferred_element_type=f32)


def iota(shape, axis):
    return lax.broadcasted_iota(i32, shape, axis)


def to_column(row):
    n = row.shape[1]
    eye = iota((n, n), 0) == iota((n, n), 1)
    return jnp.sum(jnp.where(eye, row, 0.0), axis=1, keepdims=True)


def to_row(column):
    n = column.shape[0]
    eye = iota((n, n), 0) == iota((n, n), 1)
    return jnp.sum(jnp.where(eye, column, 0.0), axis=0, keepdims=True)


def id_digits(ids_row):
    low = (ids_row & 255).astype(f32)
    mid = ((ids_row >> 8) & 255).astype(f32)
    high = (ids_row >> 16).astype(f32)
    return low, mid, high


def lane_columns(columns, rows):
    lane = iota((rows, LANES), 1)
    out = jnp.zeros((rows, LANES), f32)
    for at, column in enumerate(columns):
        out = jnp.where(lane == at, column, out)
    return out


class Copies:
    def __init__(self, source, target, sems, first, count):
        size = source.shape[0] // count
        self.copies = [
            pltpu.make_async_copy(
                source.at[pl.ds(at * size, size)],
                target.at[pl.ds(at * size, size)],
                sems.at[first + at],
            )
            for at in range(count)
        ]
        for copy in self.copies:
            copy.start()

    def wait(self):
        for copy in self.copies:
            copy.wait()


def select_kernel(
    fetch,
    rows,
    negs,
    ids,
    counts,
    out_ref,
    packed,
    fetch_ref,
    rows_ref,
    extra_ref,
    ids_ref,
    counts_ref,
    sems,
):
    small = [
        Copies(ids, ids_ref, sems, 4, 1),
        Copies(counts, counts_ref, sems, 5, 1),
    ]
    kept = negs.shape[0]
    body = pltpu.make_async_copy(negs, packed.at[pl.ds(0, kept)], sems.at[2])
    body.start()
    table = pltpu.make_async_copy(fetch, fetch_ref, sems.at[0])
    table.start()
    copy = pltpu.make_async_copy(rows, rows_ref, sems.at[1])
    copy.start()
    _, cap, blocks = fetch_ref.shape
    count = blocks * cap
    row = iota((count, blocks), 0)
    block = iota((count, blocks), 1)
    pick = jnp.where((row >= block * cap) & (row < block * cap + cap), 1.0, 0.0).astype(bf16)
    for one in small:
        one.wait()
    numbers = id_digits(ids_ref[...]) + (counts_ref[...].astype(f32),)
    at = iota((EXTRA, kept), 0)
    extra = jnp.zeros((EXTRA, kept), f32)
    for place, one in enumerate(numbers):
        extra = jnp.where(at == place, one, extra)
    extra_ref[...] = jnp.zeros(extra_ref.shape, bf16)
    extra_ref[:, :kept] = extra.astype(bf16)
    tail = pltpu.make_async_copy(extra_ref, packed.at[pl.ds(kept, EXTRA)], sems.at[3])
    tail.start()
    table.wait()
    picked = fetch_ref[0]
    high = mm_nt(pick, (picked >> 7).astype(f32).astype(bf16))
    low = mm_nt(pick, (picked & 127).astype(f32).astype(bf16))
    place = iota((count, cap), 1) == lax.rem(iota((count, cap), 0), jnp.int32(cap))
    column = jnp.sum(jnp.where(place, high * 128.0 + low, 0.0), axis=1, keepdims=True)
    item = iota((count, rows_ref.shape[0]), 1).astype(f32)
    chosen = jnp.where(item == column, 1.0, 0.0).astype(bf16)
    copy.wait()
    out_ref[...] = mm(chosen, rows_ref[...]).astype(bf16)
    body.wait()
    tail.wait()


def select_rows(fetch, rows, negs, ids, counts):
    blocks, _, cap = fetch.shape
    packed = (negs.shape[0] + EXTRA, negs.shape[1])
    return pl.pallas_call(
        select_kernel,
        in_specs=[OUTSIDE] * 5,
        out_specs=[INSIDE, OUTSIDE],
        out_shape=[
            pltpu.VMEM((blocks * cap, rows.shape[1]), bf16),
            jax.ShapeDtypeStruct(packed, bf16),
        ],
        scratch_shapes=[
            pltpu.VMEM((1, cap, blocks), i32),
            pltpu.VMEM(rows.shape, bf16),
            pltpu.VMEM((EXTRA, negs.shape[1]), bf16),
            pltpu.VMEM(ids.shape, i32),
            pltpu.VMEM(counts.shape, i32),
            pltpu.SemaphoreType.DMA((6,)),
        ],
        compiler_params=PARAMS,
        name="select_rows",
    )(*[far(one) for one in (fetch.transpose(1, 2, 0), rows, negs, ids, counts)])


def tower(rows_ref, w_in_ref, bias, w_out, bias_ref, out_ref, sems):
    small = Copies(bias, bias_ref, sems, 0, 1)
    large = Copies(w_out, out_ref, sems, 1, SPLIT)
    hidden = mm(rows_ref[...], w_in_ref[...])
    small.wait()
    hidden = jnp.maximum(hidden + bias_ref[...], 0.0).astype(bf16)
    large.wait()
    embedding = mm(hidden, out_ref[...])
    total = jnp.sum(embedding * embedding, axis=1, keepdims=True)
    return embedding * lax.rsqrt(total + norm_epsilon)


def neg_kernel(
    own_ref, apart_ref, w_in_ref, bias, w_out, out_ref, rows_ref, bias_ref, w_out_ref, sems
):
    count = rows_ref.shape[0] // 2
    rows_ref[:count, :] = own_ref[:count, :]
    rows_ref[count:, :] = apart_ref[:count, :]
    unit = tower(rows_ref, w_in_ref, bias, w_out, bias_ref, w_out_ref, sems)
    width = unit.shape[1]
    out_ref[:width, :] = unit.T.astype(bf16)
    out_ref[width:, :count] = own_ref[count:, :count]
    out_ref[width:, count:] = apart_ref[count:, :count]


def neg_tower(own, apart, weights):
    count = own.shape[0] - EXTRA
    width = own.shape[1]
    return pl.pallas_call(
        neg_kernel,
        in_specs=[INSIDE, INSIDE, INSIDE, OUTSIDE, OUTSIDE],
        out_shape=pltpu.VMEM((width + EXTRA, 2 * count), bf16),
        scratch_shapes=[
            pltpu.VMEM((2 * count, width), bf16),
            pltpu.VMEM(weights[1].shape, f32),
            pltpu.VMEM(weights[2].shape, bf16),
            pltpu.SemaphoreType.DMA((1 + SPLIT,)),
        ],
        compiler_params=PARAMS,
        name="neg_tower",
    )(near(own), near(apart), *weights)


def event_weights(logits, live):
    raised = [jnp.exp(one) for one in logits]
    total = functools.reduce(jnp.add, raised)
    return [(one / total * live).astype(bf16).astype(f32) for one in raised]


def scatter_weights(weights, upper, onehot_ref, slot_ref):
    users = weights[0].shape[0]
    pages = slot_ref.shape[1] // LANES
    count = pages * INTERESTS * SUB
    for group in range(users // GROUP_USERS):
        at = slice(group * GROUP_USERS, (group + 1) * GROUP_USERS)
        base = jnp.concatenate(
            [
                jnp.where(upper[at] == page, weights[k][at], 0.0)
                for page in range(pages)
                for k in range(INTERESTS)
            ],
            axis=0,
        )
        user = iota((count, 1), 0) & (GROUP_USERS - 1)
        left = jnp.concatenate(
            [
                jnp.where((user >> 1) == pair, base, 0.0).astype(bf16)
                for pair in range(GROUP_USERS // 2)
            ],
            axis=1,
        )
        both = mm_nt(left, onehot_ref[group])
        own = jnp.where((user & 1) == 0, both[:, :LANES], both[:, LANES:])
        for page in range(pages):
            for k in range(INTERESTS):
                source = (page * INTERESTS + k) * SUB
                target = k * users + group * GROUP_USERS
                slot_ref[target : target + SUB, page * LANES : (page + 1) * LANES] = own[
                    source : source + SUB
                ]


def live_mask(length_ref, shape):
    length = to_column(length_ref[...].astype(f32))
    return jnp.where(iota(shape, 1).astype(f32) < length, 1.0, 0.0)


def prepare_kernel(index_ref, length_ref, init_ref, onehot_ref, slot_ref):
    users, events = index_ref.shape
    index = index_ref[...]
    upper = index >> 7
    lower = index & (LANES - 1)
    lane_id = iota((LANES, events), 0)
    for user in range(users):
        group, within = divmod(user, GROUP_USERS)
        pair, side = divmod(within, 2)
        hit = jnp.where(lane_id == lower[user : user + 1], 1.0, 0.0).astype(bf16)
        onehot_ref[
            group, side * LANES : (side + 1) * LANES, pair * events : (pair + 1) * events
        ] = hit
    live = live_mask(length_ref, index.shape)
    weights = event_weights([init_ref[:, k, :] for k in range(INTERESTS)], live)
    scatter_weights(weights, upper, onehot_ref, slot_ref)


def prepare(index, length, init, slots):
    users, events = index.shape
    return pl.pallas_call(
        prepare_kernel,
        out_shape=[
            jax.ShapeDtypeStruct(
                (users // GROUP_USERS, 2 * LANES, GROUP_USERS // 2 * events), bf16
            ),
            pltpu.VMEM((INTERESTS * users, slots), f32),
        ],
        compiler_params=PARAMS,
        name="prepare",
    )(near(index), length, near(init))


def route_kernel(
    rows_ref,
    w_in_ref,
    first_ref,
    bias,
    w_out,
    bilinear,
    onehot,
    index,
    length,
    init,
    label,
    ids,
    counts,
    interests_ref,
    vec_ref,
    positive_ref,
    bias_ref,
    out_ref,
    map_ref,
    onehot_ref,
    index_ref,
    length_ref,
    init_ref,
    label_ref,
    ids_ref,
    counts_ref,
    slot_ref,
    sems,
):
    pairs = (
        (bilinear, map_ref),
        (index, index_ref),
        (length, length_ref),
        (init, init_ref),
        (label, label_ref),
        (ids, ids_ref),
        (counts, counts_ref),
    )
    start = 1 + SPLIT
    others = [Copies(*pair, sems, start + at, 1) for at, pair in enumerate(pairs)]
    unit = tower(rows_ref, w_in_ref, bias, w_out, bias_ref, out_ref, sems).astype(bf16)
    fetch = Copies(onehot, onehot_ref, sems, start + len(pairs), onehot.shape[0])
    for other in others:
        other.wait()
    mapped = mm(unit, map_ref[...]).astype(bf16)
    users, events = index_ref.shape
    slots, width = mapped.shape
    index = index_ref[...]
    upper = index >> 7
    lower = index & (LANES - 1)
    live = live_mask(length_ref, index.shape)
    logits = [init_ref[:, k, :] for k in range(INTERESTS)]
    capsules = None
    for iteration in range(ITERS):
        if iteration == 1:
            fetch.wait()
        if iteration:
            scatter_weights(event_weights(logits, live), upper, onehot_ref, slot_ref)
        slot_weights = first_ref[...] if iteration == 0 else slot_ref[...]
        coarse = slot_weights.astype(bf16)
        rest = (slot_weights - coarse.astype(f32)).astype(bf16)
        sums = mm(coarse, mapped) + mm(rest, mapped)
        norm_sq = jnp.sum(sums * sums, axis=1, keepdims=True)
        capsules = sums * (jnp.sqrt(norm_sq) / (1.0 + norm_sq))
        if iteration + 1 < ITERS:
            scores = mm_nt(capsules.astype(bf16), mapped)
            for k in range(INTERESTS):
                chunks = []
                for at in range(0, events, LANES):
                    low = lower[:, at : at + LANES]
                    high = upper[:, at : at + LANES]
                    found = jnp.zeros((users, LANES), f32)
                    for page in range(slots // LANES):
                        piece = scores[
                            k * users : (k + 1) * users, page * LANES : (page + 1) * LANES
                        ]
                        taken = jnp.take_along_axis(
                            piece, low, axis=1, mode="promise_in_bounds"
                        )
                        found = jnp.where(high == page, taken, found)
                    chunks.append(found)
                logits[k] = logits[k] + jnp.concatenate(chunks, axis=1)
    each = [capsules[k * users : (k + 1) * users] for k in range(INTERESTS)]
    for k in range(INTERESTS):
        interests_ref[:, k * width : (k + 1) * width] = each[k]
    label = to_column(label_ref[...].astype(f32))
    chosen = jnp.where(iota((users, slots), 1).astype(f32) == label, 1.0, 0.0).astype(bf16)
    label_rows = mm(chosen, unit)
    raised = [
        jnp.exp(attend_scale * jnp.sum(one * label_rows, axis=1, keepdims=True)) for one in each
    ]
    total = functools.reduce(jnp.add, raised)
    user_vec = functools.reduce(jnp.add, [(r / total) * one for r, one in zip(raised, each)])
    user_vec = user_vec.astype(bf16)
    vec_ref[:, :width] = user_vec
    vec_ref[:, width:] = lane_columns([to_column(one) for one in id_digits(ids_ref[...])], users).astype(bf16)
    match = jnp.sum(user_vec.astype(f32) * label_rows, axis=1, keepdims=True)
    positive_ref[...] = logit_scale * to_row(match) - jnp.log(counts_ref[...].astype(f32))


def route(rows, w_in, first, *others):
    _, _, bilinear, onehot, index, _, _, _, _, _ = others
    users = index.shape[0]
    width = bilinear.shape[1]
    return pl.pallas_call(
        route_kernel,
        in_specs=[INSIDE] * 3 + [OUTSIDE] * len(others),
        out_shape=[
            jax.ShapeDtypeStruct((users, INTERESTS * width), f32),
            pltpu.VMEM((users, width + LANES), bf16),
            pltpu.VMEM((1, users), f32),
        ],
        scratch_shapes=[pltpu.VMEM(one.shape, one.dtype) for one in others]
        + [
            pltpu.VMEM(first.shape, f32),
            pltpu.SemaphoreType.DMA((SPLIT + len(others) - 1 + onehot.shape[0],)),
        ],
        compiler_params=PARAMS,
        name="route",
    )(near(rows), near(w_in), near(first), *[far(one) for one in others])


def sums_kernel(parts, pieces, *refs):
    vec_refs = refs[:parts]
    neg_refs = refs[parts : parts + pieces]
    out_refs = refs[parts + pieces :]
    vec = jnp.concatenate([ref[...] for ref in vec_refs], axis=0)
    users = vec_refs[0].shape[0]
    width = vec.shape[1] - LANES
    digits = vec[:, width:].astype(f32)
    label_ids = digits[:, 0:1] + 256.0 * digits[:, 1:2] + 65536.0 * digits[:, 2:3]
    vec = vec[:, :width]
    total = None
    for ref in neg_refs:
        extra = ref[width:, :].astype(f32)
        ids = extra[0:1] + 256.0 * extra[1:2] + 65536.0 * extra[2:3]
        terms = jnp.exp(logit_scale * mm(vec, ref[:width, :])) * (1.0 / extra[3:4])
        terms = jnp.where(ids != label_ids, terms, 0.0)
        total = terms if total is None else total + terms
    total = to_row(jnp.sum(total, axis=1, keepdims=True))
    for part, ref in enumerate(out_refs):
        ref[...] = total[:, part * users : (part + 1) * users]


def negative_sums(vecs, negs):
    users = vecs[0].shape[0]
    return pl.pallas_call(
        functools.partial(sums_kernel, len(vecs), len(negs)),
        out_shape=[pltpu.VMEM((1, users), f32) for _ in vecs],
        compiler_params=PARAMS,
        name="negative_sums",
    )(*[near(one) for one in [*vecs, *negs]])


def swap_pool(array, size, bit):
    return lax.ppermute(array, "pool", [(at, at ^ bit) for at in range(size)])


def rotate_user(array, size, step):
    return lax.ppermute(array, "user", [(at, (at + step) % size) for at in range(size)])


def gather_negatives(own, bits, size):
    pieces = {0: own}
    for mask in range(1, 1 << len(bits)):
        last = mask.bit_length() - 1
        pieces[mask] = swap_pool(pieces[mask ^ (1 << last)], size, bits[last])
    return list(pieces.values())


def on_device(
    user_size,
    pool_size,
    item_feats,
    w_in,
    bias_in,
    w_out,
    bilinear,
    fetch_table,
    hist_index,
    hist_len,
    route_init,
    label_index,
    label_ids,
    label_counts,
    neg_feats,
    neg_ids,
    neg_counts,
):
    weights = (near(w_in), far(bias_in.reshape(1, -1)), far(w_out))
    outgoing, packed = select_rows(
        fetch_table, item_feats, neg_feats, neg_ids.reshape(1, -1), neg_counts.reshape(1, -1)
    )
    apart = swap_pool(packed, pool_size, pool_size // 2)
    arrived = lax.all_to_all(
        outgoing.reshape(fetch_table.shape[0], fetch_table.shape[2], -1),
        ("user", "pool"),
        split_axis=0,
        concat_axis=0,
        tiled=True,
    )
    arrived = arrived.reshape(outgoing.shape)

    own_neg = neg_tower(packed, apart, weights)
    length = hist_len.reshape(1, -1)
    onehot, first = prepare(hist_index, length, route_init, outgoing.shape[0])
    bits = [1 << at for at in range(pool_size.bit_length() - 2)]
    negs = gather_negatives(own_neg, bits[1:] + bits[:1], pool_size)

    interests, vec, positive = route(
        arrived,
        w_in,
        first,
        bias_in.reshape(1, -1),
        w_out,
        bilinear,
        onehot,
        hist_index,
        length,
        route_init,
        label_index.reshape(1, -1),
        label_ids.reshape(1, -1),
        label_counts.reshape(1, -1),
    )
    vecs = [vec] + [rotate_user(vec, user_size, step) for step in range(1, user_size)]
    sums = negative_sums(vecs, negs)
    partition = jnp.exp(positive) + sums[0]
    for step in range(1, user_size):
        partition += rotate_user(sums[step], user_size, user_size - step)
    user_loss = jnp.log(partition) - positive
    return (interests, user_loss.reshape(-1))


def solution(mesh):
    both = ("user", "pool")
    in_specs = (
        P(both, None),
        P(),
        P(),
        P(),
        P(),
        P(None, both, None),
        P(both, None),
        P(both),
        P(both, None, None),
        P(both),
        P(both),
        P(both),
        P(both, None),
        P(both),
        P(both),
    )
    out_specs = (P(both, None), P(both))

    def body(*args):
        return on_device(mesh.shape["user"], mesh.shape["pool"], *args)

    return jax.shard_map(body, mesh=mesh, in_specs=in_specs, out_specs=out_specs, check_vma=False)
```

```python
import functools

import jax
import jax.numpy as jnp
from jax import lax
from jax.experimental import pallas as pl
from jax.experimental.pallas import tpu as pltpu
from jax.sharding import PartitionSpec as P


INTERESTS = 4
ITERS = 3
LANES = 128
SUB = 8
EXTRA = 16
SPLIT = 4
GROUP_USERS = 8

norm_epsilon = 1e-06
attend_scale = 8.0
logit_scale = 20.0

f32 = jnp.float32
bf16 = jnp.bfloat16
i32 = jnp.int32


INSIDE = pl.BlockSpec(memory_space=pltpu.VMEM)
OUTSIDE = pl.BlockSpec(memory_space=pltpu.HBM)
PARAMS = pltpu.CompilerParams(vmem_limit_bytes=20 << 20)


def near(array):
    return pltpu.with_memory_space_constraint(array, pltpu.VMEM)


def far(array):
    return pltpu.with_memory_space_constraint(array, pltpu.HBM)


def mm(a, b):
    return jnp.dot(a, b, preferred_element_type=f32)


def mm_nt(a, b):
    return lax.dot_general(a, b, (((1,), (1,)), ((), ())), preferred_element_type=f32)


def iota(shape, axis):
    return lax.broadcasted_iota(i32, shape, axis)


def to_column(row):
    n = row.shape[1]
    eye = iota((n, n), 0) == iota((n, n), 1)
    return jnp.sum(jnp.where(eye, row, 0.0), axis=1, keepdims=True)


def to_row(column):
    n = column.shape[0]
    eye = iota((n, n), 0) == iota((n, n), 1)
    return jnp.sum(jnp.where(eye, column, 0.0), axis=0, keepdims=True)


def id_digits(ids_row):
    low = (ids_row & 255).astype(f32)
    mid = ((ids_row >> 8) & 255).astype(f32)
    high = (ids_row >> 16).astype(f32)
    return low, mid, high


def lane_columns(columns, rows):
    lane = iota((rows, LANES), 1)
    out = jnp.zeros((rows, LANES), f32)
    for at, column in enumerate(columns):
        out = jnp.where(lane == at, column, out)
    return out


class Copies:
    def __init__(self, source, target, sems, first, count):
        size = source.shape[0] // count
        self.copies = [
            pltpu.make_async_copy(
                source.at[pl.ds(at * size, size)],
                target.at[pl.ds(at * size, size)],
                sems.at[first + at],
            )
            for at in range(count)
        ]
        for copy in self.copies:
            copy.start()

    def wait(self):
        for copy in self.copies:
            copy.wait()


def select_kernel(
    fetch,
    rows,
    negs,
    ids,
    counts,
    out_ref,
    packed,
    fetch_ref,
    rows_ref,
    extra_ref,
    ids_ref,
    counts_ref,
    sems,
):
    small = [
        Copies(ids, ids_ref, sems, 4, 1),
        Copies(counts, counts_ref, sems, 5, 1),
    ]
    kept = negs.shape[0]
    body = pltpu.make_async_copy(negs, packed.at[pl.ds(0, kept)], sems.at[2])
    body.start()
    table = pltpu.make_async_copy(fetch, fetch_ref, sems.at[0])
    table.start()
    copy = pltpu.make_async_copy(rows, rows_ref, sems.at[1])
    copy.start()
    _, cap, blocks = fetch_ref.shape
    count = blocks * cap
    row = iota((count, blocks), 0)
    block = iota((count, blocks), 1)
    pick = jnp.where((row >= block * cap) & (row < block * cap + cap), 1.0, 0.0).astype(bf16)
    for one in small:
        one.wait()
    numbers = id_digits(ids_ref[...]) + (counts_ref[...].astype(f32),)
    at = iota((EXTRA, kept), 0)
    extra = jnp.zeros((EXTRA, kept), f32)
    for place, one in enumerate(numbers):
        extra = jnp.where(at == place, one, extra)
    extra_ref[...] = jnp.zeros(extra_ref.shape, bf16)
    extra_ref[:, :kept] = extra.astype(bf16)
    tail = pltpu.make_async_copy(extra_ref, packed.at[pl.ds(kept, EXTRA)], sems.at[3])
    tail.start()
    table.wait()
    picked = fetch_ref[0]
    high = mm_nt(pick, (picked >> 7).astype(f32).astype(bf16))
    low = mm_nt(pick, (picked & 127).astype(f32).astype(bf16))
    place = iota((count, cap), 1) == lax.rem(iota((count, cap), 0), jnp.int32(cap))
    column = jnp.sum(jnp.where(place, high * 128.0 + low, 0.0), axis=1, keepdims=True)
    item = iota((count, rows_ref.shape[0]), 1).astype(f32)
    chosen = jnp.where(item == column, 1.0, 0.0).astype(bf16)
    copy.wait()
    out_ref[...] = mm(chosen, rows_ref[...]).astype(bf16)
    body.wait()
    tail.wait()


def select_rows(fetch, rows, negs, ids, counts):
    blocks, _, cap = fetch.shape
    packed = (negs.shape[0] + EXTRA, negs.shape[1])
    return pl.pallas_call(
        select_kernel,
        in_specs=[OUTSIDE] * 5,
        out_specs=[INSIDE, OUTSIDE],
        out_shape=[
            pltpu.VMEM((blocks * cap, rows.shape[1]), bf16),
            jax.ShapeDtypeStruct(packed, bf16),
        ],
        scratch_shapes=[
            pltpu.VMEM((1, cap, blocks), i32),
            pltpu.VMEM(rows.shape, bf16),
            pltpu.VMEM((EXTRA, negs.shape[1]), bf16),
            pltpu.VMEM(ids.shape, i32),
            pltpu.VMEM(counts.shape, i32),
            pltpu.SemaphoreType.DMA((6,)),
        ],
        compiler_params=PARAMS,
        name="select_rows",
    )(*[far(one) for one in (fetch.transpose(1, 2, 0), rows, negs, ids, counts)])


def tower(rows_ref, w_in_ref, bias, w_out, bias_ref, out_ref, sems, parts=None):
    small = Copies(bias, bias_ref, sems, 0, 1)
    large = Copies(w_out, out_ref, sems, 1, SPLIT)
    if parts is None:
        hidden = mm(rows_ref[...], w_in_ref[...])
        small.wait()
        hidden = jnp.maximum(hidden + bias_ref[...], 0.0).astype(bf16)
    else:
        small.wait()
        pieces = []
        for at, part in enumerate(parts):
            part.wait()
            size = w_in_ref.shape[1] // len(parts)
            cut = slice(at * size, (at + 1) * size)
            piece = mm(rows_ref[...], w_in_ref[:, cut]) + bias_ref[:, cut]
            pieces.append(jnp.maximum(piece, 0.0).astype(bf16))
        hidden = jnp.concatenate(pieces, axis=1)
    large.wait()
    embedding = mm(hidden, out_ref[...])
    total = jnp.sum(embedding * embedding, axis=1, keepdims=True)
    return embedding * lax.rsqrt(total + norm_epsilon)


def neg_kernel(
    own_ref, apart_ref, w_in, bias, w_out, out_ref, rows_ref, w_in_ref, bias_ref, w_out_ref, sems
):
    size = w_in.shape[1] // SPLIT
    parts = [
        pltpu.make_async_copy(
            w_in.at[:, pl.ds(at * size, size)],
            w_in_ref.at[:, pl.ds(at * size, size)],
            sems.at[1 + SPLIT + at],
        )
        for at in range(SPLIT)
    ]
    for part in parts:
        part.start()
    count = rows_ref.shape[0] // 2
    rows_ref[:count, :] = own_ref[:count, :]
    rows_ref[count:, :] = apart_ref[:count, :]
    unit = tower(rows_ref, w_in_ref, bias, w_out, bias_ref, w_out_ref, sems, parts)
    width = unit.shape[1]
    out_ref[:width, :] = unit.T.astype(bf16)
    out_ref[width:, :count] = own_ref[count:, :count]
    out_ref[width:, count:] = apart_ref[count:, :count]


def neg_tower(own, apart, weights):
    count = own.shape[0] - EXTRA
    width = own.shape[1]
    return pl.pallas_call(
        neg_kernel,
        in_specs=[INSIDE, INSIDE, OUTSIDE, OUTSIDE, OUTSIDE],
        out_shape=pltpu.VMEM((width + EXTRA, 2 * count), bf16),
        scratch_shapes=[pltpu.VMEM((2 * count, width), bf16)]
        + [pltpu.VMEM(one.shape, one.dtype) for one in weights]
        + [pltpu.SemaphoreType.DMA((1 + 2 * SPLIT,))],
        compiler_params=PARAMS,
        name="neg_tower",
    )(near(own), near(apart), *[far(one) for one in weights])


def event_weights(logits, live):
    raised = [jnp.exp(one) for one in logits]
    total = functools.reduce(jnp.add, raised)
    return [(one / total * live).astype(bf16).astype(f32) for one in raised]


def scatter_weights(weights, upper, onehot_ref, slot_ref):
    users = weights[0].shape[0]
    pages = slot_ref.shape[1] // LANES
    count = pages * INTERESTS * SUB
    for group in range(users // GROUP_USERS):
        at = slice(group * GROUP_USERS, (group + 1) * GROUP_USERS)
        base = jnp.concatenate(
            [
                jnp.where(upper[at] == page, weights[k][at], 0.0)
                for page in range(pages)
                for k in range(INTERESTS)
            ],
            axis=0,
        )
        user = iota((count, 1), 0) & (GROUP_USERS - 1)
        left = jnp.concatenate(
            [
                jnp.where((user >> 1) == pair, base, 0.0).astype(bf16)
                for pair in range(GROUP_USERS // 2)
            ],
            axis=1,
        )
        both = mm_nt(left, onehot_ref[group])
        own = jnp.where((user & 1) == 0, both[:, :LANES], both[:, LANES:])
        for page in range(pages):
            for k in range(INTERESTS):
                source = (page * INTERESTS + k) * SUB
                target = k * users + group * GROUP_USERS
                slot_ref[target : target + SUB, page * LANES : (page + 1) * LANES] = own[
                    source : source + SUB
                ]


def live_mask(length_ref, shape):
    length = to_column(length_ref[...].astype(f32))
    return jnp.where(iota(shape, 1).astype(f32) < length, 1.0, 0.0)


def prepare_kernel(index_ref, length_ref, init_ref, onehot_ref, slot_ref):
    users, events = index_ref.shape
    index = index_ref[...]
    upper = index >> 7
    lower = index & (LANES - 1)
    lane_id = iota((LANES, events), 0)
    for user in range(users):
        group, within = divmod(user, GROUP_USERS)
        pair, side = divmod(within, 2)
        hit = jnp.where(lane_id == lower[user : user + 1], 1.0, 0.0).astype(bf16)
        onehot_ref[
            group, side * LANES : (side + 1) * LANES, pair * events : (pair + 1) * events
        ] = hit
    live = live_mask(length_ref, index.shape)
    weights = event_weights([init_ref[:, k, :] for k in range(INTERESTS)], live)
    scatter_weights(weights, upper, onehot_ref, slot_ref)


def prepare(index, length, init, slots):
    users, events = index.shape
    return pl.pallas_call(
        prepare_kernel,
        out_shape=[
            jax.ShapeDtypeStruct(
                (users // GROUP_USERS, 2 * LANES, GROUP_USERS // 2 * events), bf16
            ),
            jax.ShapeDtypeStruct((INTERESTS * users, slots), f32),
        ],
        compiler_params=PARAMS,
        name="prepare",
    )(near(index), length, near(init))


def route_kernel(
    rows_ref,
    w_in_ref,
    bias,
    w_out,
    bilinear,
    onehot,
    first,
    index,
    length,
    init,
    label,
    ids,
    counts,
    interests_ref,
    vec_ref,
    positive_ref,
    bias_ref,
    out_ref,
    map_ref,
    onehot_ref,
    first_ref,
    index_ref,
    length_ref,
    init_ref,
    label_ref,
    ids_ref,
    counts_ref,
    slot_ref,
    sems,
):
    pairs = (
        (bilinear, map_ref),
        (first, first_ref),
        (index, index_ref),
        (length, length_ref),
        (init, init_ref),
        (label, label_ref),
        (ids, ids_ref),
        (counts, counts_ref),
    )
    start = 1 + SPLIT
    others = [Copies(*pair, sems, start + at, 1) for at, pair in enumerate(pairs)]
    unit = tower(rows_ref, w_in_ref, bias, w_out, bias_ref, out_ref, sems).astype(bf16)
    fetch = Copies(onehot, onehot_ref, sems, start + len(pairs), onehot.shape[0])
    for other in others:
        other.wait()
    mapped = mm(unit, map_ref[...]).astype(bf16)
    users, events = index_ref.shape
    slots, width = mapped.shape
    index = index_ref[...]
    upper = index >> 7
    lower = index & (LANES - 1)
    live = live_mask(length_ref, index.shape)
    logits = [init_ref[:, k, :] for k in range(INTERESTS)]
    capsules = None
    for iteration in range(ITERS):
        if iteration == 1:
            fetch.wait()
        if iteration:
            scatter_weights(event_weights(logits, live), upper, onehot_ref, slot_ref)
        slot_weights = first_ref[...] if iteration == 0 else slot_ref[...]
        coarse = slot_weights.astype(bf16)
        rest = (slot_weights - coarse.astype(f32)).astype(bf16)
        sums = mm(coarse, mapped) + mm(rest, mapped)
        norm_sq = jnp.sum(sums * sums, axis=1, keepdims=True)
        capsules = sums * (jnp.sqrt(norm_sq) / (1.0 + norm_sq))
        if iteration + 1 < ITERS:
            scores = mm_nt(capsules.astype(bf16), mapped)
            for k in range(INTERESTS):
                chunks = []
                for at in range(0, events, LANES):
                    low = lower[:, at : at + LANES]
                    high = upper[:, at : at + LANES]
                    found = jnp.zeros((users, LANES), f32)
                    for page in range(slots // LANES):
                        piece = scores[
                            k * users : (k + 1) * users, page * LANES : (page + 1) * LANES
                        ]
                        taken = jnp.take_along_axis(
                            piece, low, axis=1, mode="promise_in_bounds"
                        )
                        found = jnp.where(high == page, taken, found)
                    chunks.append(found)
                logits[k] = logits[k] + jnp.concatenate(chunks, axis=1)
    each = [capsules[k * users : (k + 1) * users] for k in range(INTERESTS)]
    for k in range(INTERESTS):
        interests_ref[:, k * width : (k + 1) * width] = each[k]
    label = to_column(label_ref[...].astype(f32))
    chosen = jnp.where(iota((users, slots), 1).astype(f32) == label, 1.0, 0.0).astype(bf16)
    label_rows = mm(chosen, unit)
    raised = [
        jnp.exp(attend_scale * jnp.sum(one * label_rows, axis=1, keepdims=True)) for one in each
    ]
    total = functools.reduce(jnp.add, raised)
    user_vec = functools.reduce(jnp.add, [(r / total) * one for r, one in zip(raised, each)])
    user_vec = user_vec.astype(bf16)
    vec_ref[:, :width] = user_vec
    vec_ref[:, width:] = lane_columns([to_column(one) for one in id_digits(ids_ref[...])], users).astype(bf16)
    match = jnp.sum(user_vec.astype(f32) * label_rows, axis=1, keepdims=True)
    positive_ref[...] = logit_scale * to_row(match) - jnp.log(counts_ref[...].astype(f32))


def route(rows, w_in, *others):
    _, _, bilinear, onehot, first, index, _, _, _, _, _ = others
    users = index.shape[0]
    width = bilinear.shape[1]
    return pl.pallas_call(
        route_kernel,
        in_specs=[INSIDE] * 2 + [OUTSIDE] * len(others),
        out_shape=[
            jax.ShapeDtypeStruct((users, INTERESTS * width), f32),
            pltpu.VMEM((users, width + LANES), bf16),
            pltpu.VMEM((1, users), f32),
        ],
        scratch_shapes=[pltpu.VMEM(one.shape, one.dtype) for one in others]
        + [
            pltpu.VMEM(first.shape, f32),
            pltpu.SemaphoreType.DMA((SPLIT + len(others) - 1 + onehot.shape[0],)),
        ],
        compiler_params=PARAMS,
        name="route",
    )(near(rows), near(w_in), *[far(one) for one in others])


def sums_kernel(parts, pieces, *refs):
    vec_refs = refs[:parts]
    neg_refs = refs[parts : parts + pieces]
    out_refs = refs[parts + pieces :]
    vec = jnp.concatenate([ref[...] for ref in vec_refs], axis=0)
    users = vec_refs[0].shape[0]
    width = vec.shape[1] - LANES
    digits = vec[:, width:].astype(f32)
    label_ids = digits[:, 0:1] + 256.0 * digits[:, 1:2] + 65536.0 * digits[:, 2:3]
    vec = vec[:, :width]
    total = None
    for ref in neg_refs:
        extra = ref[width:, :].astype(f32)
        ids = extra[0:1] + 256.0 * extra[1:2] + 65536.0 * extra[2:3]
        terms = jnp.exp(logit_scale * mm(vec, ref[:width, :])) * (1.0 / extra[3:4])
        terms = jnp.where(ids != label_ids, terms, 0.0)
        total = terms if total is None else total + terms
    total = to_row(jnp.sum(total, axis=1, keepdims=True))
    for part, ref in enumerate(out_refs):
        ref[...] = total[:, part * users : (part + 1) * users]


def negative_sums(vecs, negs):
    users = vecs[0].shape[0]
    return pl.pallas_call(
        functools.partial(sums_kernel, len(vecs), len(negs)),
        out_shape=[pltpu.VMEM((1, users), f32) for _ in vecs],
        compiler_params=PARAMS,
        name="negative_sums",
    )(*[near(one) for one in [*vecs, *negs]])


def swap_pool(array, size, bit):
    return lax.ppermute(array, "pool", [(at, at ^ bit) for at in range(size)])


def rotate_user(array, size, step):
    return lax.ppermute(array, "user", [(at, (at + step) % size) for at in range(size)])


def gather_negatives(own, size):
    pieces = [own]
    for mask in range(1, size // 2):
        pieces.append(swap_pool(own, size, mask))
    return pieces


def on_device(
    user_size,
    pool_size,
    item_feats,
    w_in,
    bias_in,
    w_out,
    bilinear,
    fetch_table,
    hist_index,
    hist_len,
    route_init,
    label_index,
    label_ids,
    label_counts,
    neg_feats,
    neg_ids,
    neg_counts,
):
    weights = (w_in, bias_in.reshape(1, -1), w_out)
    outgoing, packed = select_rows(
        fetch_table, item_feats, neg_feats, neg_ids.reshape(1, -1), neg_counts.reshape(1, -1)
    )
    apart = swap_pool(packed, pool_size, pool_size // 2)
    arrived = lax.all_to_all(
        outgoing.reshape(fetch_table.shape[0], fetch_table.shape[2], -1),
        ("user", "pool"),
        split_axis=0,
        concat_axis=0,
        tiled=True,
    )
    arrived = arrived.reshape(outgoing.shape)

    own_neg = neg_tower(packed, apart, weights)
    length = hist_len.reshape(1, -1)
    onehot, first = prepare(hist_index, length, route_init, outgoing.shape[0])
    negs = gather_negatives(own_neg, pool_size)

    interests, vec, positive = route(
        arrived,
        w_in,
        bias_in.reshape(1, -1),
        w_out,
        bilinear,
        onehot,
        first,
        hist_index,
        length,
        route_init,
        label_index.reshape(1, -1),
        label_ids.reshape(1, -1),
        label_counts.reshape(1, -1),
    )
    vecs = [vec] + [rotate_user(vec, user_size, step) for step in range(1, user_size)]
    sums = negative_sums(vecs, negs)
    partition = jnp.exp(positive) + sums[0]
    for step in range(1, user_size):
        partition += rotate_user(sums[step], user_size, user_size - step)
    user_loss = jnp.log(partition) - positive
    return (interests, user_loss.reshape(-1))


def solution(mesh):
    both = ("user", "pool")
    in_specs = (
        P(both, None),
        P(),
        P(),
        P(),
        P(),
        P(None, both, None),
        P(both, None),
        P(both),
        P(both, None, None),
        P(both),
        P(both),
        P(both),
        P(both, None),
        P(both),
        P(both),
    )
    out_specs = (P(both, None), P(both))

    def body(*args):
        return on_device(mesh.shape["user"], mesh.shape["pool"], *args)

    return jax.shard_map(body, mesh=mesh, in_specs=in_specs, out_specs=out_specs, check_vma=False)
```

```python
import functools

import jax
import jax.numpy as jnp
from jax import lax
from jax.experimental import pallas as pl
from jax.experimental.pallas import tpu as pltpu
from jax.sharding import PartitionSpec as P


INTERESTS = 4
ITERS = 3
LANES = 128
SUB = 8
EXTRA = 16
SPLIT = 4
GROUP_USERS = 8

norm_epsilon = 1e-06
attend_scale = 8.0
logit_scale = 20.0

f32 = jnp.float32
bf16 = jnp.bfloat16
i32 = jnp.int32


INSIDE = pl.BlockSpec(memory_space=pltpu.VMEM)
OUTSIDE = pl.BlockSpec(memory_space=pltpu.HBM)
PARAMS = pltpu.CompilerParams(vmem_limit_bytes=20 << 20)


def near(array):
    return pltpu.with_memory_space_constraint(array, pltpu.VMEM)


def far(array):
    return pltpu.with_memory_space_constraint(array, pltpu.HBM)


def mm(a, b):
    return jnp.dot(a, b, preferred_element_type=f32)


def mm_nt(a, b):
    return lax.dot_general(a, b, (((1,), (1,)), ((), ())), preferred_element_type=f32)


def iota(shape, axis):
    return lax.broadcasted_iota(i32, shape, axis)


def to_column(row):
    n = row.shape[1]
    eye = iota((n, n), 0) == iota((n, n), 1)
    return jnp.sum(jnp.where(eye, row, 0.0), axis=1, keepdims=True)


def to_row(column):
    n = column.shape[0]
    eye = iota((n, n), 0) == iota((n, n), 1)
    return jnp.sum(jnp.where(eye, column, 0.0), axis=0, keepdims=True)


def id_digits(ids_row):
    low = (ids_row & 255).astype(f32)
    mid = ((ids_row >> 8) & 255).astype(f32)
    high = (ids_row >> 16).astype(f32)
    return low, mid, high


def lane_columns(columns, rows):
    lane = iota((rows, LANES), 1)
    out = jnp.zeros((rows, LANES), f32)
    for at, column in enumerate(columns):
        out = jnp.where(lane == at, column, out)
    return out


def shift_of(size):
    assert size & (size - 1) == 0
    return size.bit_length() - 1


def renumber(slot, cap, user_size, pool_size):
    block = slot >> shift_of(cap)
    place = ((block & (pool_size - 1)) << shift_of(user_size)) + (block >> shift_of(pool_size))
    return (place << shift_of(cap)) + (slot & (cap - 1))


class Copies:
    def __init__(self, source, target, sems, first, count):
        size = source.shape[0] // count
        self.copies = [
            pltpu.make_async_copy(
                source.at[pl.ds(at * size, size)],
                target.at[pl.ds(at * size, size)],
                sems.at[first + at],
            )
            for at in range(count)
        ]
        for copy in self.copies:
            copy.start()

    def wait(self):
        for copy in self.copies:
            copy.wait()


def select_kernel(
    user_size,
    pool_size,
    fetch,
    rows,
    negs,
    ids,
    counts,
    out,
    packed,
    fetch_ref,
    rows_ref,
    out_ref,
    extra_ref,
    ids_ref,
    counts_ref,
    sems,
):
    table = Copies(fetch, fetch_ref, sems, 0, 1)
    small = [Copies(ids, ids_ref, sems, 1, 1), Copies(counts, counts_ref, sems, 2, 1)]
    copy = Copies(rows, rows_ref, sems, 5, SPLIT)
    kept = negs.shape[0]
    body = pltpu.make_async_copy(negs, packed.at[pl.ds(0, kept)], sems.at[3])
    body.start()
    _, cap, blocks = fetch_ref.shape
    count = blocks * cap
    row = iota((count, blocks), 0)
    start = renumber(iota((1, blocks), 1) * cap, cap, user_size, pool_size)
    pick = jnp.where((row >= start) & (row < start + cap), 1.0, 0.0).astype(bf16)
    place = iota((count, cap), 1) == (iota((count, cap), 0) & (cap - 1))
    table.wait()
    picked = fetch_ref[0]
    high = mm_nt(pick, (picked >> 7).astype(f32).astype(bf16))
    low = mm_nt(pick, (picked & 127).astype(f32).astype(bf16))
    column = jnp.sum(jnp.where(place, high * 128.0 + low, 0.0), axis=1, keepdims=True)
    item = iota((count, rows_ref.shape[0]), 1).astype(f32)
    chosen = jnp.where(item == column, 1.0, 0.0).astype(bf16)
    for one in small:
        one.wait()
    numbers = id_digits(ids_ref[...]) + (counts_ref[...].astype(f32),)
    at = iota((EXTRA, kept), 0)
    extra = jnp.zeros((EXTRA, kept), f32)
    for line, one in enumerate(numbers):
        extra = jnp.where(at == line, one, extra)
    extra_ref[...] = jnp.zeros(extra_ref.shape, bf16)
    extra_ref[:, :kept] = extra.astype(bf16)
    tail = pltpu.make_async_copy(extra_ref, packed.at[pl.ds(kept, EXTRA)], sems.at[4])
    tail.start()
    copy.wait()
    size = count // SPLIT
    for part in range(SPLIT):
        cut = slice(part * size, (part + 1) * size)
        out_ref[cut, :] = mm(chosen[cut], rows_ref[...]).astype(bf16)
        Copies(out_ref.at[pl.ds(part * size, size)], out.at[pl.ds(part * size, size)], sems, 5 + SPLIT + part, 1)
    body.wait()
    tail.wait()
    for part in range(SPLIT):
        there = pl.ds(part * size, size)
        pltpu.make_async_copy(out_ref.at[there], out.at[there], sems.at[5 + SPLIT + part]).wait()


def select_rows(user_size, pool_size, fetch, rows, negs, ids, counts):
    blocks, _, cap = fetch.shape
    packed = (negs.shape[0] + EXTRA, negs.shape[1])
    chosen = (blocks * cap, rows.shape[1])
    return pl.pallas_call(
        functools.partial(select_kernel, user_size, pool_size),
        in_specs=[OUTSIDE] * 5,
        out_specs=[OUTSIDE, OUTSIDE],
        out_shape=[jax.ShapeDtypeStruct(chosen, bf16), jax.ShapeDtypeStruct(packed, bf16)],
        scratch_shapes=[
            pltpu.VMEM((1, cap, blocks), i32),
            pltpu.VMEM(rows.shape, bf16),
            pltpu.VMEM(chosen, bf16),
            pltpu.VMEM((EXTRA, negs.shape[1]), bf16),
            pltpu.VMEM(ids.shape, i32),
            pltpu.VMEM(counts.shape, i32),
            pltpu.SemaphoreType.DMA((5 + 2 * SPLIT,)),
        ],
        compiler_params=PARAMS,
        name="select_rows",
    )(*[far(one) for one in (fetch.transpose(1, 2, 0), rows, negs, ids, counts)])


def tower(rows_ref, w_in_ref, bias, w_out, bias_ref, out_ref, sems, parts=None):
    small = Copies(bias, bias_ref, sems, 0, 1)
    large = Copies(w_out, out_ref, sems, 1, SPLIT)
    if parts is None:
        hidden = mm(rows_ref[...], w_in_ref[...])
        small.wait()
        hidden = jnp.maximum(hidden + bias_ref[...], 0.0).astype(bf16)
    else:
        small.wait()
        pieces = []
        for at, part in enumerate(parts):
            part.wait()
            size = w_in_ref.shape[1] // len(parts)
            cut = slice(at * size, (at + 1) * size)
            piece = mm(rows_ref[...], w_in_ref[:, cut]) + bias_ref[:, cut]
            pieces.append(jnp.maximum(piece, 0.0).astype(bf16))
        hidden = jnp.concatenate(pieces, axis=1)
    large.wait()
    embedding = mm(hidden, out_ref[...])
    total = jnp.sum(embedding * embedding, axis=1, keepdims=True)
    return embedding * lax.rsqrt(total + norm_epsilon)


def neg_kernel(
    own_ref, apart_ref, w_in, bias, w_out, out_ref, rows_ref, w_in_ref, bias_ref, w_out_ref, sems
):
    size = w_in.shape[1] // SPLIT
    parts = [
        pltpu.make_async_copy(
            w_in.at[:, pl.ds(at * size, size)],
            w_in_ref.at[:, pl.ds(at * size, size)],
            sems.at[1 + SPLIT + at],
        )
        for at in range(SPLIT)
    ]
    for part in parts:
        part.start()
    count = rows_ref.shape[0] // 2
    rows_ref[:count, :] = own_ref[:count, :]
    rows_ref[count:, :] = apart_ref[:count, :]
    unit = tower(rows_ref, w_in_ref, bias, w_out, bias_ref, w_out_ref, sems, parts)
    width = unit.shape[1]
    out_ref[:width, :] = unit.T.astype(bf16)
    out_ref[width:, :count] = own_ref[count:, :count]
    out_ref[width:, count:] = apart_ref[count:, :count]


def neg_tower(own, apart, weights):
    count = own.shape[0] - EXTRA
    width = own.shape[1]
    return pl.pallas_call(
        neg_kernel,
        in_specs=[INSIDE, INSIDE, OUTSIDE, OUTSIDE, OUTSIDE],
        out_shape=pltpu.VMEM((width + EXTRA, 2 * count), bf16),
        scratch_shapes=[pltpu.VMEM((2 * count, width), bf16)]
        + [pltpu.VMEM(one.shape, one.dtype) for one in weights]
        + [pltpu.SemaphoreType.DMA((1 + 2 * SPLIT,))],
        compiler_params=PARAMS,
        name="neg_tower",
    )(near(own), near(apart), *[far(one) for one in weights])


def event_weights(logits, live):
    raised = [jnp.exp(one) for one in logits]
    total = functools.reduce(jnp.add, raised)
    return [(one / total * live).astype(bf16).astype(f32) for one in raised]


def scatter_weights(weights, upper, onehot_ref, slot_ref):
    users = weights[0].shape[0]
    pages = slot_ref.shape[1] // LANES
    count = pages * INTERESTS * SUB
    for group in range(users // GROUP_USERS):
        at = slice(group * GROUP_USERS, (group + 1) * GROUP_USERS)
        base = jnp.concatenate(
            [
                jnp.where(upper[at] == page, weights[k][at], 0.0)
                for page in range(pages)
                for k in range(INTERESTS)
            ],
            axis=0,
        )
        user = iota((count, 1), 0) & (GROUP_USERS - 1)
        left = jnp.concatenate(
            [
                jnp.where((user >> 1) == pair, base, 0.0).astype(bf16)
                for pair in range(GROUP_USERS // 2)
            ],
            axis=1,
        )
        both = mm(left, onehot_ref[group])
        own = jnp.where((user & 1) == 0, both[:, :LANES], both[:, LANES:])
        for page in range(pages):
            for k in range(INTERESTS):
                source = (page * INTERESTS + k) * SUB
                target = k * users + group * GROUP_USERS
                slot_ref[target : target + SUB, page * LANES : (page + 1) * LANES] = own[
                    source : source + SUB
                ]


def live_mask(length_ref, shape):
    length = to_column(length_ref[...].astype(f32))
    return jnp.where(iota(shape, 1).astype(f32) < length, 1.0, 0.0)


def prepare_kernel(
    renumbered,
    index,
    length,
    init,
    onehot,
    slots,
    moved,
    index_ref,
    length_ref,
    init_ref,
    onehot_ref,
    slot_ref,
    moved_ref,
    sems,
):
    pairs = ((index, index_ref), (length, length_ref), (init, init_ref))
    copies = [Copies(*pair, sems, at, 1) for at, pair in enumerate(pairs)]
    users, events = index_ref.shape
    groups = users // GROUP_USERS
    copies[0].wait()
    index = renumbered(index_ref[...])
    moved_ref[...] = index
    back = [Copies(moved_ref, moved, sems, 3, 1)]
    upper = index >> 7
    lower = (index & (LANES - 1)).astype(f32).T
    lane_id = iota((events, LANES), 1).astype(f32)
    for group in range(groups):
        for within in range(GROUP_USERS):
            user = group * GROUP_USERS + within
            pair, side = divmod(within, 2)
            hit = jnp.where(lane_id == lower[:, user : user + 1], 1.0, 0.0).astype(bf16)
            onehot_ref[
                group, pair * events : (pair + 1) * events, side * LANES : (side + 1) * LANES
            ] = hit
        there = pl.ds(group, 1)
        back.append(Copies(onehot_ref.at[there], onehot.at[there], sems, 5 + group, 1))
    for one in copies[1:]:
        one.wait()
    live = live_mask(length_ref, index.shape)
    weights = event_weights([init_ref[:, k, :] for k in range(INTERESTS)], live)
    scatter_weights(weights, upper, onehot_ref, slot_ref)
    back.append(Copies(slot_ref, slots, sems, 4, 1))
    for one in back:
        one.wait()


def prepare(renumbered, index, length, init, slots):
    users, events = index.shape
    groups = users // GROUP_USERS
    onehot = (groups, GROUP_USERS // 2 * events, 2 * LANES)
    first = (INTERESTS * users, slots)
    return pl.pallas_call(
        functools.partial(prepare_kernel, renumbered),
        in_specs=[OUTSIDE] * 3,
        out_specs=[OUTSIDE] * 3,
        out_shape=[
            pltpu.HBM(onehot, bf16),
            pltpu.HBM(first, f32),
            pltpu.HBM(index.shape, i32),
        ],
        scratch_shapes=[
            pltpu.VMEM(index.shape, i32),
            pltpu.VMEM(length.shape, i32),
            pltpu.VMEM(init.shape, f32),
            pltpu.VMEM(onehot, bf16),
            pltpu.VMEM(first, f32),
            pltpu.VMEM(index.shape, i32),
            pltpu.SemaphoreType.DMA((5 + groups,)),
        ],
        compiler_params=PARAMS,
        name="prepare",
    )(far(index), far(length), far(init))


def route_kernel(
    renumbered,
    rows_ref,
    w_in_ref,
    bias,
    w_out,
    bilinear,
    onehot,
    first,
    index,
    length,
    init,
    label,
    ids,
    counts,
    interests_ref,
    vec_ref,
    positive_ref,
    bias_ref,
    out_ref,
    map_ref,
    onehot_ref,
    first_ref,
    index_ref,
    length_ref,
    init_ref,
    label_ref,
    ids_ref,
    counts_ref,
    slot_ref,
    sems,
):
    pairs = (
        (bilinear, map_ref),
        (first, first_ref),
        (index, index_ref),
        (length, length_ref),
        (init, init_ref),
        (label, label_ref),
        (ids, ids_ref),
        (counts, counts_ref),
    )
    start = 1 + SPLIT
    others = [Copies(*pair, sems, start + at, 1) for at, pair in enumerate(pairs)]
    unit = tower(rows_ref, w_in_ref, bias, w_out, bias_ref, out_ref, sems).astype(bf16)
    fetch = Copies(onehot, onehot_ref, sems, start + len(pairs), onehot.shape[0])
    for other in others:
        other.wait()
    mapped = mm(unit, map_ref[...]).astype(bf16)
    users, events = index_ref.shape
    slots, width = mapped.shape
    index = index_ref[...]
    upper = index >> 7
    lower = index & (LANES - 1)
    live = live_mask(length_ref, index.shape)
    logits = [init_ref[:, k, :] for k in range(INTERESTS)]
    capsules = None
    for iteration in range(ITERS):
        if iteration == 1:
            fetch.wait()
        if iteration:
            scatter_weights(event_weights(logits, live), upper, onehot_ref, slot_ref)
        slot_weights = first_ref[...] if iteration == 0 else slot_ref[...]
        coarse = slot_weights.astype(bf16)
        rest = (slot_weights - coarse.astype(f32)).astype(bf16)
        sums = mm(coarse, mapped) + mm(rest, mapped)
        norm_sq = jnp.sum(sums * sums, axis=1, keepdims=True)
        capsules = sums * (jnp.sqrt(norm_sq) / (1.0 + norm_sq))
        if iteration + 1 < ITERS:
            scores = mm_nt(capsules.astype(bf16), mapped)
            for k in range(INTERESTS):
                chunks = []
                for at in range(0, events, LANES):
                    low = lower[:, at : at + LANES]
                    high = upper[:, at : at + LANES]
                    found = jnp.zeros((users, LANES), f32)
                    for page in range(slots // LANES):
                        piece = scores[
                            k * users : (k + 1) * users, page * LANES : (page + 1) * LANES
                        ]
                        taken = jnp.take_along_axis(
                            piece, low, axis=1, mode="promise_in_bounds"
                        )
                        found = jnp.where(high == page, taken, found)
                    chunks.append(found)
                logits[k] = logits[k] + jnp.concatenate(chunks, axis=1)
    each = [capsules[k * users : (k + 1) * users] for k in range(INTERESTS)]
    for k in range(INTERESTS):
        interests_ref[:, k * width : (k + 1) * width] = each[k]
    label = to_column(renumbered(label_ref[...]).astype(f32))
    chosen = jnp.where(iota((users, slots), 1).astype(f32) == label, 1.0, 0.0).astype(bf16)
    label_rows = mm(chosen, unit)
    raised = [
        jnp.exp(attend_scale * jnp.sum(one * label_rows, axis=1, keepdims=True)) for one in each
    ]
    total = functools.reduce(jnp.add, raised)
    user_vec = functools.reduce(jnp.add, [(r / total) * one for r, one in zip(raised, each)])
    user_vec = user_vec.astype(bf16)
    vec_ref[:, :width] = user_vec
    vec_ref[:, width:] = lane_columns([to_column(one) for one in id_digits(ids_ref[...])], users).astype(bf16)
    match = jnp.sum(user_vec.astype(f32) * label_rows, axis=1, keepdims=True)
    positive_ref[...] = logit_scale * to_row(match) - jnp.log(counts_ref[...].astype(f32))


def route(renumbered, rows, w_in, *others):
    _, _, bilinear, onehot, first, index, _, _, _, _, _ = others
    users = index.shape[0]
    width = bilinear.shape[1]
    return pl.pallas_call(
        functools.partial(route_kernel, renumbered),
        in_specs=[INSIDE] * 2 + [OUTSIDE] * len(others),
        out_shape=[
            jax.ShapeDtypeStruct((users, INTERESTS * width), f32),
            pltpu.VMEM((users, width + LANES), bf16),
            pltpu.VMEM((1, users), f32),
        ],
        scratch_shapes=[pltpu.VMEM(one.shape, one.dtype) for one in others]
        + [
            pltpu.VMEM(first.shape, f32),
            pltpu.SemaphoreType.DMA((SPLIT + len(others) - 1 + onehot.shape[0],)),
        ],
        compiler_params=PARAMS,
        name="route",
    )(near(rows), near(w_in), *[far(one) for one in others])


def sums_kernel(parts, pieces, *refs):
    vec_refs = refs[:parts]
    neg_refs = refs[parts : parts + pieces]
    out_refs = refs[parts + pieces :]
    vec = jnp.concatenate([ref[...] for ref in vec_refs], axis=0)
    users = vec_refs[0].shape[0]
    width = vec.shape[1] - LANES
    digits = vec[:, width:].astype(f32)
    label_ids = digits[:, 0:1] + 256.0 * digits[:, 1:2] + 65536.0 * digits[:, 2:3]
    vec = vec[:, :width]
    total = None
    for ref in neg_refs:
        extra = ref[width:, :].astype(f32)
        ids = extra[0:1] + 256.0 * extra[1:2] + 65536.0 * extra[2:3]
        terms = jnp.exp(logit_scale * mm(vec, ref[:width, :])) * (1.0 / extra[3:4])
        terms = jnp.where(ids != label_ids, terms, 0.0)
        total = terms if total is None else total + terms
    total = to_row(jnp.sum(total, axis=1, keepdims=True))
    for part, ref in enumerate(out_refs):
        ref[...] = total[:, part * users : (part + 1) * users]


def negative_sums(vecs, negs):
    users = vecs[0].shape[0]
    return pl.pallas_call(
        functools.partial(sums_kernel, len(vecs), len(negs)),
        out_shape=[pltpu.VMEM((1, users), f32) for _ in vecs],
        compiler_params=PARAMS,
        name="negative_sums",
    )(*[near(one) for one in [*vecs, *negs]])


def swap_pool(array, size, bit):
    return lax.ppermute(array, "pool", [(at, at ^ bit) for at in range(size)])


def rotate_user(array, size, step):
    return lax.ppermute(array, "user", [(at, (at + step) % size) for at in range(size)])


def gather_negatives(own, size):
    pieces = [own]
    for mask in range(1, size // 2):
        pieces.append(swap_pool(own, size, mask))
    return pieces


def on_device(
    user_size,
    pool_size,
    item_feats,
    w_in,
    bias_in,
    w_out,
    bilinear,
    fetch_table,
    hist_index,
    hist_len,
    route_init,
    label_index,
    label_ids,
    label_counts,
    neg_feats,
    neg_ids,
    neg_counts,
):
    weights = (w_in, bias_in.reshape(1, -1), w_out)
    outgoing, packed = select_rows(
        user_size, pool_size, fetch_table, item_feats, neg_feats, neg_ids.reshape(1, -1), neg_counts.reshape(1, -1)
    )
    apart = swap_pool(packed, pool_size, pool_size // 2)
    arrived = lax.all_to_all(
        outgoing.reshape(fetch_table.shape[0], fetch_table.shape[2], -1),
        ("pool", "user"),
        split_axis=0,
        concat_axis=0,
        tiled=True,
    )
    arrived = arrived.reshape(outgoing.shape)

    own_neg = neg_tower(packed, apart, weights)
    length = hist_len.reshape(1, -1)
    renumbered = functools.partial(
        renumber, cap=fetch_table.shape[2], user_size=user_size, pool_size=pool_size
    )
    onehot, first, moved = prepare(renumbered, hist_index, length, route_init, outgoing.shape[0])
    negs = gather_negatives(own_neg, pool_size)

    interests, vec, positive = route(
        renumbered,
        arrived,
        w_in,
        bias_in.reshape(1, -1),
        w_out,
        bilinear,
        onehot,
        first,
        moved,
        length,
        route_init,
        label_index.reshape(1, -1),
        label_ids.reshape(1, -1),
        label_counts.reshape(1, -1),
    )
    vecs = [vec] + [rotate_user(vec, user_size, step) for step in range(1, user_size)]
    sums = negative_sums(vecs, negs)
    partition = jnp.exp(positive) + sums[0]
    for step in range(1, user_size):
        partition += rotate_user(sums[step], user_size, user_size - step)
    user_loss = jnp.log(partition) - positive
    return (interests, user_loss.reshape(-1))


def solution(mesh):
    both = ("user", "pool")
    in_specs = (
        P(both, None),
        P(),
        P(),
        P(),
        P(),
        P(None, both, None),
        P(both, None),
        P(both),
        P(both, None, None),
        P(both),
        P(both),
        P(both),
        P(both, None),
        P(both),
        P(both),
    )
    out_specs = (P(both, None), P(both))

    def body(*args):
        return on_device(mesh.shape["user"], mesh.shape["pool"], *args)

    return jax.shard_map(body, mesh=mesh, in_specs=in_specs, out_specs=out_specs, check_vma=False)
```

```python
import functools

import jax
import jax.numpy as jnp
from jax import lax
from jax.experimental import pallas as pl
from jax.experimental.pallas import tpu as pltpu
from jax.sharding import PartitionSpec as P


INTERESTS = 4
ITERS = 3
LANES = 128
SUB = 8
EXTRA = 16
SPLIT = 4
GROUP_USERS = 8

norm_epsilon = 1e-06
attend_scale = 8.0
logit_scale = 20.0

f32 = jnp.float32
bf16 = jnp.bfloat16
i32 = jnp.int32


INSIDE = pl.BlockSpec(memory_space=pltpu.VMEM)
OUTSIDE = pl.BlockSpec(memory_space=pltpu.HBM)
PARAMS = pltpu.CompilerParams(vmem_limit_bytes=20 << 20)


def near(array):
    return pltpu.with_memory_space_constraint(array, pltpu.VMEM)


def far(array):
    return pltpu.with_memory_space_constraint(array, pltpu.HBM)


def mm(a, b):
    return jnp.dot(a, b, preferred_element_type=f32)


def mm_nt(a, b):
    return lax.dot_general(a, b, (((1,), (1,)), ((), ())), preferred_element_type=f32)


def iota(shape, axis):
    return lax.broadcasted_iota(i32, shape, axis)


def to_column(row):
    n = row.shape[1]
    eye = iota((n, n), 0) == iota((n, n), 1)
    return jnp.sum(jnp.where(eye, row, 0.0), axis=1, keepdims=True)


def to_row(column):
    n = column.shape[0]
    eye = iota((n, n), 0) == iota((n, n), 1)
    return jnp.sum(jnp.where(eye, column, 0.0), axis=0, keepdims=True)


def id_digits(ids_row):
    low = (ids_row & 255).astype(f32)
    mid = ((ids_row >> 8) & 255).astype(f32)
    high = (ids_row >> 16).astype(f32)
    return low, mid, high


def lane_columns(columns, rows):
    lane = iota((rows, LANES), 1)
    out = jnp.zeros((rows, LANES), f32)
    for at, column in enumerate(columns):
        out = jnp.where(lane == at, column, out)
    return out


def shift_of(size):
    assert size & (size - 1) == 0
    return size.bit_length() - 1


def renumber(slot, cap, user_size, pool_size):
    block = slot >> shift_of(cap)
    place = ((block & (pool_size - 1)) << shift_of(user_size)) + (block >> shift_of(pool_size))
    return (place << shift_of(cap)) + (slot & (cap - 1))


class Copies:
    def __init__(self, source, target, sems, first, count):
        size = source.shape[0] // count
        self.copies = [
            pltpu.make_async_copy(
                source.at[pl.ds(at * size, size)],
                target.at[pl.ds(at * size, size)],
                sems.at[first + at],
            )
            for at in range(count)
        ]
        for copy in self.copies:
            copy.start()

    def wait(self):
        for copy in self.copies:
            copy.wait()


def select_kernel(
    user_size,
    pool_size,
    fetch,
    rows,
    negs,
    ids,
    counts,
    out,
    packed,
    fetch_ref,
    rows_ref,
    out_ref,
    extra_ref,
    ids_ref,
    counts_ref,
    sems,
):
    table = Copies(fetch, fetch_ref, sems, 0, 1)
    small = [Copies(ids, ids_ref, sems, 1, 1), Copies(counts, counts_ref, sems, 2, 1)]
    copy = Copies(rows, rows_ref, sems, 5, SPLIT)
    kept = negs.shape[0]
    body = pltpu.make_async_copy(negs, packed.at[pl.ds(0, kept)], sems.at[3])
    body.start()
    _, cap, blocks = fetch_ref.shape
    count = blocks * cap
    row = iota((count, blocks), 0)
    start = renumber(iota((1, blocks), 1) * cap, cap, user_size, pool_size)
    pick = jnp.where((row >= start) & (row < start + cap), 1.0, 0.0).astype(bf16)
    place = iota((count, cap), 1) == (iota((count, cap), 0) & (cap - 1))
    table.wait()
    picked = fetch_ref[0]
    high = mm_nt(pick, (picked >> 7).astype(f32).astype(bf16))
    low = mm_nt(pick, (picked & 127).astype(f32).astype(bf16))
    column = jnp.sum(jnp.where(place, high * 128.0 + low, 0.0), axis=1, keepdims=True)
    item = iota((count, rows_ref.shape[0]), 1).astype(f32)
    chosen = jnp.where(item == column, 1.0, 0.0).astype(bf16)
    for one in small:
        one.wait()
    numbers = id_digits(ids_ref[...]) + (counts_ref[...].astype(f32),)
    at = iota((EXTRA, kept), 0)
    extra = jnp.zeros((EXTRA, kept), f32)
    for line, one in enumerate(numbers):
        extra = jnp.where(at == line, one, extra)
    extra_ref[...] = jnp.zeros(extra_ref.shape, bf16)
    extra_ref[:, :kept] = extra.astype(bf16)
    tail = pltpu.make_async_copy(extra_ref, packed.at[pl.ds(kept, EXTRA)], sems.at[4])
    tail.start()
    copy.wait()
    size = count // SPLIT
    for part in range(SPLIT):
        cut = slice(part * size, (part + 1) * size)
        out_ref[cut, :] = mm(chosen[cut], rows_ref[...]).astype(bf16)
        Copies(out_ref.at[pl.ds(part * size, size)], out.at[pl.ds(part * size, size)], sems, 5 + SPLIT + part, 1)
    body.wait()
    tail.wait()
    for part in range(SPLIT):
        there = pl.ds(part * size, size)
        pltpu.make_async_copy(out_ref.at[there], out.at[there], sems.at[5 + SPLIT + part]).wait()


def select_rows(user_size, pool_size, fetch, rows, negs, ids, counts):
    blocks, _, cap = fetch.shape
    packed = (negs.shape[0] + EXTRA, negs.shape[1])
    chosen = (blocks * cap, rows.shape[1])
    return pl.pallas_call(
        functools.partial(select_kernel, user_size, pool_size),
        in_specs=[OUTSIDE] * 5,
        out_specs=[OUTSIDE, OUTSIDE],
        out_shape=[jax.ShapeDtypeStruct(chosen, bf16), jax.ShapeDtypeStruct(packed, bf16)],
        scratch_shapes=[
            pltpu.VMEM((1, cap, blocks), i32),
            pltpu.VMEM(rows.shape, bf16),
            pltpu.VMEM(chosen, bf16),
            pltpu.VMEM((EXTRA, negs.shape[1]), bf16),
            pltpu.VMEM(ids.shape, i32),
            pltpu.VMEM(counts.shape, i32),
            pltpu.SemaphoreType.DMA((5 + 2 * SPLIT,)),
        ],
        compiler_params=PARAMS,
        name="select_rows",
    )(*[far(one) for one in (fetch.transpose(1, 2, 0), rows, negs, ids, counts)])


def tower(rows_ref, w_in_ref, bias, w_out, bias_ref, out_ref, sems, parts=None):
    small = Copies(bias, bias_ref, sems, 0, 1)
    large = Copies(w_out, out_ref, sems, 1, SPLIT)
    if parts is None:
        hidden = mm(rows_ref[...], w_in_ref[...])
        small.wait()
        hidden = jnp.maximum(hidden + bias_ref[...], 0.0).astype(bf16)
    else:
        small.wait()
        pieces = []
        for at, part in enumerate(parts):
            part.wait()
            size = w_in_ref.shape[1] // len(parts)
            cut = slice(at * size, (at + 1) * size)
            piece = mm(rows_ref[...], w_in_ref[:, cut]) + bias_ref[:, cut]
            pieces.append(jnp.maximum(piece, 0.0).astype(bf16))
        hidden = jnp.concatenate(pieces, axis=1)
    large.wait()
    embedding = mm(hidden, out_ref[...])
    total = jnp.sum(embedding * embedding, axis=1, keepdims=True)
    return embedding * lax.rsqrt(total + norm_epsilon)


def neg_kernel(
    own_ref, apart_ref, w_in, bias, w_out, out_ref, rows_ref, w_in_ref, bias_ref, w_out_ref, sems
):
    size = w_in.shape[1] // SPLIT
    parts = [
        pltpu.make_async_copy(
            w_in.at[:, pl.ds(at * size, size)],
            w_in_ref.at[:, pl.ds(at * size, size)],
            sems.at[1 + SPLIT + at],
        )
        for at in range(SPLIT)
    ]
    for part in parts:
        part.start()
    count = rows_ref.shape[0] // 2
    rows_ref[:count, :] = own_ref[:count, :]
    rows_ref[count:, :] = apart_ref[:count, :]
    unit = tower(rows_ref, w_in_ref, bias, w_out, bias_ref, w_out_ref, sems, parts)
    width = unit.shape[1]
    out_ref[:width, :] = unit.T.astype(bf16)
    out_ref[width:, :count] = own_ref[count:, :count]
    out_ref[width:, count:] = apart_ref[count:, :count]


def neg_tower(own, apart, weights):
    count = own.shape[0] - EXTRA
    width = own.shape[1]
    return pl.pallas_call(
        neg_kernel,
        in_specs=[INSIDE, INSIDE, OUTSIDE, OUTSIDE, OUTSIDE],
        out_shape=pltpu.VMEM((width + EXTRA, 2 * count), bf16),
        scratch_shapes=[pltpu.VMEM((2 * count, width), bf16)]
        + [pltpu.VMEM(one.shape, one.dtype) for one in weights]
        + [pltpu.SemaphoreType.DMA((1 + 2 * SPLIT,))],
        compiler_params=PARAMS,
        name="neg_tower",
    )(near(own), near(apart), *[far(one) for one in weights])


def event_weights(logits, live):
    raised = [jnp.exp(one) for one in logits]
    total = functools.reduce(jnp.add, raised)
    return [(one / total * live).astype(bf16).astype(f32) for one in raised]


def scatter_weights(weights, upper, onehot_ref, slot_ref):
    users = weights[0].shape[0]
    pages = slot_ref.shape[1] // LANES
    count = pages * INTERESTS * SUB
    for group in range(users // GROUP_USERS):
        at = slice(group * GROUP_USERS, (group + 1) * GROUP_USERS)
        base = jnp.concatenate(
            [
                jnp.where(upper[at] == page, weights[k][at], 0.0)
                for page in range(pages)
                for k in range(INTERESTS)
            ],
            axis=0,
        )
        user = iota((count, 1), 0) & (GROUP_USERS - 1)
        left = jnp.concatenate(
            [
                jnp.where((user >> 1) == pair, base, 0.0).astype(bf16)
                for pair in range(GROUP_USERS // 2)
            ],
            axis=1,
        )
        both = mm(left, onehot_ref[group])
        own = jnp.where((user & 1) == 0, both[:, :LANES], both[:, LANES:])
        for page in range(pages):
            for k in range(INTERESTS):
                source = (page * INTERESTS + k) * SUB
                target = k * users + group * GROUP_USERS
                slot_ref[target : target + SUB, page * LANES : (page + 1) * LANES] = own[
                    source : source + SUB
                ]


def live_mask(length_ref, shape):
    length = to_column(length_ref[...].astype(f32))
    return jnp.where(iota(shape, 1).astype(f32) < length, 1.0, 0.0)


def prepare_kernel(
    renumbered,
    index,
    length,
    init,
    onehot,
    slots,
    moved,
    index_ref,
    length_ref,
    init_ref,
    onehot_ref,
    slot_ref,
    moved_ref,
    sems,
):
    pairs = ((index, index_ref), (length, length_ref), (init, init_ref))
    copies = [Copies(*pair, sems, at, 1) for at, pair in enumerate(pairs)]
    users, events = index_ref.shape
    groups = users // GROUP_USERS
    copies[0].wait()
    index = renumbered(index_ref[...])
    moved_ref[...] = index
    back = [Copies(moved_ref, moved, sems, 3, 1)]
    upper = index >> 7
    lower = (index & (LANES - 1)).astype(f32).T
    lane_id = iota((events, LANES), 1).astype(f32)
    for group in range(groups):
        for within in range(GROUP_USERS):
            user = group * GROUP_USERS + within
            pair, side = divmod(within, 2)
            hit = jnp.where(lane_id == lower[:, user : user + 1], 1.0, 0.0).astype(bf16)
            onehot_ref[
                group, pair * events : (pair + 1) * events, side * LANES : (side + 1) * LANES
            ] = hit
        there = pl.ds(group, 1)
        back.append(Copies(onehot_ref.at[there], onehot.at[there], sems, 5 + group, 1))
    for one in copies[1:]:
        one.wait()
    live = live_mask(length_ref, index.shape)
    weights = event_weights([init_ref[:, k, :] for k in range(INTERESTS)], live)
    scatter_weights(weights, upper, onehot_ref, slot_ref)
    back.append(Copies(slot_ref, slots, sems, 4, 1))
    for one in back:
        one.wait()


def prepare(renumbered, index, length, init, slots):
    users, events = index.shape
    groups = users // GROUP_USERS
    onehot = (groups, GROUP_USERS // 2 * events, 2 * LANES)
    first = (INTERESTS * users, slots)
    return pl.pallas_call(
        functools.partial(prepare_kernel, renumbered),
        in_specs=[OUTSIDE] * 3,
        out_specs=[OUTSIDE] * 3,
        out_shape=[
            pltpu.HBM(onehot, bf16),
            pltpu.HBM(first, f32),
            pltpu.HBM(index.shape, i32),
        ],
        scratch_shapes=[
            pltpu.VMEM(index.shape, i32),
            pltpu.VMEM(length.shape, i32),
            pltpu.VMEM(init.shape, f32),
            pltpu.VMEM(onehot, bf16),
            pltpu.VMEM(first, f32),
            pltpu.VMEM(index.shape, i32),
            pltpu.SemaphoreType.DMA((5 + groups,)),
        ],
        compiler_params=PARAMS,
        name="prepare",
    )(far(index), far(length), far(init))


def route_kernel(
    renumbered,
    rows_ref,
    w_in_ref,
    bias,
    w_out,
    bilinear,
    onehot,
    first,
    index,
    length,
    init,
    label,
    ids,
    counts,
    interests_ref,
    vec_ref,
    positive_ref,
    bias_ref,
    out_ref,
    map_ref,
    onehot_ref,
    first_ref,
    index_ref,
    length_ref,
    init_ref,
    label_ref,
    ids_ref,
    counts_ref,
    slot_ref,
    sems,
):
    pairs = (
        (bilinear, map_ref),
        (first, first_ref),
        (index, index_ref),
        (length, length_ref),
        (init, init_ref),
        (label, label_ref),
        (ids, ids_ref),
        (counts, counts_ref),
    )
    start = 1 + SPLIT
    others = [Copies(*pair, sems, start + at, 1) for at, pair in enumerate(pairs)]
    unit = tower(rows_ref, w_in_ref, bias, w_out, bias_ref, out_ref, sems).astype(bf16)
    fetch = Copies(onehot, onehot_ref, sems, start + len(pairs), onehot.shape[0])
    for other in others:
        other.wait()
    mapped = mm(unit, map_ref[...]).astype(bf16)
    users, events = index_ref.shape
    slots, width = mapped.shape
    index = index_ref[...]
    upper = index >> 7
    lower = index & (LANES - 1)
    live = live_mask(length_ref, index.shape)
    logits = [init_ref[:, k, :] for k in range(INTERESTS)]
    capsules = None
    for iteration in range(ITERS):
        if iteration == 1:
            fetch.wait()
        if iteration:
            scatter_weights(event_weights(logits, live), upper, onehot_ref, slot_ref)
        slot_weights = first_ref[...] if iteration == 0 else slot_ref[...]
        coarse = slot_weights.astype(bf16)
        rest = (slot_weights - coarse.astype(f32)).astype(bf16)
        sums = mm(coarse, mapped) + mm(rest, mapped)
        norm_sq = jnp.sum(sums * sums, axis=1, keepdims=True)
        capsules = sums * (jnp.sqrt(norm_sq) / (1.0 + norm_sq))
        if iteration + 1 < ITERS:
            scores = mm_nt(capsules.astype(bf16), mapped)
            for k in range(INTERESTS):
                chunks = []
                for at in range(0, events, LANES):
                    low = lower[:, at : at + LANES]
                    high = upper[:, at : at + LANES]
                    found = jnp.zeros((users, LANES), f32)
                    for page in range(slots // LANES):
                        piece = scores[
                            k * users : (k + 1) * users, page * LANES : (page + 1) * LANES
                        ]
                        taken = jnp.take_along_axis(
                            piece, low, axis=1, mode="promise_in_bounds"
                        )
                        found = jnp.where(high == page, taken, found)
                    chunks.append(found)
                logits[k] = logits[k] + jnp.concatenate(chunks, axis=1)
    each = [capsules[k * users : (k + 1) * users] for k in range(INTERESTS)]
    for k in range(INTERESTS):
        interests_ref[:, k * width : (k + 1) * width] = each[k]
    label = to_column(renumbered(label_ref[...]).astype(f32))
    chosen = jnp.where(iota((users, slots), 1).astype(f32) == label, 1.0, 0.0).astype(bf16)
    label_rows = mm(chosen, unit)
    raised = [
        jnp.exp(attend_scale * jnp.sum(one * label_rows, axis=1, keepdims=True)) for one in each
    ]
    total = functools.reduce(jnp.add, raised)
    user_vec = functools.reduce(jnp.add, [(r / total) * one for r, one in zip(raised, each)])
    user_vec = user_vec.astype(bf16)
    vec_ref[:, :width] = user_vec
    vec_ref[:, width:] = lane_columns([to_column(one) for one in id_digits(ids_ref[...])], users).astype(bf16)
    match = jnp.sum(user_vec.astype(f32) * label_rows, axis=1, keepdims=True)
    positive_ref[...] = logit_scale * to_row(match) - jnp.log(counts_ref[...].astype(f32))


def route(renumbered, rows, w_in, *others):
    _, _, bilinear, onehot, first, index, _, _, _, _, _ = others
    users = index.shape[0]
    width = bilinear.shape[1]
    return pl.pallas_call(
        functools.partial(route_kernel, renumbered),
        in_specs=[INSIDE] * 2 + [OUTSIDE] * len(others),
        out_shape=[
            jax.ShapeDtypeStruct((users, INTERESTS * width), f32),
            pltpu.VMEM((users, width + LANES), bf16),
            pltpu.VMEM((1, users), f32),
        ],
        scratch_shapes=[pltpu.VMEM(one.shape, one.dtype) for one in others]
        + [
            pltpu.VMEM(first.shape, f32),
            pltpu.SemaphoreType.DMA((SPLIT + len(others) - 1 + onehot.shape[0],)),
        ],
        compiler_params=PARAMS,
        name="route",
    )(near(rows), near(w_in), *[far(one) for one in others])


def sums_kernel(parts, pieces, *refs):
    vec_refs = refs[:parts]
    neg_refs = refs[parts : parts + pieces]
    out_refs = refs[parts + pieces :]
    vec = jnp.concatenate([ref[...] for ref in vec_refs], axis=0)
    users = vec_refs[0].shape[0]
    width = vec.shape[1] - LANES
    digits = vec[:, width:].astype(f32)
    label_ids = digits[:, 0:1] + 256.0 * digits[:, 1:2] + 65536.0 * digits[:, 2:3]
    vec = vec[:, :width]
    total = None
    for ref in neg_refs:
        extra = ref[width:, :].astype(f32)
        ids = extra[0:1] + 256.0 * extra[1:2] + 65536.0 * extra[2:3]
        terms = jnp.exp(logit_scale * mm(vec, ref[:width, :])) * (1.0 / extra[3:4])
        terms = jnp.where(ids != label_ids, terms, 0.0)
        total = terms if total is None else total + terms
    total = to_row(jnp.sum(total, axis=1, keepdims=True))
    for part, ref in enumerate(out_refs):
        ref[...] = total[:, part * users : (part + 1) * users]


def negative_sums(vecs, negs):
    users = vecs[0].shape[0]
    return pl.pallas_call(
        functools.partial(sums_kernel, len(vecs), len(negs)),
        out_shape=[pltpu.VMEM((1, users), f32) for _ in vecs],
        compiler_params=PARAMS,
        name="negative_sums",
    )(*[near(one) for one in [*vecs, *negs]])


def swap_pool(array, size, bit):
    return lax.ppermute(array, "pool", [(at, at ^ bit) for at in range(size)])


def swap_user(array, size, mask):
    return lax.ppermute(array, "user", [(at, at ^ mask) for at in range(size)])


def gather_negatives(own, user_size, pool_size):
    pieces = [own]
    for mask in range(1, pool_size // 2):
        pieces.append(swap_pool(own, pool_size, mask))
    others = []
    for piece in pieces:
        others.append(swap_user(piece, user_size, 1))
    return pieces + others


def on_device(
    user_size,
    pool_size,
    item_feats,
    w_in,
    bias_in,
    w_out,
    bilinear,
    fetch_table,
    hist_index,
    hist_len,
    route_init,
    label_index,
    label_ids,
    label_counts,
    neg_feats,
    neg_ids,
    neg_counts,
):
    weights = (w_in, bias_in.reshape(1, -1), w_out)
    outgoing, packed = select_rows(
        user_size, pool_size, fetch_table, item_feats, neg_feats, neg_ids.reshape(1, -1), neg_counts.reshape(1, -1)
    )
    apart = swap_pool(packed, pool_size, pool_size // 2)
    arrived = lax.all_to_all(
        outgoing.reshape(fetch_table.shape[0], fetch_table.shape[2], -1),
        ("pool", "user"),
        split_axis=0,
        concat_axis=0,
        tiled=True,
    )
    arrived = arrived.reshape(outgoing.shape)

    own_neg = neg_tower(packed, apart, weights)
    length = hist_len.reshape(1, -1)
    renumbered = functools.partial(
        renumber, cap=fetch_table.shape[2], user_size=user_size, pool_size=pool_size
    )
    onehot, first, moved = prepare(renumbered, hist_index, length, route_init, outgoing.shape[0])
    negs = gather_negatives(own_neg, user_size, pool_size)

    interests, vec, positive = route(
        renumbered,
        arrived,
        w_in,
        bias_in.reshape(1, -1),
        w_out,
        bilinear,
        onehot,
        first,
        moved,
        length,
        route_init,
        label_index.reshape(1, -1),
        label_ids.reshape(1, -1),
        label_counts.reshape(1, -1),
    )
    away = range(2, user_size, 2)
    vecs = [vec]
    for mask in away:
        vecs.append(swap_user(vec, user_size, mask))
    sums = negative_sums(vecs, negs)
    partition = jnp.exp(positive) + sums[0]
    for mask, one in zip(away, sums[1:]):
        partition += swap_user(one, user_size, mask)
    user_loss = jnp.log(partition) - positive
    return (interests, user_loss.reshape(-1))


def solution(mesh):
    both = ("user", "pool")
    in_specs = (
        P(both, None),
        P(),
        P(),
        P(),
        P(),
        P(None, both, None),
        P(both, None),
        P(both),
        P(both, None, None),
        P(both),
        P(both),
        P(both),
        P(both, None),
        P(both),
        P(both),
    )
    out_specs = (P(both, None), P(both))

    def body(*args):
        return on_device(mesh.shape["user"], mesh.shape["pool"], *args)

    return jax.shard_map(body, mesh=mesh, in_specs=in_specs, out_specs=out_specs, check_vma=False)
```

```python
import functools

import jax
import jax.numpy as jnp
from jax import lax
from jax.experimental import pallas as pl
from jax.experimental.pallas import tpu as pltpu
from jax.sharding import PartitionSpec as P


INTERESTS = 4
ITERS = 3
LANES = 128
SUB = 8
EXTRA = 16
SPLIT = 4
GROUP_USERS = 8

norm_epsilon = 1e-06
attend_scale = 8.0
logit_scale = 20.0

f32 = jnp.float32
bf16 = jnp.bfloat16
i32 = jnp.int32


INSIDE = pl.BlockSpec(memory_space=pltpu.VMEM)
OUTSIDE = pl.BlockSpec(memory_space=pltpu.HBM)
PARAMS = pltpu.CompilerParams(vmem_limit_bytes=20 << 20)


def near(array):
    return pltpu.with_memory_space_constraint(array, pltpu.VMEM)


def far(array):
    return pltpu.with_memory_space_constraint(array, pltpu.HBM)


def mm(a, b):
    return jnp.dot(a, b, preferred_element_type=f32)


def mm_nt(a, b):
    return lax.dot_general(a, b, (((1,), (1,)), ((), ())), preferred_element_type=f32)


def iota(shape, axis):
    return lax.broadcasted_iota(i32, shape, axis)


def to_column(row):
    n = row.shape[1]
    eye = iota((n, n), 0) == iota((n, n), 1)
    return jnp.sum(jnp.where(eye, row, 0.0), axis=1, keepdims=True)


def to_row(column):
    n = column.shape[0]
    eye = iota((n, n), 0) == iota((n, n), 1)
    return jnp.sum(jnp.where(eye, column, 0.0), axis=0, keepdims=True)


def id_digits(ids_row):
    low = (ids_row & 255).astype(f32)
    mid = ((ids_row >> 8) & 255).astype(f32)
    high = (ids_row >> 16).astype(f32)
    return low, mid, high


def lane_columns(columns, rows):
    lane = iota((rows, LANES), 1)
    out = jnp.zeros((rows, LANES), f32)
    for at, column in enumerate(columns):
        out = jnp.where(lane == at, column, out)
    return out


def shift_of(size):
    assert size & (size - 1) == 0
    return size.bit_length() - 1


def renumber(slot, cap, user_size, pool_size):
    block = slot >> shift_of(cap)
    place = ((block & (pool_size - 1)) << shift_of(user_size)) + (block >> shift_of(pool_size))
    return (place << shift_of(cap)) + (slot & (cap - 1))


class Copies:
    def __init__(self, source, target, sems, first, count):
        size = source.shape[0] // count
        self.copies = [
            pltpu.make_async_copy(
                source.at[pl.ds(at * size, size)],
                target.at[pl.ds(at * size, size)],
                sems.at[first + at],
            )
            for at in range(count)
        ]
        for copy in self.copies:
            copy.start()

    def wait(self):
        for copy in self.copies:
            copy.wait()


def select_kernel(
    user_size,
    pool_size,
    fetch,
    rows,
    negs,
    ids,
    counts,
    out,
    packed,
    fetch_ref,
    rows_ref,
    out_ref,
    extra_ref,
    ids_ref,
    counts_ref,
    sems,
):
    table = Copies(fetch, fetch_ref, sems, 0, 1)
    small = [Copies(ids, ids_ref, sems, 1, 1), Copies(counts, counts_ref, sems, 2, 1)]
    copy = Copies(rows, rows_ref, sems, 5, SPLIT)
    kept = negs.shape[0]
    body = pltpu.make_async_copy(negs, packed.at[pl.ds(0, kept)], sems.at[3])
    body.start()
    _, cap, blocks = fetch_ref.shape
    count = blocks * cap
    row = iota((count, blocks), 0)
    start = renumber(iota((1, blocks), 1) * cap, cap, user_size, pool_size)
    pick = jnp.where((row >= start) & (row < start + cap), 1.0, 0.0).astype(bf16)
    place = iota((count, cap), 1) == (iota((count, cap), 0) & (cap - 1))
    table.wait()
    picked = fetch_ref[0]
    high = mm_nt(pick, (picked >> 7).astype(f32).astype(bf16))
    low = mm_nt(pick, (picked & 127).astype(f32).astype(bf16))
    column = jnp.sum(jnp.where(place, high * 128.0 + low, 0.0), axis=1, keepdims=True)
    item = iota((count, rows_ref.shape[0]), 1).astype(f32)
    chosen = jnp.where(item == column, 1.0, 0.0).astype(bf16)
    for one in small:
        one.wait()
    numbers = id_digits(ids_ref[...]) + (counts_ref[...].astype(f32),)
    at = iota((EXTRA, kept), 0)
    extra = jnp.zeros((EXTRA, kept), f32)
    for line, one in enumerate(numbers):
        extra = jnp.where(at == line, one, extra)
    extra_ref[...] = jnp.zeros(extra_ref.shape, bf16)
    extra_ref[:, :kept] = extra.astype(bf16)
    tail = pltpu.make_async_copy(extra_ref, packed.at[pl.ds(kept, EXTRA)], sems.at[4])
    tail.start()
    copy.wait()
    size = count // SPLIT
    for part in range(SPLIT):
        cut = slice(part * size, (part + 1) * size)
        out_ref[cut, :] = mm(chosen[cut], rows_ref[...]).astype(bf16)
        Copies(out_ref.at[pl.ds(part * size, size)], out.at[pl.ds(part * size, size)], sems, 5 + SPLIT + part, 1)
    body.wait()
    tail.wait()
    for part in range(SPLIT):
        there = pl.ds(part * size, size)
        pltpu.make_async_copy(out_ref.at[there], out.at[there], sems.at[5 + SPLIT + part]).wait()


def select_rows(user_size, pool_size, fetch, rows, negs, ids, counts):
    blocks, _, cap = fetch.shape
    packed = (negs.shape[0] + EXTRA, negs.shape[1])
    chosen = (blocks * cap, rows.shape[1])
    return pl.pallas_call(
        functools.partial(select_kernel, user_size, pool_size),
        in_specs=[OUTSIDE] * 5,
        out_specs=[OUTSIDE, OUTSIDE],
        out_shape=[jax.ShapeDtypeStruct(chosen, bf16), jax.ShapeDtypeStruct(packed, bf16)],
        scratch_shapes=[
            pltpu.VMEM((1, cap, blocks), i32),
            pltpu.VMEM(rows.shape, bf16),
            pltpu.VMEM(chosen, bf16),
            pltpu.VMEM((EXTRA, negs.shape[1]), bf16),
            pltpu.VMEM(ids.shape, i32),
            pltpu.VMEM(counts.shape, i32),
            pltpu.SemaphoreType.DMA((5 + 2 * SPLIT,)),
        ],
        compiler_params=PARAMS,
        name="select_rows",
    )(*[far(one) for one in (fetch.transpose(1, 2, 0), rows, negs, ids, counts)])


def tower(rows_ref, w_in_ref, bias, w_out, bias_ref, out_ref, sems):
    small = Copies(bias, bias_ref, sems, 0, 1)
    large = Copies(w_out, out_ref, sems, 1, SPLIT)
    hidden = mm(rows_ref[...], w_in_ref[...])
    small.wait()
    hidden = jnp.maximum(hidden + bias_ref[...], 0.0).astype(bf16)
    large.wait()
    embedding = mm(hidden, out_ref[...])
    total = jnp.sum(embedding * embedding, axis=1, keepdims=True)
    return embedding * lax.rsqrt(total + norm_epsilon)


def neg_kernel(
    own_ref, apart_ref, w_in_ref, bias, w_out, out_ref, rows_ref, bias_ref, w_out_ref, sems
):
    count = rows_ref.shape[0] // 2
    rows_ref[:count, :] = own_ref[:count, :]
    rows_ref[count:, :] = apart_ref[:count, :]
    unit = tower(rows_ref, w_in_ref, bias, w_out, bias_ref, w_out_ref, sems)
    width = unit.shape[1]
    out_ref[:width, :] = unit.T.astype(bf16)
    out_ref[width:, :count] = own_ref[count:, :count]
    out_ref[width:, count:] = apart_ref[count:, :count]


def neg_tower(own, apart, w_in, bias, w_out):
    count = own.shape[0] - EXTRA
    width = own.shape[1]
    return pl.pallas_call(
        neg_kernel,
        in_specs=[INSIDE, INSIDE, INSIDE, OUTSIDE, OUTSIDE],
        out_shape=pltpu.VMEM((width + EXTRA, 2 * count), bf16),
        scratch_shapes=[
            pltpu.VMEM((2 * count, width), bf16),
            pltpu.VMEM(bias.shape, f32),
            pltpu.VMEM(w_out.shape, bf16),
            pltpu.SemaphoreType.DMA((1 + SPLIT,)),
        ],
        compiler_params=PARAMS,
        name="neg_tower",
    )(near(own), near(apart), near(w_in), far(bias), far(w_out))


def event_weights(logits, live):
    raised = [jnp.exp(one) for one in logits]
    total = functools.reduce(jnp.add, raised)
    return [(one / total * live).astype(bf16).astype(f32) for one in raised]


def scatter_weights(weights, upper, onehot_ref, slot_ref):
    users = weights[0].shape[0]
    pages = slot_ref.shape[1] // LANES
    count = pages * INTERESTS * SUB
    for group in range(users // GROUP_USERS):
        at = slice(group * GROUP_USERS, (group + 1) * GROUP_USERS)
        base = jnp.concatenate(
            [
                jnp.where(upper[at] == page, weights[k][at], 0.0)
                for page in range(pages)
                for k in range(INTERESTS)
            ],
            axis=0,
        )
        user = iota((count, 1), 0) & (GROUP_USERS - 1)
        left = jnp.concatenate(
            [
                jnp.where((user >> 1) == pair, base, 0.0).astype(bf16)
                for pair in range(GROUP_USERS // 2)
            ],
            axis=1,
        )
        both = mm(left, onehot_ref[group])
        own = jnp.where((user & 1) == 0, both[:, :LANES], both[:, LANES:])
        for page in range(pages):
            for k in range(INTERESTS):
                source = (page * INTERESTS + k) * SUB
                target = k * users + group * GROUP_USERS
                slot_ref[target : target + SUB, page * LANES : (page + 1) * LANES] = own[
                    source : source + SUB
                ]


def live_mask(length_ref, shape):
    length = to_column(length_ref[...].astype(f32))
    return jnp.where(iota(shape, 1).astype(f32) < length, 1.0, 0.0)


def prepare_kernel(
    renumbered,
    index,
    length,
    init,
    w_in,
    onehot,
    slots,
    moved,
    w_in_ref,
    index_ref,
    length_ref,
    init_ref,
    onehot_ref,
    slot_ref,
    moved_ref,
    sems,
):
    pairs = ((index, index_ref), (length, length_ref), (init, init_ref))
    copies = [Copies(*pair, sems, at, 1) for at, pair in enumerate(pairs)]
    users, events = index_ref.shape
    groups = users // GROUP_USERS
    weight = Copies(w_in, w_in_ref, sems, 5 + groups, SPLIT)
    copies[0].wait()
    index = renumbered(index_ref[...])
    moved_ref[...] = index
    back = [Copies(moved_ref, moved, sems, 3, 1)]
    upper = index >> 7
    lower = (index & (LANES - 1)).astype(f32).T
    lane_id = iota((events, LANES), 1).astype(f32)
    for group in range(groups):
        for within in range(GROUP_USERS):
            user = group * GROUP_USERS + within
            pair, side = divmod(within, 2)
            hit = jnp.where(lane_id == lower[:, user : user + 1], 1.0, 0.0).astype(bf16)
            onehot_ref[
                group, pair * events : (pair + 1) * events, side * LANES : (side + 1) * LANES
            ] = hit
        there = pl.ds(group, 1)
        back.append(Copies(onehot_ref.at[there], onehot.at[there], sems, 5 + group, 1))
    for one in copies[1:]:
        one.wait()
    live = live_mask(length_ref, index.shape)
    weights = event_weights([init_ref[:, k, :] for k in range(INTERESTS)], live)
    scatter_weights(weights, upper, onehot_ref, slot_ref)
    back.append(Copies(slot_ref, slots, sems, 4, 1))
    back.append(weight)
    for one in back:
        one.wait()


def prepare(renumbered, index, length, init, w_in, slots):
    users, events = index.shape
    groups = users // GROUP_USERS
    onehot = (groups, GROUP_USERS // 2 * events, 2 * LANES)
    first = (INTERESTS * users, slots)
    return pl.pallas_call(
        functools.partial(prepare_kernel, renumbered),
        in_specs=[OUTSIDE] * 4,
        out_specs=[OUTSIDE] * 3 + [INSIDE],
        out_shape=[
            pltpu.HBM(onehot, bf16),
            pltpu.HBM(first, f32),
            pltpu.HBM(index.shape, i32),
            pltpu.VMEM(w_in.shape, bf16),
        ],
        scratch_shapes=[
            pltpu.VMEM(index.shape, i32),
            pltpu.VMEM(length.shape, i32),
            pltpu.VMEM(init.shape, f32),
            pltpu.VMEM(onehot, bf16),
            pltpu.VMEM(first, f32),
            pltpu.VMEM(index.shape, i32),
            pltpu.SemaphoreType.DMA((5 + groups + SPLIT,)),
        ],
        compiler_params=PARAMS,
        name="prepare",
    )(far(index), far(length), far(init), far(w_in))


def route_kernel(
    renumbered,
    rows_ref,
    w_in_ref,
    bias,
    w_out,
    bilinear,
    onehot,
    first,
    index,
    length,
    init,
    label,
    ids,
    counts,
    interests_ref,
    vec_ref,
    positive_ref,
    bias_ref,
    out_ref,
    map_ref,
    onehot_ref,
    first_ref,
    index_ref,
    length_ref,
    init_ref,
    label_ref,
    ids_ref,
    counts_ref,
    slot_ref,
    sems,
):
    pairs = (
        (bilinear, map_ref),
        (first, first_ref),
        (index, index_ref),
        (length, length_ref),
        (init, init_ref),
        (label, label_ref),
        (ids, ids_ref),
        (counts, counts_ref),
    )
    start = 1 + SPLIT
    others = [Copies(*pair, sems, start + at, 1) for at, pair in enumerate(pairs)]
    unit = tower(rows_ref, w_in_ref, bias, w_out, bias_ref, out_ref, sems).astype(bf16)
    fetch = Copies(onehot, onehot_ref, sems, start + len(pairs), onehot.shape[0])
    for other in others:
        other.wait()
    mapped = mm(unit, map_ref[...]).astype(bf16)
    users, events = index_ref.shape
    slots, width = mapped.shape
    index = index_ref[...]
    upper = index >> 7
    lower = index & (LANES - 1)
    live = live_mask(length_ref, index.shape)
    logits = [init_ref[:, k, :] for k in range(INTERESTS)]
    capsules = None
    for iteration in range(ITERS):
        if iteration == 1:
            fetch.wait()
        if iteration:
            scatter_weights(event_weights(logits, live), upper, onehot_ref, slot_ref)
        slot_weights = first_ref[...] if iteration == 0 else slot_ref[...]
        coarse = slot_weights.astype(bf16)
        rest = (slot_weights - coarse.astype(f32)).astype(bf16)
        sums = mm(coarse, mapped) + mm(rest, mapped)
        norm_sq = jnp.sum(sums * sums, axis=1, keepdims=True)
        capsules = sums * (jnp.sqrt(norm_sq) / (1.0 + norm_sq))
        if iteration + 1 < ITERS:
            scores = mm_nt(capsules.astype(bf16), mapped)
            for k in range(INTERESTS):
                chunks = []
                for at in range(0, events, LANES):
                    low = lower[:, at : at + LANES]
                    high = upper[:, at : at + LANES]
                    found = jnp.zeros((users, LANES), f32)
                    for page in range(slots // LANES):
                        piece = scores[
                            k * users : (k + 1) * users, page * LANES : (page + 1) * LANES
                        ]
                        taken = jnp.take_along_axis(
                            piece, low, axis=1, mode="promise_in_bounds"
                        )
                        found = jnp.where(high == page, taken, found)
                    chunks.append(found)
                logits[k] = logits[k] + jnp.concatenate(chunks, axis=1)
    each = [capsules[k * users : (k + 1) * users] for k in range(INTERESTS)]
    for k in range(INTERESTS):
        interests_ref[:, k * width : (k + 1) * width] = each[k]
    label = to_column(renumbered(label_ref[...]).astype(f32))
    chosen = jnp.where(iota((users, slots), 1).astype(f32) == label, 1.0, 0.0).astype(bf16)
    label_rows = mm(chosen, unit)
    raised = [
        jnp.exp(attend_scale * jnp.sum(one * label_rows, axis=1, keepdims=True)) for one in each
    ]
    total = functools.reduce(jnp.add, raised)
    user_vec = functools.reduce(jnp.add, [(r / total) * one for r, one in zip(raised, each)])
    user_vec = user_vec.astype(bf16)
    vec_ref[:, :width] = user_vec
    vec_ref[:, width:] = lane_columns([to_column(one) for one in id_digits(ids_ref[...])], users).astype(bf16)
    match = jnp.sum(user_vec.astype(f32) * label_rows, axis=1, keepdims=True)
    positive_ref[...] = logit_scale * to_row(match) - jnp.log(counts_ref[...].astype(f32))


def route(renumbered, rows, w_in, *others):
    _, _, bilinear, onehot, first, index, _, _, _, _, _ = others
    users = index.shape[0]
    width = bilinear.shape[1]
    return pl.pallas_call(
        functools.partial(route_kernel, renumbered),
        in_specs=[INSIDE] * 2 + [OUTSIDE] * len(others),
        out_shape=[
            jax.ShapeDtypeStruct((users, INTERESTS * width), f32),
            pltpu.VMEM((users, width + LANES), bf16),
            pltpu.VMEM((1, users), f32),
        ],
        scratch_shapes=[pltpu.VMEM(one.shape, one.dtype) for one in others]
        + [
            pltpu.VMEM(first.shape, f32),
            pltpu.SemaphoreType.DMA((SPLIT + len(others) - 1 + onehot.shape[0],)),
        ],
        compiler_params=PARAMS,
        name="route",
    )(near(rows), near(w_in), *[far(one) for one in others])


def sums_kernel(parts, pieces, *refs):
    vec_refs = refs[:parts]
    neg_refs = refs[parts : parts + pieces]
    out_refs = refs[parts + pieces :]
    vec = jnp.concatenate([ref[...] for ref in vec_refs], axis=0)
    users = vec_refs[0].shape[0]
    width = vec.shape[1] - LANES
    digits = vec[:, width:].astype(f32)
    label_ids = digits[:, 0:1] + 256.0 * digits[:, 1:2] + 65536.0 * digits[:, 2:3]
    vec = vec[:, :width]
    total = None
    for ref in neg_refs:
        extra = ref[width:, :].astype(f32)
        ids = extra[0:1] + 256.0 * extra[1:2] + 65536.0 * extra[2:3]
        terms = jnp.exp(logit_scale * mm(vec, ref[:width, :])) * (1.0 / extra[3:4])
        terms = jnp.where(ids != label_ids, terms, 0.0)
        total = terms if total is None else total + terms
    total = to_row(jnp.sum(total, axis=1, keepdims=True))
    for part, ref in enumerate(out_refs):
        ref[...] = total[:, part * users : (part + 1) * users]


def negative_sums(vecs, negs):
    users = vecs[0].shape[0]
    return pl.pallas_call(
        functools.partial(sums_kernel, len(vecs), len(negs)),
        out_shape=[pltpu.VMEM((1, users), f32) for _ in vecs],
        compiler_params=PARAMS,
        name="negative_sums",
    )(*[near(one) for one in [*vecs, *negs]])


def swap_pool(array, size, bit):
    return lax.ppermute(array, "pool", [(at, at ^ bit) for at in range(size)])


def late_masks(pool_size):
    return range(2, pool_size // 2, 2)


def swap_user(array, size, mask):
    return lax.ppermute(array, "user", [(at, at ^ mask) for at in range(size)])


def swap_both(array, user_size, pool_size, user_mask, pool_mask):
    perm = [
        (user * pool_size + pool, (user ^ user_mask) * pool_size + (pool ^ pool_mask))
        for user in range(user_size)
        for pool in range(pool_size)
    ]
    return lax.ppermute(array, ("user", "pool"), perm)


def piece_masks(user_size):
    masks = [(user, pool) for user in range(0, user_size, 2) for pool in (0, 1)]
    return masks[:0:-1]


def gather_negatives(own, user_size, pool_size):
    pieces = [own]
    for user, pool in piece_masks(user_size):
        pieces.append(swap_both(own, user_size, pool_size, user, pool))
    others = []
    for piece in pieces:
        others.append(swap_user(piece, user_size, 1))
    return pieces + others


def on_device(
    user_size,
    pool_size,
    item_feats,
    w_in,
    bias_in,
    w_out,
    bilinear,
    fetch_table,
    hist_index,
    hist_len,
    route_init,
    label_index,
    label_ids,
    label_counts,
    neg_feats,
    neg_ids,
    neg_counts,
):
    outgoing, packed = select_rows(
        user_size, pool_size, fetch_table, item_feats, neg_feats, neg_ids.reshape(1, -1), neg_counts.reshape(1, -1)
    )
    apart = swap_pool(packed, pool_size, pool_size // 2)
    arrived = lax.all_to_all(
        outgoing.reshape(fetch_table.shape[0], fetch_table.shape[2], -1),
        ("pool", "user"),
        split_axis=0,
        concat_axis=0,
        tiled=True,
    )
    arrived = arrived.reshape(outgoing.shape)

    length = hist_len.reshape(1, -1)
    renumbered = functools.partial(
        renumber, cap=fetch_table.shape[2], user_size=user_size, pool_size=pool_size
    )
    onehot, first, moved, w_in = prepare(
        renumbered, hist_index, length, route_init, w_in, outgoing.shape[0]
    )
    own_neg = neg_tower(packed, apart, w_in, bias_in.reshape(1, -1), w_out)
    negs = gather_negatives(own_neg, user_size, pool_size)

    interests, vec, positive = route(
        renumbered,
        arrived,
        w_in,
        bias_in.reshape(1, -1),
        w_out,
        bilinear,
        onehot,
        first,
        moved,
        length,
        route_init,
        label_index.reshape(1, -1),
        label_ids.reshape(1, -1),
        label_counts.reshape(1, -1),
    )
    away = late_masks(pool_size)
    vecs = [vec]
    for mask in away:
        vecs.append(swap_pool(vec, pool_size, mask))
    sums = negative_sums(vecs, negs)
    partition = jnp.exp(positive) + sums[0]
    for mask, one in zip(away, sums[1:]):
        partition += swap_pool(one, pool_size, mask)
    user_loss = jnp.log(partition) - positive
    return (interests, user_loss.reshape(-1))


def solution(mesh):
    both = ("user", "pool")
    in_specs = (
        P(both, None),
        P(),
        P(),
        P(),
        P(),
        P(None, both, None),
        P(both, None),
        P(both),
        P(both, None, None),
        P(both),
        P(both),
        P(both),
        P(both, None),
        P(both),
        P(both),
    )
    out_specs = (P(both, None), P(both))

    def body(*args):
        return on_device(mesh.shape["user"], mesh.shape["pool"], *args)

    return jax.shard_map(body, mesh=mesh, in_specs=in_specs, out_specs=out_specs, check_vma=False)
```

```python
import functools

import jax
import jax.numpy as jnp
from jax import lax
from jax.experimental import pallas as pl
from jax.experimental.pallas import tpu as pltpu
from jax.sharding import PartitionSpec as P


INTERESTS = 4
ITERS = 3
LANES = 128
SUB = 8
EXTRA = 16
SPLIT = 4
HALVES = 2
GROUP_USERS = 8

norm_epsilon = 1e-06
attend_scale = 8.0
logit_scale = 20.0

f32 = jnp.float32
bf16 = jnp.bfloat16
i32 = jnp.int32


INSIDE = pl.BlockSpec(memory_space=pltpu.VMEM)
OUTSIDE = pl.BlockSpec(memory_space=pltpu.HBM)
PARAMS = pltpu.CompilerParams(vmem_limit_bytes=20 << 20)


def near(array):
    return pltpu.with_memory_space_constraint(array, pltpu.VMEM)


def far(array):
    return pltpu.with_memory_space_constraint(array, pltpu.HBM)


def mm(a, b):
    return jnp.dot(a, b, preferred_element_type=f32)


def mm_nt(a, b):
    return lax.dot_general(a, b, (((1,), (1,)), ((), ())), preferred_element_type=f32)


def iota(shape, axis):
    return lax.broadcasted_iota(i32, shape, axis)


def to_column(row):
    n = row.shape[1]
    eye = iota((n, n), 0) == iota((n, n), 1)
    return jnp.sum(jnp.where(eye, row, 0.0), axis=1, keepdims=True)


def to_row(column):
    n = column.shape[0]
    eye = iota((n, n), 0) == iota((n, n), 1)
    return jnp.sum(jnp.where(eye, column, 0.0), axis=0, keepdims=True)


def id_digits(ids_row):
    low = (ids_row & 255).astype(f32)
    mid = ((ids_row >> 8) & 255).astype(f32)
    high = (ids_row >> 16).astype(f32)
    return low, mid, high


def lane_columns(columns, rows):
    lane = iota((rows, LANES), 1)
    out = jnp.zeros((rows, LANES), f32)
    for at, column in enumerate(columns):
        out = jnp.where(lane == at, column, out)
    return out


def shift_of(size):
    assert size & (size - 1) == 0
    return size.bit_length() - 1


def renumber(slot, cap, user_size, pool_size):
    block = slot >> shift_of(cap)
    place = ((block & (pool_size - 1)) << shift_of(user_size)) + (block >> shift_of(pool_size))
    return (place << shift_of(cap)) + (slot & (cap - 1))


class Copies:
    def __init__(self, source, target, sems, first, count):
        size = source.shape[0] // count
        self.copies = [
            pltpu.make_async_copy(
                source.at[pl.ds(at * size, size)],
                target.at[pl.ds(at * size, size)],
                sems.at[first + at],
            )
            for at in range(count)
        ]
        for copy in self.copies:
            copy.start()

    def wait(self):
        for copy in self.copies:
            copy.wait()


def select_kernel(
    user_size,
    pool_size,
    fetch,
    rows,
    negs,
    ids,
    counts,
    out,
    packed,
    fetch_ref,
    rows_ref,
    out_ref,
    extra_ref,
    ids_ref,
    counts_ref,
    sems,
):
    table = Copies(fetch, fetch_ref, sems, 0, 1)
    small = [Copies(ids, ids_ref, sems, 1, 1), Copies(counts, counts_ref, sems, 2, 1)]
    copy = Copies(rows, rows_ref, sems, 5, SPLIT)
    kept = negs.shape[0]
    body = pltpu.make_async_copy(negs, packed.at[pl.ds(0, kept)], sems.at[3])
    body.start()
    _, cap, blocks = fetch_ref.shape
    count = blocks * cap
    row = iota((count, blocks), 0)
    start = renumber(iota((1, blocks), 1) * cap, cap, user_size, pool_size)
    pick = jnp.where((row >= start) & (row < start + cap), 1.0, 0.0).astype(bf16)
    place = iota((count, cap), 1) == (iota((count, cap), 0) & (cap - 1))
    table.wait()
    picked = fetch_ref[0]
    high = mm_nt(pick, (picked >> 7).astype(f32).astype(bf16))
    low = mm_nt(pick, (picked & 127).astype(f32).astype(bf16))
    column = jnp.sum(jnp.where(place, high * 128.0 + low, 0.0), axis=1, keepdims=True)
    item = iota((count, rows_ref.shape[0]), 1).astype(f32)
    chosen = jnp.where(item == column, 1.0, 0.0).astype(bf16)
    for one in small:
        one.wait()
    numbers = id_digits(ids_ref[...]) + (counts_ref[...].astype(f32),)
    at = iota((EXTRA, kept), 0)
    extra = jnp.zeros((EXTRA, kept), f32)
    for line, one in enumerate(numbers):
        extra = jnp.where(at == line, one, extra)
    extra_ref[...] = jnp.zeros(extra_ref.shape, bf16)
    extra_ref[:, :kept] = extra.astype(bf16)
    tail = pltpu.make_async_copy(extra_ref, packed.at[pl.ds(kept, EXTRA)], sems.at[4])
    tail.start()
    copy.wait()
    size = count // HALVES
    for part in range(HALVES):
        cut = slice(part * size, (part + 1) * size)
        out_ref[cut, :] = mm(chosen[cut], rows_ref[...]).astype(bf16)
        Copies(out_ref.at[pl.ds(part * size, size)], out.at[pl.ds(part * size, size)], sems, 5 + SPLIT + part, 1)
    body.wait()
    tail.wait()
    for part in range(HALVES):
        there = pl.ds(part * size, size)
        pltpu.make_async_copy(out_ref.at[there], out.at[there], sems.at[5 + SPLIT + part]).wait()


def select_rows(user_size, pool_size, fetch, rows, negs, ids, counts):
    blocks, _, cap = fetch.shape
    packed = (negs.shape[0] + EXTRA, negs.shape[1])
    chosen = (blocks * cap, rows.shape[1])
    return pl.pallas_call(
        functools.partial(select_kernel, user_size, pool_size),
        in_specs=[OUTSIDE] * 5,
        out_specs=[OUTSIDE, OUTSIDE],
        out_shape=[jax.ShapeDtypeStruct(chosen, bf16), jax.ShapeDtypeStruct(packed, bf16)],
        scratch_shapes=[
            pltpu.VMEM((1, cap, blocks), i32),
            pltpu.VMEM(rows.shape, bf16),
            pltpu.VMEM(chosen, bf16),
            pltpu.VMEM((EXTRA, negs.shape[1]), bf16),
            pltpu.VMEM(ids.shape, i32),
            pltpu.VMEM(counts.shape, i32),
            pltpu.SemaphoreType.DMA((5 + 2 * SPLIT,)),
        ],
        compiler_params=PARAMS,
        name="select_rows",
    )(*[far(one) for one in (fetch.transpose(1, 2, 0), rows, negs, ids, counts)])


def tower(rows_ref, w_in_ref, bias, w_out, bias_ref, out_ref, sems):
    small = Copies(bias, bias_ref, sems, 0, 1)
    large = Copies(w_out, out_ref, sems, 1, SPLIT)
    hidden = mm(rows_ref[...], w_in_ref[...])
    small.wait()
    hidden = jnp.maximum(hidden + bias_ref[...], 0.0).astype(bf16)
    large.wait()
    embedding = mm(hidden, out_ref[...])
    total = jnp.sum(embedding * embedding, axis=1, keepdims=True)
    return embedding * lax.rsqrt(total + norm_epsilon)


def neg_kernel(
    own_ref, apart_ref, w_in_ref, bias, w_out, out_ref, rows_ref, bias_ref, w_out_ref, sems
):
    count = rows_ref.shape[0] // 2
    rows_ref[:count, :] = own_ref[:count, :]
    rows_ref[count:, :] = apart_ref[:count, :]
    unit = tower(rows_ref, w_in_ref, bias, w_out, bias_ref, w_out_ref, sems)
    width = unit.shape[1]
    out_ref[:width, :] = unit.T.astype(bf16)
    out_ref[width:, :count] = own_ref[count:, :count]
    out_ref[width:, count:] = apart_ref[count:, :count]


def neg_tower(own, apart, w_in, bias, w_out):
    count = own.shape[0] - EXTRA
    width = own.shape[1]
    return pl.pallas_call(
        neg_kernel,
        in_specs=[INSIDE, INSIDE, INSIDE, OUTSIDE, OUTSIDE],
        out_shape=pltpu.HBM((width + EXTRA, 2 * count), bf16),
        scratch_shapes=[
            pltpu.VMEM((2 * count, width), bf16),
            pltpu.VMEM(bias.shape, f32),
            pltpu.VMEM(w_out.shape, bf16),
            pltpu.SemaphoreType.DMA((1 + SPLIT,)),
        ],
        compiler_params=PARAMS,
        name="neg_tower",
    )(near(own), near(apart), near(w_in), far(bias), far(w_out))


def event_weights(logits, live):
    raised = [jnp.exp(one) for one in logits]
    total = functools.reduce(jnp.add, raised)
    return [(one / total * live).astype(bf16).astype(f32) for one in raised]


def scatter_weights(weights, upper, onehot_ref, slot_ref):
    users = weights[0].shape[0]
    pages = slot_ref.shape[1] // LANES
    count = pages * INTERESTS * SUB
    for group in range(users // GROUP_USERS):
        at = slice(group * GROUP_USERS, (group + 1) * GROUP_USERS)
        base = jnp.concatenate(
            [
                jnp.where(upper[at] == page, weights[k][at], 0.0)
                for page in range(pages)
                for k in range(INTERESTS)
            ],
            axis=0,
        )
        user = iota((count, 1), 0) & (GROUP_USERS - 1)
        left = jnp.concatenate(
            [
                jnp.where((user >> 1) == pair, base, 0.0).astype(bf16)
                for pair in range(GROUP_USERS // 2)
            ],
            axis=1,
        )
        both = mm(left, onehot_ref[group])
        own = jnp.where((user & 1) == 0, both[:, :LANES], both[:, LANES:])
        for page in range(pages):
            for k in range(INTERESTS):
                source = (page * INTERESTS + k) * SUB
                target = k * users + group * GROUP_USERS
                slot_ref[target : target + SUB, page * LANES : (page + 1) * LANES] = own[
                    source : source + SUB
                ]


def live_mask(length_ref, shape):
    length = to_column(length_ref[...].astype(f32))
    return jnp.where(iota(shape, 1).astype(f32) < length, 1.0, 0.0)


def prepare_kernel(
    renumbered,
    index,
    length,
    init,
    w_in,
    onehot,
    slots,
    moved,
    w_in_ref,
    index_ref,
    length_ref,
    init_ref,
    onehot_ref,
    slot_ref,
    moved_ref,
    sems,
):
    pairs = ((index, index_ref), (length, length_ref), (init, init_ref))
    copies = [Copies(*pair, sems, at, 1) for at, pair in enumerate(pairs)]
    users, events = index_ref.shape
    groups = users // GROUP_USERS
    weight = Copies(w_in, w_in_ref, sems, 5 + groups, SPLIT)
    copies[0].wait()
    index = renumbered(index_ref[...])
    moved_ref[...] = index
    back = [Copies(moved_ref, moved, sems, 3, 1)]
    upper = index >> 7
    lower = (index & (LANES - 1)).astype(f32).T
    lane_id = iota((events, LANES), 1).astype(f32)
    for group in range(groups):
        for within in range(GROUP_USERS):
            user = group * GROUP_USERS + within
            pair, side = divmod(within, 2)
            hit = jnp.where(lane_id == lower[:, user : user + 1], 1.0, 0.0).astype(bf16)
            onehot_ref[
                group, pair * events : (pair + 1) * events, side * LANES : (side + 1) * LANES
            ] = hit
        there = pl.ds(group, 1)
        back.append(Copies(onehot_ref.at[there], onehot.at[there], sems, 5 + group, 1))
    for one in copies[1:]:
        one.wait()
    live = live_mask(length_ref, index.shape)
    weights = event_weights([init_ref[:, k, :] for k in range(INTERESTS)], live)
    scatter_weights(weights, upper, onehot_ref, slot_ref)
    back.append(Copies(slot_ref, slots, sems, 4, 1))
    back.append(weight)
    for one in back:
        one.wait()


def prepare(renumbered, index, length, init, w_in, slots):
    users, events = index.shape
    groups = users // GROUP_USERS
    onehot = (groups, GROUP_USERS // 2 * events, 2 * LANES)
    first = (INTERESTS * users, slots)
    return pl.pallas_call(
        functools.partial(prepare_kernel, renumbered),
        in_specs=[OUTSIDE] * 4,
        out_specs=[OUTSIDE] * 3 + [INSIDE],
        out_shape=[
            pltpu.HBM(onehot, bf16),
            pltpu.HBM(first, f32),
            pltpu.HBM(index.shape, i32),
            pltpu.VMEM(w_in.shape, bf16),
        ],
        scratch_shapes=[
            pltpu.VMEM(index.shape, i32),
            pltpu.VMEM(length.shape, i32),
            pltpu.VMEM(init.shape, f32),
            pltpu.VMEM(onehot, bf16),
            pltpu.VMEM(first, f32),
            pltpu.VMEM(index.shape, i32),
            pltpu.SemaphoreType.DMA((5 + groups + SPLIT,)),
        ],
        compiler_params=PARAMS,
        name="prepare",
    )(far(index), far(length), far(init), far(w_in))


def route_kernel(
    renumbered,
    rows_ref,
    w_in_ref,
    bias,
    w_out,
    bilinear,
    onehot,
    first,
    index,
    length,
    init,
    label,
    ids,
    counts,
    interests_ref,
    vec_ref,
    positive_ref,
    bias_ref,
    out_ref,
    map_ref,
    onehot_ref,
    first_ref,
    index_ref,
    length_ref,
    init_ref,
    label_ref,
    ids_ref,
    counts_ref,
    slot_ref,
    sems,
):
    pairs = (
        (bilinear, map_ref),
        (first, first_ref),
        (index, index_ref),
        (length, length_ref),
        (init, init_ref),
        (label, label_ref),
        (ids, ids_ref),
        (counts, counts_ref),
    )
    start = 1 + SPLIT
    others = [Copies(*pair, sems, start + at, 1) for at, pair in enumerate(pairs)]
    unit = tower(rows_ref, w_in_ref, bias, w_out, bias_ref, out_ref, sems).astype(bf16)
    fetch = Copies(onehot, onehot_ref, sems, start + len(pairs), onehot.shape[0])
    for other in others:
        other.wait()
    mapped = mm(unit, map_ref[...]).astype(bf16)
    users, events = index_ref.shape
    slots, width = mapped.shape
    index = index_ref[...]
    upper = index >> 7
    lower = index & (LANES - 1)
    live = live_mask(length_ref, index.shape)
    logits = [init_ref[:, k, :] for k in range(INTERESTS)]
    capsules = None
    for iteration in range(ITERS):
        if iteration == 1:
            fetch.wait()
        if iteration:
            scatter_weights(event_weights(logits, live), upper, onehot_ref, slot_ref)
        slot_weights = first_ref[...] if iteration == 0 else slot_ref[...]
        coarse = slot_weights.astype(bf16)
        rest = (slot_weights - coarse.astype(f32)).astype(bf16)
        sums = mm(coarse, mapped) + mm(rest, mapped)
        norm_sq = jnp.sum(sums * sums, axis=1, keepdims=True)
        capsules = sums * (jnp.sqrt(norm_sq) / (1.0 + norm_sq))
        if iteration + 1 < ITERS:
            scores = mm_nt(capsules.astype(bf16), mapped)
            found = [[None] * (events // LANES) for _ in range(INTERESTS)]
            for part in range(events // LANES):
                rows = [[] for _ in range(INTERESTS)]
                for user in range(0, users, SUB):
                    low = lower[user : user + SUB, part * LANES : (part + 1) * LANES]
                    high = upper[user : user + SUB, part * LANES : (part + 1) * LANES]
                    for k in range(INTERESTS):
                        one = None
                        for page in range(slots // LANES):
                            piece = scores[
                                k * users + user : k * users + user + SUB,
                                page * LANES : (page + 1) * LANES,
                            ]
                            taken = jnp.take_along_axis(
                                piece, low, axis=1, mode="promise_in_bounds"
                            )
                            one = taken if one is None else jnp.where(high == page, taken, one)
                        rows[k].append(one)
                for k in range(INTERESTS):
                    found[k][part] = jnp.concatenate(rows[k], axis=0)
            for k in range(INTERESTS):
                logits[k] = logits[k] + jnp.concatenate(found[k], axis=1)
    each = [capsules[k * users : (k + 1) * users] for k in range(INTERESTS)]
    for k in range(INTERESTS):
        interests_ref[:, k * width : (k + 1) * width] = each[k]
    label = to_column(renumbered(label_ref[...]).astype(f32))
    chosen = jnp.where(iota((users, slots), 1).astype(f32) == label, 1.0, 0.0).astype(bf16)
    label_rows = mm(chosen, unit)
    raised = [
        jnp.exp(attend_scale * jnp.sum(one * label_rows, axis=1, keepdims=True)) for one in each
    ]
    total = functools.reduce(jnp.add, raised)
    user_vec = functools.reduce(jnp.add, [(r / total) * one for r, one in zip(raised, each)])
    user_vec = user_vec.astype(bf16)
    vec_ref[:, :width] = user_vec
    vec_ref[:, width:] = lane_columns([to_column(one) for one in id_digits(ids_ref[...])], users).astype(bf16)
    match = jnp.sum(user_vec.astype(f32) * label_rows, axis=1, keepdims=True)
    positive_ref[...] = logit_scale * to_row(match) - jnp.log(counts_ref[...].astype(f32))


def route(renumbered, rows, w_in, *others):
    _, _, bilinear, onehot, first, index, _, _, _, _, _ = others
    users = index.shape[0]
    width = bilinear.shape[1]
    return pl.pallas_call(
        functools.partial(route_kernel, renumbered),
        in_specs=[INSIDE] * 2 + [OUTSIDE] * len(others),
        out_shape=[
            jax.ShapeDtypeStruct((users, INTERESTS * width), f32),
            pltpu.VMEM((users, width + LANES), bf16),
            pltpu.VMEM((1, users), f32),
        ],
        scratch_shapes=[pltpu.VMEM(one.shape, one.dtype) for one in others]
        + [
            pltpu.VMEM(first.shape, f32),
            pltpu.SemaphoreType.DMA((SPLIT + len(others) - 1 + onehot.shape[0],)),
        ],
        compiler_params=PARAMS,
        name="route",
    )(near(rows), near(w_in), *[far(one) for one in others])


def sums_kernel(parts, pieces, *refs):
    vec_refs = refs[:parts]
    own, *neg_refs = refs[parts : parts + pieces]
    out_refs = refs[parts + pieces : -2]
    own_ref, sems = refs[-2:]
    fetch = Copies(own, own_ref, sems, 0, 1)
    vec = jnp.concatenate([ref[...] for ref in vec_refs], axis=0)
    users = vec_refs[0].shape[0]
    width = vec.shape[1] - LANES
    digits = vec[:, width:].astype(f32)
    label_ids = digits[:, 0:1] + 256.0 * digits[:, 1:2] + 65536.0 * digits[:, 2:3]
    vec = vec[:, :width]
    total = None
    for ref in [*neg_refs, own_ref]:
        if ref is own_ref:
            fetch.wait()
        extra = ref[width:, :].astype(f32)
        ids = extra[0:1] + 256.0 * extra[1:2] + 65536.0 * extra[2:3]
        terms = jnp.exp(logit_scale * mm(vec, ref[:width, :])) * (1.0 / extra[3:4])
        terms = jnp.where(ids != label_ids, terms, 0.0)
        total = terms if total is None else total + terms
    total = to_row(jnp.sum(total, axis=1, keepdims=True))
    for part, ref in enumerate(out_refs):
        ref[...] = total[:, part * users : (part + 1) * users]


def negative_sums(vecs, negs):
    users = vecs[0].shape[0]
    return pl.pallas_call(
        functools.partial(sums_kernel, len(vecs), len(negs)),
        in_specs=[INSIDE] * len(vecs) + [OUTSIDE] + [INSIDE] * (len(negs) - 1),
        scratch_shapes=[pltpu.VMEM(negs[0].shape, bf16), pltpu.SemaphoreType.DMA((1,))],
        out_shape=[pltpu.VMEM((1, users), f32) for _ in vecs],
        compiler_params=PARAMS,
        name="negative_sums",
    )(*[near(one) for one in vecs], far(negs[0]), *[near(one) for one in negs[1:]])


def swap_pool(array, size, bit):
    return lax.ppermute(array, "pool", [(at, at ^ bit) for at in range(size)])


def late_masks(pool_size):
    return range(2, pool_size // 2, 2)


def swap_user(array, size, mask):
    return lax.ppermute(array, "user", [(at, at ^ mask) for at in range(size)])


def swap_both(array, user_size, pool_size, user_mask, pool_mask):
    perm = [
        (user * pool_size + pool, (user ^ user_mask) * pool_size + (pool ^ pool_mask))
        for user in range(user_size)
        for pool in range(pool_size)
    ]
    return lax.ppermute(array, ("user", "pool"), perm)


def piece_masks(user_size):
    masks = [(user, pool) for user in range(0, user_size, 2) for pool in (0, 1)]
    return masks[:0:-1]


def gather_negatives(own, user_size, pool_size):
    pieces = [own]
    for user, pool in piece_masks(user_size):
        pieces.append(swap_both(own, user_size, pool_size, user, pool))
    others = []
    for piece in pieces:
        others.append(swap_user(piece, user_size, 1))
    return pieces + others


def on_device(
    user_size,
    pool_size,
    item_feats,
    w_in,
    bias_in,
    w_out,
    bilinear,
    fetch_table,
    hist_index,
    hist_len,
    route_init,
    label_index,
    label_ids,
    label_counts,
    neg_feats,
    neg_ids,
    neg_counts,
):
    outgoing, packed = select_rows(
        user_size, pool_size, fetch_table, item_feats, neg_feats, neg_ids.reshape(1, -1), neg_counts.reshape(1, -1)
    )
    apart = swap_pool(packed, pool_size, pool_size // 2)
    arrived = lax.all_to_all(
        outgoing.reshape(fetch_table.shape[0], fetch_table.shape[2], -1),
        ("pool", "user"),
        split_axis=0,
        concat_axis=0,
        tiled=True,
    )
    arrived = arrived.reshape(outgoing.shape)

    length = hist_len.reshape(1, -1)
    renumbered = functools.partial(
        renumber, cap=fetch_table.shape[2], user_size=user_size, pool_size=pool_size
    )
    onehot, first, moved, w_in = prepare(
        renumbered, hist_index, length, route_init, w_in, outgoing.shape[0]
    )
    own_neg = neg_tower(packed, apart, w_in, bias_in.reshape(1, -1), w_out)
    negs = gather_negatives(own_neg, user_size, pool_size)

    interests, vec, positive = route(
        renumbered,
        arrived,
        w_in,
        bias_in.reshape(1, -1),
        w_out,
        bilinear,
        onehot,
        first,
        moved,
        length,
        route_init,
        label_index.reshape(1, -1),
        label_ids.reshape(1, -1),
        label_counts.reshape(1, -1),
    )
    away = late_masks(pool_size)
    vecs = [vec]
    for mask in away:
        vecs.append(swap_pool(vec, pool_size, mask))
    sums = negative_sums(vecs, negs)
    partition = jnp.exp(positive) + sums[0]
    for mask, one in zip(away, sums[1:]):
        partition += swap_pool(one, pool_size, mask)
    user_loss = jnp.log(partition) - positive
    return (interests, user_loss.reshape(-1))


def solution(mesh):
    both = ("user", "pool")
    in_specs = (
        P(both, None),
        P(),
        P(),
        P(),
        P(),
        P(None, both, None),
        P(both, None),
        P(both),
        P(both, None, None),
        P(both),
        P(both),
        P(both),
        P(both, None),
        P(both),
        P(both),
    )
    out_specs = (P(both, None), P(both))

    def body(*args):
        return on_device(mesh.shape["user"], mesh.shape["pool"], *args)

    return jax.shard_map(body, mesh=mesh, in_specs=in_specs, out_specs=out_specs, check_vma=False)
```

```python
import functools

import jax
import jax.numpy as jnp
from jax import lax
from jax.experimental import pallas as pl
from jax.experimental.pallas import tpu as pltpu
from jax.sharding import PartitionSpec as P


INTERESTS = 4
ITERS = 3
LANES = 128
SUB = 8
EXTRA = 16
SPLIT = 4
GROUP_USERS = 8

norm_epsilon = 1e-06
attend_scale = 8.0
logit_scale = 20.0

f32 = jnp.float32
bf16 = jnp.bfloat16
i32 = jnp.int32


INSIDE = pl.BlockSpec(memory_space=pltpu.VMEM)
OUTSIDE = pl.BlockSpec(memory_space=pltpu.HBM)
PARAMS = pltpu.CompilerParams(vmem_limit_bytes=20 << 20)


def near(array):
    return pltpu.with_memory_space_constraint(array, pltpu.VMEM)


def far(array):
    return pltpu.with_memory_space_constraint(array, pltpu.HBM)


def mm(a, b):
    return jnp.dot(a, b, preferred_element_type=f32)


def mm_nt(a, b):
    return lax.dot_general(a, b, (((1,), (1,)), ((), ())), preferred_element_type=f32)


def iota(shape, axis):
    return lax.broadcasted_iota(i32, shape, axis)


def to_column(row):
    n = row.shape[1]
    eye = iota((n, n), 0) == iota((n, n), 1)
    return jnp.sum(jnp.where(eye, row, 0.0), axis=1, keepdims=True)


def to_row(column):
    n = column.shape[0]
    eye = iota((n, n), 0) == iota((n, n), 1)
    return jnp.sum(jnp.where(eye, column, 0.0), axis=0, keepdims=True)


def id_digits(ids_row):
    low = (ids_row & 255).astype(f32)
    mid = ((ids_row >> 8) & 255).astype(f32)
    high = (ids_row >> 16).astype(f32)
    return low, mid, high


def lane_columns(columns, rows):
    lane = iota((rows, LANES), 1)
    out = jnp.zeros((rows, LANES), f32)
    for at, column in enumerate(columns):
        out = jnp.where(lane == at, column, out)
    return out


def shift_of(size):
    assert size & (size - 1) == 0
    return size.bit_length() - 1


def renumber(slot, cap, user_size, pool_size):
    block = slot >> shift_of(cap)
    place = ((block & (pool_size - 1)) << shift_of(user_size)) + (block >> shift_of(pool_size))
    return (place << shift_of(cap)) + (slot & (cap - 1))


class Copies:
    def __init__(self, source, target, sems, first, count):
        size = source.shape[0] // count
        self.copies = [
            pltpu.make_async_copy(
                source.at[pl.ds(at * size, size)],
                target.at[pl.ds(at * size, size)],
                sems.at[first + at],
            )
            for at in range(count)
        ]
        for copy in self.copies:
            copy.start()

    def wait(self):
        for copy in self.copies:
            copy.wait()


def select_kernel(
    user_size,
    pool_size,
    fetch,
    rows,
    negs,
    ids,
    counts,
    out,
    packed,
    fetch_ref,
    rows_ref,
    out_ref,
    extra_ref,
    ids_ref,
    counts_ref,
    sems,
):
    table = Copies(fetch, fetch_ref, sems, 0, 1)
    small = [Copies(ids, ids_ref, sems, 1, 1), Copies(counts, counts_ref, sems, 2, 1)]
    copy = Copies(rows, rows_ref, sems, 5, SPLIT)
    kept = negs.shape[0]
    body = pltpu.make_async_copy(negs, packed.at[pl.ds(0, kept)], sems.at[3])
    body.start()
    _, cap, blocks = fetch_ref.shape
    count = blocks * cap
    row = iota((count, blocks), 0)
    start = renumber(iota((1, blocks), 1) * cap, cap, user_size, pool_size)
    pick = jnp.where((row >= start) & (row < start + cap), 1.0, 0.0).astype(bf16)
    place = iota((count, cap), 1) == (iota((count, cap), 0) & (cap - 1))
    table.wait()
    picked = fetch_ref[0]
    high = mm_nt(pick, (picked >> 7).astype(f32).astype(bf16))
    low = mm_nt(pick, (picked & 127).astype(f32).astype(bf16))
    column = jnp.sum(jnp.where(place, high * 128.0 + low, 0.0), axis=1, keepdims=True)
    item = iota((count, rows_ref.shape[0]), 1).astype(f32)
    chosen = jnp.where(item == column, 1.0, 0.0).astype(bf16)
    for one in small:
        one.wait()
    numbers = id_digits(ids_ref[...]) + (counts_ref[...].astype(f32),)
    at = iota((EXTRA, kept), 0)
    extra = jnp.zeros((EXTRA, kept), f32)
    for line, one in enumerate(numbers):
        extra = jnp.where(at == line, one, extra)
    extra_ref[...] = jnp.zeros(extra_ref.shape, bf16)
    extra_ref[:, :kept] = extra.astype(bf16)
    tail = pltpu.make_async_copy(extra_ref, packed.at[pl.ds(kept, EXTRA)], sems.at[4])
    tail.start()
    copy.wait()
    size = count // SPLIT
    for part in range(SPLIT):
        cut = slice(part * size, (part + 1) * size)
        out_ref[cut, :] = mm(chosen[cut], rows_ref[...]).astype(bf16)
        Copies(out_ref.at[pl.ds(part * size, size)], out.at[pl.ds(part * size, size)], sems, 5 + SPLIT + part, 1)
    body.wait()
    tail.wait()
    for part in range(SPLIT):
        there = pl.ds(part * size, size)
        pltpu.make_async_copy(out_ref.at[there], out.at[there], sems.at[5 + SPLIT + part]).wait()


def select_rows(user_size, pool_size, fetch, rows, negs, ids, counts):
    blocks, _, cap = fetch.shape
    packed = (negs.shape[0] + EXTRA, negs.shape[1])
    chosen = (blocks * cap, rows.shape[1])
    return pl.pallas_call(
        functools.partial(select_kernel, user_size, pool_size),
        in_specs=[OUTSIDE] * 5,
        out_specs=[OUTSIDE, OUTSIDE],
        out_shape=[jax.ShapeDtypeStruct(chosen, bf16), jax.ShapeDtypeStruct(packed, bf16)],
        scratch_shapes=[
            pltpu.VMEM((1, cap, blocks), i32),
            pltpu.VMEM(rows.shape, bf16),
            pltpu.VMEM(chosen, bf16),
            pltpu.VMEM((EXTRA, negs.shape[1]), bf16),
            pltpu.VMEM(ids.shape, i32),
            pltpu.VMEM(counts.shape, i32),
            pltpu.SemaphoreType.DMA((5 + 2 * SPLIT,)),
        ],
        compiler_params=PARAMS,
        name="select_rows",
    )(*[far(one) for one in (fetch.transpose(1, 2, 0), rows, negs, ids, counts)])


def tower(rows_ref, w_in_ref, bias, w_out, bias_ref, out_ref, sems):
    small = Copies(bias, bias_ref, sems, 0, 1)
    large = Copies(w_out, out_ref, sems, 1, SPLIT)
    hidden = mm(rows_ref[...], w_in_ref[...])
    small.wait()
    hidden = jnp.maximum(hidden + bias_ref[...], 0.0).astype(bf16)
    large.wait()
    embedding = mm(hidden, out_ref[...])
    total = jnp.sum(embedding * embedding, axis=1, keepdims=True)
    return embedding * lax.rsqrt(total + norm_epsilon)


def neg_kernel(
    own_ref, apart_ref, w_in_ref, bias, w_out, out_ref, rows_ref, bias_ref, w_out_ref, sems
):
    count = rows_ref.shape[0] // 2
    rows_ref[:count, :] = own_ref[:count, :]
    rows_ref[count:, :] = apart_ref[:count, :]
    unit = tower(rows_ref, w_in_ref, bias, w_out, bias_ref, w_out_ref, sems)
    width = unit.shape[1]
    out_ref[:width, :] = unit.T.astype(bf16)
    out_ref[width:, :count] = own_ref[count:, :count]
    out_ref[width:, count:] = apart_ref[count:, :count]


def neg_tower(own, apart, w_in, bias, w_out):
    count = own.shape[0] - EXTRA
    width = own.shape[1]
    return pl.pallas_call(
        neg_kernel,
        in_specs=[INSIDE, INSIDE, INSIDE, OUTSIDE, OUTSIDE],
        out_shape=pltpu.HBM((width + EXTRA, 2 * count), bf16),
        scratch_shapes=[
            pltpu.VMEM((2 * count, width), bf16),
            pltpu.VMEM(bias.shape, f32),
            pltpu.VMEM(w_out.shape, bf16),
            pltpu.SemaphoreType.DMA((1 + SPLIT,)),
        ],
        compiler_params=PARAMS,
        name="neg_tower",
    )(near(own), near(apart), near(w_in), far(bias), far(w_out))


def event_weights(logits, live):
    raised = [jnp.exp(one) for one in logits]
    total = functools.reduce(jnp.add, raised)
    return [(one / total * live).astype(bf16).astype(f32) for one in raised]


def scatter_weights(weights, upper, onehot_ref, slot_ref):
    users = weights[0].shape[0]
    pages = slot_ref.shape[1] // LANES
    count = pages * INTERESTS * SUB
    for group in range(users // GROUP_USERS):
        at = slice(group * GROUP_USERS, (group + 1) * GROUP_USERS)
        base = jnp.concatenate(
            [
                jnp.where(upper[at] == page, weights[k][at], 0.0)
                for page in range(pages)
                for k in range(INTERESTS)
            ],
            axis=0,
        )
        user = iota((count, 1), 0) & (GROUP_USERS - 1)
        left = jnp.concatenate(
            [
                jnp.where((user >> 1) == pair, base, 0.0).astype(bf16)
                for pair in range(GROUP_USERS // 2)
            ],
            axis=1,
        )
        both = mm(left, onehot_ref[group])
        own = jnp.where((user & 1) == 0, both[:, :LANES], both[:, LANES:])
        for page in range(pages):
            for k in range(INTERESTS):
                source = (page * INTERESTS + k) * SUB
                target = k * users + group * GROUP_USERS
                slot_ref[target : target + SUB, page * LANES : (page + 1) * LANES] = own[
                    source : source + SUB
                ]


def live_mask(length_ref, shape):
    length = to_column(length_ref[...].astype(f32))
    return jnp.where(iota(shape, 1).astype(f32) < length, 1.0, 0.0)


def prepare_kernel(
    renumbered,
    index,
    length,
    init,
    w_in,
    onehot,
    slots,
    moved,
    w_in_ref,
    index_ref,
    length_ref,
    init_ref,
    onehot_ref,
    slot_ref,
    moved_ref,
    sems,
):
    pairs = ((index, index_ref), (length, length_ref), (init, init_ref))
    copies = [Copies(*pair, sems, at, 1) for at, pair in enumerate(pairs)]
    users, events = index_ref.shape
    groups = users // GROUP_USERS
    weight = Copies(w_in, w_in_ref, sems, 5 + groups, SPLIT)
    copies[0].wait()
    index = renumbered(index_ref[...])
    moved_ref[...] = index
    back = [Copies(moved_ref, moved, sems, 3, 1)]
    upper = index >> 7
    lower = (index & (LANES - 1)).astype(f32).T
    lane_id = iota((events, LANES), 1).astype(f32)
    for group in range(groups):
        for within in range(GROUP_USERS):
            user = group * GROUP_USERS + within
            pair, side = divmod(within, 2)
            hit = jnp.where(lane_id == lower[:, user : user + 1], 1.0, 0.0).astype(bf16)
            onehot_ref[
                group, pair * events : (pair + 1) * events, side * LANES : (side + 1) * LANES
            ] = hit
        there = pl.ds(group, 1)
        back.append(Copies(onehot_ref.at[there], onehot.at[there], sems, 5 + group, 1))
    for one in copies[1:]:
        one.wait()
    live = live_mask(length_ref, index.shape)
    weights = event_weights([init_ref[:, k, :] for k in range(INTERESTS)], live)
    scatter_weights(weights, upper, onehot_ref, slot_ref)
    back.append(Copies(slot_ref, slots, sems, 4, 1))
    back.append(weight)
    for one in back:
        one.wait()


def prepare(renumbered, index, length, init, w_in, slots):
    users, events = index.shape
    groups = users // GROUP_USERS
    onehot = (groups, GROUP_USERS // 2 * events, 2 * LANES)
    first = (INTERESTS * users, slots)
    return pl.pallas_call(
        functools.partial(prepare_kernel, renumbered),
        in_specs=[OUTSIDE] * 4,
        out_specs=[OUTSIDE] * 3 + [INSIDE],
        out_shape=[
            pltpu.HBM(onehot, bf16),
            pltpu.HBM(first, f32),
            pltpu.HBM(index.shape, i32),
            pltpu.VMEM(w_in.shape, bf16),
        ],
        scratch_shapes=[
            pltpu.VMEM(index.shape, i32),
            pltpu.VMEM(length.shape, i32),
            pltpu.VMEM(init.shape, f32),
            pltpu.VMEM(onehot, bf16),
            pltpu.VMEM(first, f32),
            pltpu.VMEM(index.shape, i32),
            pltpu.SemaphoreType.DMA((5 + groups + SPLIT,)),
        ],
        compiler_params=PARAMS,
        name="prepare",
    )(far(index), far(length), far(init), far(w_in))


def route_kernel(
    renumbered,
    rows_ref,
    w_in_ref,
    bias,
    w_out,
    bilinear,
    onehot,
    first,
    index,
    length,
    init,
    label,
    ids,
    counts,
    interests_ref,
    vec_ref,
    positive_ref,
    bias_ref,
    out_ref,
    map_ref,
    onehot_ref,
    first_ref,
    index_ref,
    length_ref,
    init_ref,
    label_ref,
    ids_ref,
    counts_ref,
    slot_ref,
    sems,
):
    pairs = (
        (bilinear, map_ref),
        (first, first_ref),
        (index, index_ref),
        (length, length_ref),
        (init, init_ref),
        (label, label_ref),
        (ids, ids_ref),
        (counts, counts_ref),
    )
    start = 1 + SPLIT
    others = [Copies(*pair, sems, start + at, 1) for at, pair in enumerate(pairs)]
    unit = tower(rows_ref, w_in_ref, bias, w_out, bias_ref, out_ref, sems).astype(bf16)
    fetch = Copies(onehot, onehot_ref, sems, start + len(pairs), onehot.shape[0])
    for other in others:
        other.wait()
    mapped = mm(unit, map_ref[...]).astype(bf16)
    users, events = index_ref.shape
    slots, width = mapped.shape
    index = index_ref[...]
    upper = index >> 7
    lower = index & (LANES - 1)
    live = live_mask(length_ref, index.shape)
    logits = [init_ref[:, k, :] for k in range(INTERESTS)]
    capsules = None
    for iteration in range(ITERS):
        if iteration == 1:
            fetch.wait()
        if iteration:
            scatter_weights(event_weights(logits, live), upper, onehot_ref, slot_ref)
        slot_weights = first_ref[...] if iteration == 0 else slot_ref[...]
        coarse = slot_weights.astype(bf16)
        rest = (slot_weights - coarse.astype(f32)).astype(bf16)
        sums = mm(coarse, mapped) + mm(rest, mapped)
        norm_sq = jnp.sum(sums * sums, axis=1, keepdims=True)
        capsules = sums * (jnp.sqrt(norm_sq) / (1.0 + norm_sq))
        if iteration + 1 < ITERS:
            scores = mm_nt(capsules.astype(bf16), mapped)
            found = [[None] * (events // LANES) for _ in range(INTERESTS)]
            for part in range(events // LANES):
                rows = [[] for _ in range(INTERESTS)]
                for user in range(0, users, SUB):
                    low = lower[user : user + SUB, part * LANES : (part + 1) * LANES]
                    high = upper[user : user + SUB, part * LANES : (part + 1) * LANES]
                    for k in range(INTERESTS):
                        one = None
                        for page in range(slots // LANES):
                            piece = scores[
                                k * users + user : k * users + user + SUB,
                                page * LANES : (page + 1) * LANES,
                            ]
                            taken = jnp.take_along_axis(
                                piece, low, axis=1, mode="promise_in_bounds"
                            )
                            one = taken if one is None else jnp.where(high == page, taken, one)
                        rows[k].append(one)
                for k in range(INTERESTS):
                    found[k][part] = jnp.concatenate(rows[k], axis=0)
            for k in range(INTERESTS):
                logits[k] = logits[k] + jnp.concatenate(found[k], axis=1)
    each = [capsules[k * users : (k + 1) * users] for k in range(INTERESTS)]
    for k in range(INTERESTS):
        interests_ref[:, k * width : (k + 1) * width] = each[k]
    label = to_column(renumbered(label_ref[...]).astype(f32))
    chosen = jnp.where(iota((users, slots), 1).astype(f32) == label, 1.0, 0.0).astype(bf16)
    label_rows = mm(chosen, unit)
    raised = [
        jnp.exp(attend_scale * jnp.sum(one * label_rows, axis=1, keepdims=True)) for one in each
    ]
    total = functools.reduce(jnp.add, raised)
    user_vec = functools.reduce(jnp.add, [(r / total) * one for r, one in zip(raised, each)])
    user_vec = user_vec.astype(bf16)
    vec_ref[:, :width] = user_vec
    vec_ref[:, width:] = lane_columns([to_column(one) for one in id_digits(ids_ref[...])], users).astype(bf16)
    match = jnp.sum(user_vec.astype(f32) * label_rows, axis=1, keepdims=True)
    positive_ref[...] = logit_scale * to_row(match) - jnp.log(counts_ref[...].astype(f32))


def route(renumbered, rows, w_in, *others):
    _, _, bilinear, onehot, first, index, _, _, _, _, _ = others
    users = index.shape[0]
    width = bilinear.shape[1]
    return pl.pallas_call(
        functools.partial(route_kernel, renumbered),
        in_specs=[INSIDE] * 2 + [OUTSIDE] * len(others),
        out_shape=[
            pltpu.VMEM((users, INTERESTS * width), f32),
            pltpu.VMEM((users, width + LANES), bf16),
            pltpu.VMEM((1, users), f32),
        ],
        scratch_shapes=[pltpu.VMEM(one.shape, one.dtype) for one in others]
        + [
            pltpu.VMEM(first.shape, f32),
            pltpu.SemaphoreType.DMA((SPLIT + len(others) - 1 + onehot.shape[0],)),
        ],
        compiler_params=PARAMS,
        name="route",
    )(near(rows), near(w_in), *[far(one) for one in others])


def sums_kernel(parts, pieces, *refs):
    vec_refs = refs[:parts]
    neg_refs = refs[parts : parts + pieces]
    out_refs = refs[parts + pieces :]
    vec = jnp.concatenate([ref[...] for ref in vec_refs], axis=0)
    users = vec_refs[0].shape[0]
    width = vec.shape[1] - LANES
    digits = vec[:, width:].astype(f32)
    label_ids = digits[:, 0:1] + 256.0 * digits[:, 1:2] + 65536.0 * digits[:, 2:3]
    vec = vec[:, :width]
    total = None
    for ref in neg_refs:
        extra = ref[width:, :].astype(f32)
        ids = extra[0:1] + 256.0 * extra[1:2] + 65536.0 * extra[2:3]
        terms = jnp.exp(logit_scale * mm(vec, ref[:width, :])) * (1.0 / extra[3:4])
        terms = jnp.where(ids != label_ids, terms, 0.0)
        total = terms if total is None else total + terms
    total = to_row(jnp.sum(total, axis=1, keepdims=True))
    for part, ref in enumerate(out_refs):
        ref[...] = total[:, part * users : (part + 1) * users]


def negative_sums(vecs, negs):
    users = vecs[0].shape[0]
    return pl.pallas_call(
        functools.partial(sums_kernel, len(vecs), len(negs)),
        out_shape=[pltpu.VMEM((1, users), f32) for _ in vecs],
        compiler_params=PARAMS,
        name="negative_sums",
    )(*[near(one) for one in [*vecs, *negs]])


def swap_pool(array, size, bit):
    return lax.ppermute(array, "pool", [(at, at ^ bit) for at in range(size)])


def late_masks(pool_size):
    return range(2, pool_size // 2, 2)


def swap_user(array, size, mask):
    return lax.ppermute(array, "user", [(at, at ^ mask) for at in range(size)])


def swap_both(array, user_size, pool_size, user_mask, pool_mask):
    perm = [
        (user * pool_size + pool, (user ^ user_mask) * pool_size + (pool ^ pool_mask))
        for user in range(user_size)
        for pool in range(pool_size)
    ]
    return lax.ppermute(array, ("user", "pool"), perm)


def piece_masks(user_size):
    masks = [(user, pool) for user in range(0, user_size, 2) for pool in (0, 1)]
    return masks[:0:-1]


def gather_negatives(own, user_size, pool_size):
    pieces = [own]
    for user, pool in piece_masks(user_size):
        pieces.append(swap_both(own, user_size, pool_size, user, pool))
    others = []
    for piece in pieces:
        others.append(swap_user(piece, user_size, 1))
    return pieces + others


def on_device(
    user_size,
    pool_size,
    item_feats,
    w_in,
    bias_in,
    w_out,
    bilinear,
    fetch_table,
    hist_index,
    hist_len,
    route_init,
    label_index,
    label_ids,
    label_counts,
    neg_feats,
    neg_ids,
    neg_counts,
):
    outgoing, packed = select_rows(
        user_size, pool_size, fetch_table, item_feats, neg_feats, neg_ids.reshape(1, -1), neg_counts.reshape(1, -1)
    )
    apart = swap_pool(packed, pool_size, pool_size // 2)
    arrived = lax.all_to_all(
        outgoing.reshape(fetch_table.shape[0], fetch_table.shape[2], -1),
        ("pool", "user"),
        split_axis=0,
        concat_axis=0,
        tiled=True,
    )
    arrived = arrived.reshape(outgoing.shape)

    length = hist_len.reshape(1, -1)
    renumbered = functools.partial(
        renumber, cap=fetch_table.shape[2], user_size=user_size, pool_size=pool_size
    )
    onehot, first, moved, w_in = prepare(
        renumbered, hist_index, length, route_init, w_in, outgoing.shape[0]
    )
    own_neg = neg_tower(packed, apart, w_in, bias_in.reshape(1, -1), w_out)
    negs = gather_negatives(own_neg, user_size, pool_size)

    interests, vec, positive = route(
        renumbered,
        arrived,
        w_in,
        bias_in.reshape(1, -1),
        w_out,
        bilinear,
        onehot,
        first,
        moved,
        length,
        route_init,
        label_index.reshape(1, -1),
        label_ids.reshape(1, -1),
        label_counts.reshape(1, -1),
    )
    away = late_masks(pool_size)
    vecs = [vec]
    for mask in away:
        vecs.append(swap_pool(vec, pool_size, mask))
    sums = negative_sums(vecs, negs)
    partition = jnp.exp(positive) + sums[0]
    for mask, one in zip(away, sums[1:]):
        partition += swap_pool(one, pool_size, mask)
    user_loss = jnp.log(partition) - positive
    return (interests, user_loss.reshape(-1))


def solution(mesh):
    both = ("user", "pool")
    in_specs = (
        P(both, None),
        P(),
        P(),
        P(),
        P(),
        P(None, both, None),
        P(both, None),
        P(both),
        P(both, None, None),
        P(both),
        P(both),
        P(both),
        P(both, None),
        P(both),
        P(both),
    )
    out_specs = (P(both, None), P(both))

    def body(*args):
        return on_device(mesh.shape["user"], mesh.shape["pool"], *args)

    return jax.shard_map(body, mesh=mesh, in_specs=in_specs, out_specs=out_specs, check_vma=False)
```

```python
import functools

import jax
import jax.numpy as jnp
from jax import lax
from jax.experimental import pallas as pl
from jax.experimental.pallas import tpu as pltpu
from jax.sharding import PartitionSpec as P


INTERESTS = 4
ITERS = 3
LANES = 128
SUB = 8
EXTRA = 16
SPLIT = 4
GROUP_USERS = 8

norm_epsilon = 1e-06
attend_scale = 8.0
logit_scale = 20.0

f32 = jnp.float32
bf16 = jnp.bfloat16
i32 = jnp.int32


INSIDE = pl.BlockSpec(memory_space=pltpu.VMEM)
OUTSIDE = pl.BlockSpec(memory_space=pltpu.HBM)
PARAMS = pltpu.CompilerParams(vmem_limit_bytes=20 << 20)


def near(array):
    return pltpu.with_memory_space_constraint(array, pltpu.VMEM)


def far(array):
    return pltpu.with_memory_space_constraint(array, pltpu.HBM)


def mm(a, b):
    return jnp.dot(a, b, preferred_element_type=f32)


def mm_nt(a, b):
    return lax.dot_general(a, b, (((1,), (1,)), ((), ())), preferred_element_type=f32)


def iota(shape, axis):
    return lax.broadcasted_iota(i32, shape, axis)


def to_column(row):
    n = row.shape[1]
    eye = iota((n, n), 0) == iota((n, n), 1)
    return jnp.sum(jnp.where(eye, row, 0.0), axis=1, keepdims=True)


def to_row(column):
    n = column.shape[0]
    eye = iota((n, n), 0) == iota((n, n), 1)
    return jnp.sum(jnp.where(eye, column, 0.0), axis=0, keepdims=True)


def id_digits(ids_row):
    low = (ids_row & 255).astype(f32)
    mid = ((ids_row >> 8) & 255).astype(f32)
    high = (ids_row >> 16).astype(f32)
    return low, mid, high


def lane_columns(columns, rows):
    lane = iota((rows, LANES), 1)
    out = jnp.zeros((rows, LANES), f32)
    for at, column in enumerate(columns):
        out = jnp.where(lane == at, column, out)
    return out


def shift_of(size):
    assert size & (size - 1) == 0
    return size.bit_length() - 1


def renumber(slot, cap, user_size, pool_size):
    block = slot >> shift_of(cap)
    place = ((block & (pool_size - 1)) << shift_of(user_size)) + (block >> shift_of(pool_size))
    return (place << shift_of(cap)) + (slot & (cap - 1))


class Copies:
    def __init__(self, source, target, sems, first, count):
        size = source.shape[0] // count
        self.copies = [
            pltpu.make_async_copy(
                source.at[pl.ds(at * size, size)],
                target.at[pl.ds(at * size, size)],
                sems.at[first + at],
            )
            for at in range(count)
        ]
        for copy in self.copies:
            copy.start()

    def wait(self):
        for copy in self.copies:
            copy.wait()


def select_kernel(
    user_size,
    pool_size,
    fetch,
    rows,
    negs,
    ids,
    counts,
    out,
    packed,
    fetch_ref,
    rows_ref,
    out_ref,
    extra_ref,
    ids_ref,
    counts_ref,
    sems,
):
    table = Copies(fetch, fetch_ref, sems, 0, 1)
    small = [Copies(ids, ids_ref, sems, 1, 1), Copies(counts, counts_ref, sems, 2, 1)]
    copy = Copies(rows, rows_ref, sems, 5, SPLIT)
    kept = negs.shape[0]
    body = pltpu.make_async_copy(negs, packed.at[pl.ds(0, kept)], sems.at[3])
    body.start()
    _, cap, blocks = fetch_ref.shape
    count = blocks * cap
    row = iota((count, blocks), 0)
    start = renumber(iota((1, blocks), 1) * cap, cap, user_size, pool_size)
    pick = jnp.where((row >= start) & (row < start + cap), 1.0, 0.0).astype(bf16)
    place = iota((count, cap), 1) == (iota((count, cap), 0) & (cap - 1))
    table.wait()
    picked = fetch_ref[0]
    high = mm_nt(pick, (picked >> 7).astype(f32).astype(bf16))
    low = mm_nt(pick, (picked & 127).astype(f32).astype(bf16))
    column = jnp.sum(jnp.where(place, high * 128.0 + low, 0.0), axis=1, keepdims=True)
    item = iota((count, rows_ref.shape[0]), 1).astype(f32)
    chosen = jnp.where(item == column, 1.0, 0.0).astype(bf16)
    for one in small:
        one.wait()
    numbers = id_digits(ids_ref[...]) + (counts_ref[...].astype(f32),)
    at = iota((EXTRA, kept), 0)
    extra = jnp.zeros((EXTRA, kept), f32)
    for line, one in enumerate(numbers):
        extra = jnp.where(at == line, one, extra)
    extra_ref[...] = jnp.zeros(extra_ref.shape, bf16)
    extra_ref[:, :kept] = extra.astype(bf16)
    tail = pltpu.make_async_copy(extra_ref, packed.at[pl.ds(kept, EXTRA)], sems.at[4])
    tail.start()
    copy.wait()
    size = count // SPLIT
    for part in range(SPLIT):
        cut = slice(part * size, (part + 1) * size)
        out_ref[cut, :] = mm(chosen[cut], rows_ref[...]).astype(bf16)
        Copies(out_ref.at[pl.ds(part * size, size)], out.at[pl.ds(part * size, size)], sems, 5 + SPLIT + part, 1)
    body.wait()
    tail.wait()
    for part in range(SPLIT):
        there = pl.ds(part * size, size)
        pltpu.make_async_copy(out_ref.at[there], out.at[there], sems.at[5 + SPLIT + part]).wait()


def select_rows(user_size, pool_size, fetch, rows, negs, ids, counts):
    blocks, _, cap = fetch.shape
    packed = (negs.shape[0] + EXTRA, negs.shape[1])
    chosen = (blocks * cap, rows.shape[1])
    return pl.pallas_call(
        functools.partial(select_kernel, user_size, pool_size),
        in_specs=[OUTSIDE] * 5,
        out_specs=[OUTSIDE, OUTSIDE],
        out_shape=[jax.ShapeDtypeStruct(chosen, bf16), jax.ShapeDtypeStruct(packed, bf16)],
        scratch_shapes=[
            pltpu.VMEM((1, cap, blocks), i32),
            pltpu.VMEM(rows.shape, bf16),
            pltpu.VMEM(chosen, bf16),
            pltpu.VMEM((EXTRA, negs.shape[1]), bf16),
            pltpu.VMEM(ids.shape, i32),
            pltpu.VMEM(counts.shape, i32),
            pltpu.SemaphoreType.DMA((5 + 2 * SPLIT,)),
        ],
        compiler_params=PARAMS,
        name="select_rows",
    )(*[far(one) for one in (fetch.transpose(1, 2, 0), rows, negs, ids, counts)])


def tower(rows_ref, w_in_ref, bias, w_out, bias_ref, out_ref, sems):
    small = Copies(bias, bias_ref, sems, 0, 1)
    large = Copies(w_out, out_ref, sems, 1, SPLIT)
    hidden = mm(rows_ref[...], w_in_ref[...])
    small.wait()
    hidden = jnp.maximum(hidden + bias_ref[...], 0.0).astype(bf16)
    large.wait()
    embedding = mm(hidden, out_ref[...])
    total = jnp.sum(embedding * embedding, axis=1, keepdims=True)
    return embedding * lax.rsqrt(total + norm_epsilon)


def neg_kernel(
    own_ref, apart_ref, w_in_ref, bias, w_out, out_ref, rows_ref, bias_ref, w_out_ref, sems
):
    count = rows_ref.shape[0] // 2
    rows_ref[:count, :] = own_ref[:count, :]
    rows_ref[count:, :] = apart_ref[:count, :]
    unit = tower(rows_ref, w_in_ref, bias, w_out, bias_ref, w_out_ref, sems)
    width = unit.shape[1]
    out_ref[:width, :] = unit.T.astype(bf16)
    out_ref[width:, :count] = own_ref[count:, :count]
    out_ref[width:, count:] = apart_ref[count:, :count]


def neg_tower(own, apart, w_in, bias, w_out):
    count = own.shape[0] - EXTRA
    width = own.shape[1]
    return pl.pallas_call(
        neg_kernel,
        in_specs=[INSIDE, INSIDE, INSIDE, OUTSIDE, OUTSIDE],
        out_shape=pltpu.HBM((width + EXTRA, 2 * count), bf16),
        scratch_shapes=[
            pltpu.VMEM((2 * count, width), bf16),
            pltpu.VMEM(bias.shape, f32),
            pltpu.VMEM(w_out.shape, bf16),
            pltpu.SemaphoreType.DMA((1 + SPLIT,)),
        ],
        compiler_params=PARAMS,
        name="neg_tower",
    )(near(own), near(apart), near(w_in), far(bias), far(w_out))


def event_weights(logits, live):
    raised = [jnp.exp(one) for one in logits]
    total = functools.reduce(jnp.add, raised)
    return [(one / total * live).astype(bf16).astype(f32) for one in raised]


def scatter_weights(weights, upper, onehot_ref, slot_ref):
    users = weights[0].shape[0]
    pages = slot_ref.shape[1] // LANES
    count = pages * INTERESTS * SUB
    for group in range(users // GROUP_USERS):
        at = slice(group * GROUP_USERS, (group + 1) * GROUP_USERS)
        base = jnp.concatenate(
            [
                jnp.where(upper[at] == page, weights[k][at], 0.0)
                for page in range(pages)
                for k in range(INTERESTS)
            ],
            axis=0,
        )
        user = iota((count, 1), 0) & (GROUP_USERS - 1)
        left = jnp.concatenate(
            [
                jnp.where((user >> 1) == pair, base, 0.0).astype(bf16)
                for pair in range(GROUP_USERS // 2)
            ],
            axis=1,
        )
        both = mm(left, onehot_ref[group])
        own = jnp.where((user & 1) == 0, both[:, :LANES], both[:, LANES:])
        for page in range(pages):
            for k in range(INTERESTS):
                source = (page * INTERESTS + k) * SUB
                target = k * users + group * GROUP_USERS
                slot_ref[target : target + SUB, page * LANES : (page + 1) * LANES] = own[
                    source : source + SUB
                ]


def live_mask(length_ref, shape):
    length = to_column(length_ref[...].astype(f32))
    return jnp.where(iota(shape, 1).astype(f32) < length, 1.0, 0.0)


def prepare_kernel(
    renumbered,
    index,
    length,
    init,
    w_in,
    onehot,
    slots,
    moved,
    w_in_ref,
    index_ref,
    length_ref,
    init_ref,
    onehot_ref,
    slot_ref,
    moved_ref,
    sems,
):
    pairs = ((index, index_ref), (length, length_ref), (init, init_ref))
    copies = [Copies(*pair, sems, at, 1) for at, pair in enumerate(pairs)]
    users, events = index_ref.shape
    groups = users // GROUP_USERS
    weight = Copies(w_in, w_in_ref, sems, 5 + groups, SPLIT)
    copies[0].wait()
    index = renumbered(index_ref[...])
    moved_ref[...] = index
    back = [Copies(moved_ref, moved, sems, 3, 1)]
    upper = index >> 7
    lower = (index & (LANES - 1)).astype(f32).T
    lane_id = iota((events, LANES), 1).astype(f32)
    for group in range(groups):
        for within in range(GROUP_USERS):
            user = group * GROUP_USERS + within
            pair, side = divmod(within, 2)
            hit = jnp.where(lane_id == lower[:, user : user + 1], 1.0, 0.0).astype(bf16)
            onehot_ref[
                group, pair * events : (pair + 1) * events, side * LANES : (side + 1) * LANES
            ] = hit
        there = pl.ds(group, 1)
        back.append(Copies(onehot_ref.at[there], onehot.at[there], sems, 5 + group, 1))
    for one in copies[1:]:
        one.wait()
    live = live_mask(length_ref, index.shape)
    weights = event_weights([init_ref[:, k, :] for k in range(INTERESTS)], live)
    scatter_weights(weights, upper, onehot_ref, slot_ref)
    back.append(Copies(slot_ref, slots, sems, 4, 1))
    back.append(weight)
    for one in back:
        one.wait()


def prepare(renumbered, index, length, init, w_in, slots):
    users, events = index.shape
    groups = users // GROUP_USERS
    onehot = (groups, GROUP_USERS // 2 * events, 2 * LANES)
    first = (INTERESTS * users, slots)
    return pl.pallas_call(
        functools.partial(prepare_kernel, renumbered),
        in_specs=[OUTSIDE] * 4,
        out_specs=[OUTSIDE] * 3 + [INSIDE],
        out_shape=[
            pltpu.HBM(onehot, bf16),
            pltpu.HBM(first, f32),
            pltpu.HBM(index.shape, i32),
            pltpu.VMEM(w_in.shape, bf16),
        ],
        scratch_shapes=[
            pltpu.VMEM(index.shape, i32),
            pltpu.VMEM(length.shape, i32),
            pltpu.VMEM(init.shape, f32),
            pltpu.VMEM(onehot, bf16),
            pltpu.VMEM(first, f32),
            pltpu.VMEM(index.shape, i32),
            pltpu.SemaphoreType.DMA((5 + groups + SPLIT,)),
        ],
        compiler_params=PARAMS,
        name="prepare",
    )(far(index), far(length), far(init), far(w_in))


def route_kernel(
    renumbered,
    rows_ref,
    w_in_ref,
    bias,
    w_out,
    bilinear,
    onehot,
    first,
    index,
    length,
    init,
    label,
    ids,
    counts,
    held,
    interests_ref,
    vec_ref,
    positive_ref,
    held_ref,
    bias_ref,
    out_ref,
    map_ref,
    onehot_ref,
    first_ref,
    index_ref,
    length_ref,
    init_ref,
    label_ref,
    ids_ref,
    counts_ref,
    slot_ref,
    sems,
):
    pairs = (
        (bilinear, map_ref),
        (first, first_ref),
        (index, index_ref),
        (length, length_ref),
        (init, init_ref),
        (label, label_ref),
        (ids, ids_ref),
        (counts, counts_ref),
    )
    start = 1 + SPLIT
    others = [Copies(*pair, sems, start + at, 1) for at, pair in enumerate(pairs)]
    unit = tower(rows_ref, w_in_ref, bias, w_out, bias_ref, out_ref, sems).astype(bf16)
    fetch = Copies(onehot, onehot_ref, sems, start + len(pairs), onehot.shape[0])
    keep = Copies(held, held_ref, sems, start + len(pairs) + onehot.shape[0], 1)
    for other in others:
        other.wait()
    mapped = mm(unit, map_ref[...]).astype(bf16)
    users, events = index_ref.shape
    slots, width = mapped.shape
    index = index_ref[...]
    upper = index >> 7
    lower = index & (LANES - 1)
    live = live_mask(length_ref, index.shape)
    logits = [init_ref[:, k, :] for k in range(INTERESTS)]
    capsules = label_rows = None
    for iteration in range(ITERS):
        if iteration == 1:
            fetch.wait()
        if iteration:
            scatter_weights(event_weights(logits, live), upper, onehot_ref, slot_ref)
        slot_weights = first_ref[...] if iteration == 0 else slot_ref[...]
        coarse = slot_weights.astype(bf16)
        rest = (slot_weights - coarse.astype(f32)).astype(bf16)
        sums = mm(coarse, mapped) + mm(rest, mapped)
        norm_sq = jnp.sum(sums * sums, axis=1, keepdims=True)
        capsules = sums * (jnp.sqrt(norm_sq) / (1.0 + norm_sq))
        if iteration + 1 < ITERS:
            scores = mm_nt(capsules.astype(bf16), mapped)
            if iteration == 0:
                label = to_column(renumbered(label_ref[...]).astype(f32))
                chosen = jnp.where(iota((users, slots), 1).astype(f32) == label, 1.0, 0.0)
                label_rows = mm(chosen.astype(bf16), unit)
            found = [[None] * (events // LANES) for _ in range(INTERESTS)]
            for part in range(events // LANES):
                rows = [[] for _ in range(INTERESTS)]
                for user in range(0, users, SUB):
                    low = lower[user : user + SUB, part * LANES : (part + 1) * LANES]
                    high = upper[user : user + SUB, part * LANES : (part + 1) * LANES]
                    for k in range(INTERESTS):
                        one = None
                        for page in range(slots // LANES):
                            piece = scores[
                                k * users + user : k * users + user + SUB,
                                page * LANES : (page + 1) * LANES,
                            ]
                            taken = jnp.take_along_axis(
                                piece, low, axis=1, mode="promise_in_bounds"
                            )
                            one = taken if one is None else jnp.where(high == page, taken, one)
                        rows[k].append(one)
                for k in range(INTERESTS):
                    found[k][part] = jnp.concatenate(rows[k], axis=0)
            for k in range(INTERESTS):
                logits[k] = logits[k] + jnp.concatenate(found[k], axis=1)
    each = [capsules[k * users : (k + 1) * users] for k in range(INTERESTS)]
    for k in range(INTERESTS):
        interests_ref[:, k * width : (k + 1) * width] = each[k]
    raised = [
        jnp.exp(attend_scale * jnp.sum(one * label_rows, axis=1, keepdims=True)) for one in each
    ]
    total = functools.reduce(jnp.add, raised)
    user_vec = functools.reduce(jnp.add, [(r / total) * one for r, one in zip(raised, each)])
    user_vec = user_vec.astype(bf16)
    vec_ref[:, :width] = user_vec
    vec_ref[:, width:] = lane_columns([to_column(one) for one in id_digits(ids_ref[...])], users).astype(bf16)
    match = jnp.sum(user_vec.astype(f32) * label_rows, axis=1, keepdims=True)
    positive_ref[...] = logit_scale * to_row(match) - jnp.log(counts_ref[...].astype(f32))
    keep.wait()


def route(renumbered, rows, w_in, *others):
    bias, w_out, bilinear, onehot, first, index, *_, held = others
    users = index.shape[0]
    width = bilinear.shape[1]
    return pl.pallas_call(
        functools.partial(route_kernel, renumbered),
        in_specs=[INSIDE] * 2 + [OUTSIDE] * len(others),
        out_shape=[
            pltpu.VMEM((users, INTERESTS * width), f32),
            pltpu.VMEM((users, width + LANES), bf16),
            pltpu.VMEM((1, users), f32),
            pltpu.VMEM(held.shape, held.dtype),
        ],
        scratch_shapes=[pltpu.VMEM(one.shape, one.dtype) for one in others[:-1]]
        + [
            pltpu.VMEM(first.shape, f32),
            pltpu.SemaphoreType.DMA((SPLIT + len(others) - 1 + onehot.shape[0],)),
        ],
        compiler_params=PARAMS,
        name="route",
    )(near(rows), near(w_in), *[far(one) for one in others])


def sums_kernel(parts, pieces, *refs):
    vec_refs = refs[:parts]
    neg_refs = refs[parts : parts + pieces]
    out_refs = refs[parts + pieces :]
    vec = jnp.concatenate([ref[...] for ref in vec_refs], axis=0)
    users = vec_refs[0].shape[0]
    width = vec.shape[1] - LANES
    digits = vec[:, width:].astype(f32)
    label_ids = digits[:, 0:1] + 256.0 * digits[:, 1:2] + 65536.0 * digits[:, 2:3]
    vec = vec[:, :width]
    total = None
    for ref in neg_refs:
        extra = ref[width:, :].astype(f32)
        ids = extra[0:1] + 256.0 * extra[1:2] + 65536.0 * extra[2:3]
        terms = jnp.exp(logit_scale * mm(vec, ref[:width, :])) * (1.0 / extra[3:4])
        terms = jnp.where(ids != label_ids, terms, 0.0)
        total = terms if total is None else total + terms
    total = to_row(jnp.sum(total, axis=1, keepdims=True))
    for part, ref in enumerate(out_refs):
        ref[...] = total[:, part * users : (part + 1) * users]


def negative_sums(vecs, negs):
    users = vecs[0].shape[0]
    return pl.pallas_call(
        functools.partial(sums_kernel, len(vecs), len(negs)),
        out_shape=[pltpu.VMEM((1, users), f32) for _ in vecs],
        compiler_params=PARAMS,
        name="negative_sums",
    )(*[near(one) for one in [*vecs, *negs]])


def swap_pool(array, size, bit):
    return lax.ppermute(array, "pool", [(at, at ^ bit) for at in range(size)])


def late_masks(pool_size):
    return range(2, pool_size // 2, 2)


def swap_user(array, size, mask):
    return lax.ppermute(array, "user", [(at, at ^ mask) for at in range(size)])


def swap_both(array, user_size, pool_size, user_mask, pool_mask):
    perm = [
        (user * pool_size + pool, (user ^ user_mask) * pool_size + (pool ^ pool_mask))
        for user in range(user_size)
        for pool in range(pool_size)
    ]
    return lax.ppermute(array, ("user", "pool"), perm)


def piece_masks(user_size):
    masks = [(user, pool) for user in range(0, user_size, 2) for pool in (0, 1)]
    return masks[:0:-1]


def gather_negatives(own, user_size, pool_size):
    pieces = [own]
    for user, pool in piece_masks(user_size):
        pieces.append(swap_both(own, user_size, pool_size, user, pool))
    others = []
    for piece in pieces:
        others.append(swap_user(piece, user_size, 1))
    return pieces + others


def on_device(
    user_size,
    pool_size,
    item_feats,
    w_in,
    bias_in,
    w_out,
    bilinear,
    fetch_table,
    hist_index,
    hist_len,
    route_init,
    label_index,
    label_ids,
    label_counts,
    neg_feats,
    neg_ids,
    neg_counts,
):
    outgoing, packed = select_rows(
        user_size, pool_size, fetch_table, item_feats, neg_feats, neg_ids.reshape(1, -1), neg_counts.reshape(1, -1)
    )
    apart = swap_pool(packed, pool_size, pool_size // 2)
    arrived = lax.all_to_all(
        outgoing.reshape(fetch_table.shape[0], fetch_table.shape[2], -1),
        ("pool", "user"),
        split_axis=0,
        concat_axis=0,
        tiled=True,
    )
    arrived = arrived.reshape(outgoing.shape)

    length = hist_len.reshape(1, -1)
    renumbered = functools.partial(
        renumber, cap=fetch_table.shape[2], user_size=user_size, pool_size=pool_size
    )
    onehot, first, moved, w_in = prepare(
        renumbered, hist_index, length, route_init, w_in, outgoing.shape[0]
    )
    own_neg = neg_tower(packed, apart, w_in, bias_in.reshape(1, -1), w_out)
    negs = gather_negatives(own_neg, user_size, pool_size)

    interests, vec, positive, negs[len(negs) // 2] = route(
        renumbered,
        arrived,
        w_in,
        bias_in.reshape(1, -1),
        w_out,
        bilinear,
        onehot,
        first,
        moved,
        length,
        route_init,
        label_index.reshape(1, -1),
        label_ids.reshape(1, -1),
        label_counts.reshape(1, -1),
        negs[len(negs) // 2],
    )
    away = late_masks(pool_size)
    vecs = [vec]
    for mask in away:
        vecs.append(swap_pool(vec, pool_size, mask))
    sums = negative_sums(vecs, negs)
    partition = jnp.exp(positive) + sums[0]
    for mask, one in zip(away, sums[1:]):
        partition += swap_pool(one, pool_size, mask)
    user_loss = jnp.log(partition) - positive
    return (interests, user_loss.reshape(-1))


def solution(mesh):
    both = ("user", "pool")
    in_specs = (
        P(both, None),
        P(),
        P(),
        P(),
        P(),
        P(None, both, None),
        P(both, None),
        P(both),
        P(both, None, None),
        P(both),
        P(both),
        P(both),
        P(both, None),
        P(both),
        P(both),
    )
    out_specs = (P(both, None), P(both))

    def body(*args):
        return on_device(mesh.shape["user"], mesh.shape["pool"], *args)

    return jax.shard_map(body, mesh=mesh, in_specs=in_specs, out_specs=out_specs, check_vma=False)
```

```python
import functools

import jax
import jax.numpy as jnp
from jax import lax
from jax.experimental import pallas as pl
from jax.experimental.pallas import tpu as pltpu
from jax.sharding import PartitionSpec as P


INTERESTS = 4
ITERS = 3
LANES = 128
SUB = 8
EXTRA = 16
SPLIT = 4
GROUP_USERS = 8

norm_epsilon = 1e-06
attend_scale = 8.0
logit_scale = 20.0

f32 = jnp.float32
bf16 = jnp.bfloat16
i32 = jnp.int32


INSIDE = pl.BlockSpec(memory_space=pltpu.VMEM)
OUTSIDE = pl.BlockSpec(memory_space=pltpu.HBM)
PARAMS = pltpu.CompilerParams(vmem_limit_bytes=20 << 20)


def near(array):
    return pltpu.with_memory_space_constraint(array, pltpu.VMEM)


def far(array):
    return pltpu.with_memory_space_constraint(array, pltpu.HBM)


def mm(a, b):
    return jnp.dot(a, b, preferred_element_type=f32)


def mm_nt(a, b):
    return lax.dot_general(a, b, (((1,), (1,)), ((), ())), preferred_element_type=f32)


def iota(shape, axis):
    return lax.broadcasted_iota(i32, shape, axis)


def to_column(row):
    n = row.shape[1]
    eye = iota((n, n), 0) == iota((n, n), 1)
    return jnp.sum(jnp.where(eye, row, 0.0), axis=1, keepdims=True)


def to_row(column):
    n = column.shape[0]
    eye = iota((n, n), 0) == iota((n, n), 1)
    return jnp.sum(jnp.where(eye, column, 0.0), axis=0, keepdims=True)


def id_digits(ids_row):
    low = (ids_row & 255).astype(f32)
    mid = ((ids_row >> 8) & 255).astype(f32)
    high = (ids_row >> 16).astype(f32)
    return low, mid, high


def lane_columns(columns, rows):
    lane = iota((rows, LANES), 1)
    out = jnp.zeros((rows, LANES), f32)
    for at, column in enumerate(columns):
        out = jnp.where(lane == at, column, out)
    return out


def shift_of(size):
    assert size & (size - 1) == 0
    return size.bit_length() - 1


def renumber(slot, cap, user_size, pool_size):
    block = slot >> shift_of(cap)
    place = ((block & (pool_size - 1)) << shift_of(user_size)) + (block >> shift_of(pool_size))
    return (place << shift_of(cap)) + (slot & (cap - 1))


class Copies:
    def __init__(self, source, target, sems, first, count):
        size = source.shape[0] // count
        self.copies = [
            pltpu.make_async_copy(
                source.at[pl.ds(at * size, size)],
                target.at[pl.ds(at * size, size)],
                sems.at[first + at],
            )
            for at in range(count)
        ]
        for copy in self.copies:
            copy.start()

    def wait(self):
        for copy in self.copies:
            copy.wait()


def select_kernel(
    user_size,
    pool_size,
    fetch,
    rows,
    negs,
    ids,
    counts,
    out,
    packed,
    fetch_ref,
    rows_ref,
    out_ref,
    extra_ref,
    ids_ref,
    counts_ref,
    sems,
):
    table = Copies(fetch, fetch_ref, sems, 0, 1)
    small = [Copies(ids, ids_ref, sems, 1, 1), Copies(counts, counts_ref, sems, 2, 1)]
    copy = Copies(rows, rows_ref, sems, 5, SPLIT)
    kept = negs.shape[0]
    body = pltpu.make_async_copy(negs, packed.at[pl.ds(0, kept)], sems.at[3])
    body.start()
    _, cap, blocks = fetch_ref.shape
    count = blocks * cap
    row = iota((count, blocks), 0)
    start = renumber(iota((1, blocks), 1) * cap, cap, user_size, pool_size)
    pick = jnp.where((row >= start) & (row < start + cap), 1.0, 0.0).astype(bf16)
    place = iota((count, cap), 1) == (iota((count, cap), 0) & (cap - 1))
    table.wait()
    picked = fetch_ref[0]
    high = mm_nt(pick, (picked >> 7).astype(f32).astype(bf16))
    low = mm_nt(pick, (picked & 127).astype(f32).astype(bf16))
    column = jnp.sum(jnp.where(place, high * 128.0 + low, 0.0), axis=1, keepdims=True)
    item = iota((count, rows_ref.shape[0]), 1).astype(f32)
    chosen = jnp.where(item == column, 1.0, 0.0).astype(bf16)
    for one in small:
        one.wait()
    numbers = id_digits(ids_ref[...]) + (counts_ref[...].astype(f32),)
    at = iota((EXTRA, kept), 0)
    extra = jnp.zeros((EXTRA, kept), f32)
    for line, one in enumerate(numbers):
        extra = jnp.where(at == line, one, extra)
    extra_ref[...] = jnp.zeros(extra_ref.shape, bf16)
    extra_ref[:, :kept] = extra.astype(bf16)
    tail = pltpu.make_async_copy(extra_ref, packed.at[pl.ds(kept, EXTRA)], sems.at[4])
    tail.start()
    copy.wait()
    size = count // SPLIT
    for part in range(SPLIT):
        cut = slice(part * size, (part + 1) * size)
        out_ref[cut, :] = mm(chosen[cut], rows_ref[...]).astype(bf16)
        Copies(out_ref.at[pl.ds(part * size, size)], out.at[pl.ds(part * size, size)], sems, 5 + SPLIT + part, 1)
    body.wait()
    tail.wait()
    for part in range(SPLIT):
        there = pl.ds(part * size, size)
        pltpu.make_async_copy(out_ref.at[there], out.at[there], sems.at[5 + SPLIT + part]).wait()


def select_rows(user_size, pool_size, fetch, rows, negs, ids, counts):
    blocks, _, cap = fetch.shape
    packed = (negs.shape[0] + EXTRA, negs.shape[1])
    chosen = (blocks * cap, rows.shape[1])
    return pl.pallas_call(
        functools.partial(select_kernel, user_size, pool_size),
        in_specs=[OUTSIDE] * 5,
        out_specs=[OUTSIDE, OUTSIDE],
        out_shape=[jax.ShapeDtypeStruct(chosen, bf16), jax.ShapeDtypeStruct(packed, bf16)],
        scratch_shapes=[
            pltpu.VMEM((1, cap, blocks), i32),
            pltpu.VMEM(rows.shape, bf16),
            pltpu.VMEM(chosen, bf16),
            pltpu.VMEM((EXTRA, negs.shape[1]), bf16),
            pltpu.VMEM(ids.shape, i32),
            pltpu.VMEM(counts.shape, i32),
            pltpu.SemaphoreType.DMA((5 + 2 * SPLIT,)),
        ],
        compiler_params=PARAMS,
        name="select_rows",
    )(*[far(one) for one in (fetch.transpose(1, 2, 0), rows, negs, ids, counts)])


def tower(rows_ref, w_in_ref, bias, w_out, bias_ref, out_ref, sems):
    small = Copies(bias, bias_ref, sems, 0, 1)
    large = Copies(w_out, out_ref, sems, 1, SPLIT)
    hidden = mm(rows_ref[...], w_in_ref[...])
    small.wait()
    hidden = jnp.maximum(hidden + bias_ref[...], 0.0).astype(bf16)
    large.wait()
    embedding = mm(hidden, out_ref[...])
    total = jnp.sum(embedding * embedding, axis=1, keepdims=True)
    return embedding * lax.rsqrt(total + norm_epsilon)


def neg_kernel(
    own_ref, apart_ref, w_in_ref, bias, w_out, out_ref, rows_ref, bias_ref, w_out_ref, sems
):
    count = rows_ref.shape[0] // 2
    rows_ref[:count, :] = own_ref[:count, :]
    rows_ref[count:, :] = apart_ref[:count, :]
    unit = tower(rows_ref, w_in_ref, bias, w_out, bias_ref, w_out_ref, sems)
    width = unit.shape[1]
    out_ref[:width, :] = unit.T.astype(bf16)
    out_ref[width:, :count] = own_ref[count:, :count]
    out_ref[width:, count:] = apart_ref[count:, :count]


def neg_tower(own, apart, w_in, bias, w_out):
    count = own.shape[0] - EXTRA
    width = own.shape[1]
    return pl.pallas_call(
        neg_kernel,
        in_specs=[INSIDE, INSIDE, INSIDE, OUTSIDE, OUTSIDE],
        out_shape=pltpu.HBM((width + EXTRA, 2 * count), bf16),
        scratch_shapes=[
            pltpu.VMEM((2 * count, width), bf16),
            pltpu.VMEM(bias.shape, f32),
            pltpu.VMEM(w_out.shape, bf16),
            pltpu.SemaphoreType.DMA((1 + SPLIT,)),
        ],
        compiler_params=PARAMS,
        name="neg_tower",
    )(near(own), near(apart), near(w_in), far(bias), far(w_out))


def event_weights(logits, live):
    raised = [jnp.exp(one) for one in logits]
    total = functools.reduce(jnp.add, raised)
    return [(one / total * live).astype(bf16).astype(f32) for one in raised]


def scatter_weights(weights, upper, onehot_ref, slot_ref):
    users = weights[0].shape[0]
    pages = slot_ref.shape[1] // LANES
    count = pages * INTERESTS * SUB
    for group in range(users // GROUP_USERS):
        at = slice(group * GROUP_USERS, (group + 1) * GROUP_USERS)
        base = jnp.concatenate(
            [
                jnp.where(upper[at] == page, weights[k][at], 0.0)
                for page in range(pages)
                for k in range(INTERESTS)
            ],
            axis=0,
        )
        user = iota((count, 1), 0) & (GROUP_USERS - 1)
        left = jnp.concatenate(
            [
                jnp.where((user >> 1) == pair, base, 0.0).astype(bf16)
                for pair in range(GROUP_USERS // 2)
            ],
            axis=1,
        )
        both = mm(left, onehot_ref[group])
        own = jnp.where((user & 1) == 0, both[:, :LANES], both[:, LANES:])
        for page in range(pages):
            for k in range(INTERESTS):
                source = (page * INTERESTS + k) * SUB
                target = k * users + group * GROUP_USERS
                slot_ref[target : target + SUB, page * LANES : (page + 1) * LANES] = own[
                    source : source + SUB
                ]


def live_mask(length_ref, shape):
    length = to_column(length_ref[...].astype(f32))
    return jnp.where(iota(shape, 1).astype(f32) < length, 1.0, 0.0)


def prepare_kernel(
    renumbered,
    index,
    length,
    init,
    w_in,
    onehot,
    slots,
    moved,
    w_in_ref,
    index_ref,
    length_ref,
    init_ref,
    onehot_ref,
    slot_ref,
    moved_ref,
    sems,
):
    pairs = ((index, index_ref), (length, length_ref), (init, init_ref))
    copies = [Copies(*pair, sems, at, 1) for at, pair in enumerate(pairs)]
    users, events = index_ref.shape
    groups = users // GROUP_USERS
    weight = Copies(w_in, w_in_ref, sems, 5 + groups, SPLIT)
    copies[0].wait()
    index = renumbered(index_ref[...])
    moved_ref[...] = index
    back = [Copies(moved_ref, moved, sems, 3, 1)]
    upper = index >> 7
    lower = (index & (LANES - 1)).astype(f32).T
    lane_id = iota((events, LANES), 1).astype(f32)
    for group in range(groups):
        for within in range(GROUP_USERS):
            user = group * GROUP_USERS + within
            pair, side = divmod(within, 2)
            hit = jnp.where(lane_id == lower[:, user : user + 1], 1.0, 0.0).astype(bf16)
            onehot_ref[
                group, pair * events : (pair + 1) * events, side * LANES : (side + 1) * LANES
            ] = hit
        there = pl.ds(group, 1)
        back.append(Copies(onehot_ref.at[there], onehot.at[there], sems, 5 + group, 1))
    for one in copies[1:]:
        one.wait()
    live = live_mask(length_ref, index.shape)
    weights = event_weights([init_ref[:, k, :] for k in range(INTERESTS)], live)
    scatter_weights(weights, upper, onehot_ref, slot_ref)
    back.append(Copies(slot_ref, slots, sems, 4, 1))
    back.append(weight)
    for one in back:
        one.wait()


def prepare(renumbered, index, length, init, w_in, slots):
    users, events = index.shape
    groups = users // GROUP_USERS
    onehot = (groups, GROUP_USERS // 2 * events, 2 * LANES)
    first = (INTERESTS * users, slots)
    return pl.pallas_call(
        functools.partial(prepare_kernel, renumbered),
        in_specs=[OUTSIDE] * 4,
        out_specs=[OUTSIDE] * 3 + [INSIDE],
        out_shape=[
            pltpu.HBM(onehot, bf16),
            pltpu.HBM(first, f32),
            pltpu.HBM(index.shape, i32),
            pltpu.VMEM(w_in.shape, bf16),
        ],
        scratch_shapes=[
            pltpu.VMEM(index.shape, i32),
            pltpu.VMEM(length.shape, i32),
            pltpu.VMEM(init.shape, f32),
            pltpu.VMEM(onehot, bf16),
            pltpu.VMEM(first, f32),
            pltpu.VMEM(index.shape, i32),
            pltpu.SemaphoreType.DMA((5 + groups + SPLIT,)),
        ],
        compiler_params=PARAMS,
        name="prepare",
    )(far(index), far(length), far(init), far(w_in))


def route_kernel(
    renumbered,
    rows_ref,
    w_in_ref,
    bias,
    w_out,
    bilinear,
    onehot,
    first,
    index,
    length,
    init,
    label,
    ids,
    counts,
    held,
    interests_ref,
    vec_ref,
    positive_ref,
    held_ref,
    bias_ref,
    out_ref,
    map_ref,
    onehot_ref,
    first_ref,
    index_ref,
    length_ref,
    init_ref,
    label_ref,
    ids_ref,
    counts_ref,
    slot_ref,
    sems,
):
    pairs = (
        (bilinear, map_ref),
        (first, first_ref),
        (index, index_ref),
        (length, length_ref),
        (init, init_ref),
        (label, label_ref),
        (ids, ids_ref),
        (counts, counts_ref),
    )
    start = 1 + SPLIT
    others = [Copies(*pair, sems, start + at, 1) for at, pair in enumerate(pairs)]
    unit = tower(rows_ref, w_in_ref, bias, w_out, bias_ref, out_ref, sems).astype(bf16)
    fetch = Copies(onehot, onehot_ref, sems, start + len(pairs), onehot.shape[0])
    keep = Copies(held, held_ref, sems, start + len(pairs) + onehot.shape[0], 1)
    for other in others:
        other.wait()
    mapped = mm(unit, map_ref[...]).astype(bf16)
    users, events = index_ref.shape
    slots, width = mapped.shape
    index = index_ref[...]
    upper = index >> 7
    lower = index & (LANES - 1)
    live = live_mask(length_ref, index.shape)
    logits = [init_ref[:, k, :] for k in range(INTERESTS)]
    capsules = None
    for iteration in range(ITERS):
        if iteration == 1:
            fetch.wait()
        if iteration:
            scatter_weights(event_weights(logits, live), upper, onehot_ref, slot_ref)
        slot_weights = first_ref[...] if iteration == 0 else slot_ref[...]
        coarse = slot_weights.astype(bf16)
        rest = (slot_weights - coarse.astype(f32)).astype(bf16)
        sums = mm(coarse, mapped) + mm(rest, mapped)
        norm_sq = jnp.sum(sums * sums, axis=1, keepdims=True)
        capsules = sums * (jnp.sqrt(norm_sq) / (1.0 + norm_sq))
        if iteration + 1 < ITERS:
            scores = mm_nt(capsules.astype(bf16), mapped)
            found = [[None] * (events // LANES) for _ in range(INTERESTS)]
            for part in range(events // LANES):
                rows = [[] for _ in range(INTERESTS)]
                for user in range(0, users, SUB):
                    low = lower[user : user + SUB, part * LANES : (part + 1) * LANES]
                    high = upper[user : user + SUB, part * LANES : (part + 1) * LANES]
                    for k in range(INTERESTS):
                        one = None
                        for page in range(slots // LANES):
                            piece = scores[
                                k * users + user : k * users + user + SUB,
                                page * LANES : (page + 1) * LANES,
                            ]
                            taken = jnp.take_along_axis(
                                piece, low, axis=1, mode="promise_in_bounds"
                            )
                            one = taken if one is None else jnp.where(high == page, taken, one)
                        rows[k].append(one)
                for k in range(INTERESTS):
                    found[k][part] = jnp.concatenate(rows[k], axis=0)
            for k in range(INTERESTS):
                logits[k] = logits[k] + jnp.concatenate(found[k], axis=1)
    each = [capsules[k * users : (k + 1) * users] for k in range(INTERESTS)]
    for k in range(INTERESTS):
        interests_ref[:, k * width : (k + 1) * width] = each[k]
    label = to_column(renumbered(label_ref[...]).astype(f32))
    chosen = jnp.where(iota((users, slots), 1).astype(f32) == label, 1.0, 0.0).astype(bf16)
    label_rows = mm(chosen, unit)
    raised = [
        jnp.exp(attend_scale * jnp.sum(one * label_rows, axis=1, keepdims=True)) for one in each
    ]
    total = functools.reduce(jnp.add, raised)
    user_vec = functools.reduce(jnp.add, [(r / total) * one for r, one in zip(raised, each)])
    user_vec = user_vec.astype(bf16)
    vec_ref[:, :width] = user_vec
    vec_ref[:, width:] = lane_columns([to_column(one) for one in id_digits(ids_ref[...])], users).astype(bf16)
    match = jnp.sum(user_vec.astype(f32) * label_rows, axis=1, keepdims=True)
    positive_ref[...] = logit_scale * to_row(match) - jnp.log(counts_ref[...].astype(f32))
    keep.wait()


def route(renumbered, rows, w_in, *others):
    bias, w_out, bilinear, onehot, first, index, *_, held = others
    users = index.shape[0]
    width = bilinear.shape[1]
    return pl.pallas_call(
        functools.partial(route_kernel, renumbered),
        in_specs=[INSIDE] * 2 + [OUTSIDE] * len(others),
        out_shape=[
            pltpu.VMEM((users, INTERESTS * width), f32),
            pltpu.VMEM((users, width + LANES), bf16),
            pltpu.VMEM((1, users), f32),
            pltpu.VMEM(held.shape, held.dtype),
        ],
        scratch_shapes=[pltpu.VMEM(one.shape, one.dtype) for one in others[:-1]]
        + [
            pltpu.VMEM(first.shape, f32),
            pltpu.SemaphoreType.DMA((SPLIT + len(others) - 1 + onehot.shape[0],)),
        ],
        compiler_params=PARAMS,
        name="route",
    )(near(rows), near(w_in), *[far(one) for one in others])


def sums_kernel(parts, pieces, *refs):
    vec_refs = refs[:parts]
    neg_refs = refs[parts : parts + pieces]
    out_refs = refs[parts + pieces :]
    vec = jnp.concatenate([ref[...] for ref in vec_refs], axis=0)
    users = vec_refs[0].shape[0]
    width = vec.shape[1] - LANES
    digits = vec[:, width:].astype(f32)
    label_ids = digits[:, 0:1] + 256.0 * digits[:, 1:2] + 65536.0 * digits[:, 2:3]
    vec = vec[:, :width]
    total = None
    for ref in neg_refs:
        extra = ref[width:, :].astype(f32)
        ids = extra[0:1] + 256.0 * extra[1:2] + 65536.0 * extra[2:3]
        terms = jnp.exp(logit_scale * mm(vec, ref[:width, :])) * (1.0 / extra[3:4])
        terms = jnp.where(ids != label_ids, terms, 0.0)
        total = terms if total is None else total + terms
    total = to_row(jnp.sum(total, axis=1, keepdims=True))
    for part, ref in enumerate(out_refs):
        ref[...] = total[:, part * users : (part + 1) * users]


def negative_sums(vecs, negs):
    users = vecs[0].shape[0]
    return pl.pallas_call(
        functools.partial(sums_kernel, len(vecs), len(negs)),
        out_shape=[pltpu.VMEM((1, users), f32) for _ in vecs],
        compiler_params=PARAMS,
        name="negative_sums",
    )(*[near(one) for one in [*vecs, *negs]])


def swap_pool(array, size, bit):
    return lax.ppermute(array, "pool", [(at, at ^ bit) for at in range(size)])


def late_masks(pool_size):
    return range(2, pool_size // 2, 2)


def swap_user(array, size, mask):
    return lax.ppermute(array, "user", [(at, at ^ mask) for at in range(size)])


def swap_both(array, user_size, pool_size, user_mask, pool_mask):
    perm = [
        (user * pool_size + pool, (user ^ user_mask) * pool_size + (pool ^ pool_mask))
        for user in range(user_size)
        for pool in range(pool_size)
    ]
    return lax.ppermute(array, ("user", "pool"), perm)


def piece_masks(user_size):
    masks = [(user, pool) for user in range(0, user_size, 2) for pool in (0, 1)]
    return masks[:0:-1]


def gather_negatives(own, user_size, pool_size):
    pieces = [own]
    for user, pool in piece_masks(user_size):
        pieces.append(swap_both(own, user_size, pool_size, user, pool))
    others = []
    for piece in pieces:
        others.append(swap_user(piece, user_size, 1))
    return pieces + others


def on_device(
    user_size,
    pool_size,
    item_feats,
    w_in,
    bias_in,
    w_out,
    bilinear,
    fetch_table,
    hist_index,
    hist_len,
    route_init,
    label_index,
    label_ids,
    label_counts,
    neg_feats,
    neg_ids,
    neg_counts,
):
    outgoing, packed = select_rows(
        user_size, pool_size, fetch_table, item_feats, neg_feats, neg_ids.reshape(1, -1), neg_counts.reshape(1, -1)
    )
    apart = swap_pool(packed, pool_size, pool_size // 2)
    arrived = lax.all_to_all(
        outgoing.reshape(fetch_table.shape[0], fetch_table.shape[2], -1),
        ("pool", "user"),
        split_axis=0,
        concat_axis=0,
        tiled=True,
    )
    arrived = arrived.reshape(outgoing.shape)

    length = hist_len.reshape(1, -1)
    renumbered = functools.partial(
        renumber, cap=fetch_table.shape[2], user_size=user_size, pool_size=pool_size
    )
    onehot, first, moved, w_in = prepare(
        renumbered, hist_index, length, route_init, w_in, outgoing.shape[0]
    )
    own_neg = neg_tower(packed, apart, w_in, bias_in.reshape(1, -1), w_out)
    negs = gather_negatives(own_neg, user_size, pool_size)

    interests, vec, positive, negs[len(negs) // 2] = route(
        renumbered,
        arrived,
        w_in,
        bias_in.reshape(1, -1),
        w_out,
        bilinear,
        onehot,
        first,
        moved,
        length,
        route_init,
        label_index.reshape(1, -1),
        label_ids.reshape(1, -1),
        label_counts.reshape(1, -1),
        negs[len(negs) // 2],
    )
    away = late_masks(pool_size)
    vecs = [vec]
    for mask in away:
        vecs.append(swap_pool(vec, pool_size, mask))
    sums = negative_sums(vecs, negs)
    partition = jnp.exp(positive) + sums[0]
    for mask, one in zip(away, sums[1:]):
        partition += swap_pool(one, pool_size, mask)
    user_loss = jnp.log(partition) - positive
    return (interests, user_loss.reshape(-1))


def solution(mesh):
    both = ("user", "pool")
    in_specs = (
        P(both, None),
        P(),
        P(),
        P(),
        P(),
        P(None, both, None),
        P(both, None),
        P(both),
        P(both, None, None),
        P(both),
        P(both),
        P(both),
        P(both, None),
        P(both),
        P(both),
    )
    out_specs = (P(both, None), P(both))

    def body(*args):
        return on_device(mesh.shape["user"], mesh.shape["pool"], *args)

    return jax.shard_map(body, mesh=mesh, in_specs=in_specs, out_specs=out_specs, check_vma=False)
```

```python
import functools

import jax
import jax.numpy as jnp
from jax import lax
from jax.experimental import pallas as pl
from jax.experimental.pallas import tpu as pltpu
from jax.sharding import PartitionSpec as P


INTERESTS = 4
ITERS = 3
LANES = 128
SUB = 8
EXTRA = 16
SPLIT = 4
GROUP_USERS = 8

norm_epsilon = 1e-06
attend_scale = 8.0
logit_scale = 20.0

f32 = jnp.float32
bf16 = jnp.bfloat16
i32 = jnp.int32


INSIDE = pl.BlockSpec(memory_space=pltpu.VMEM)
OUTSIDE = pl.BlockSpec(memory_space=pltpu.HBM)
PARAMS = pltpu.CompilerParams(vmem_limit_bytes=20 << 20)


def near(array):
    return pltpu.with_memory_space_constraint(array, pltpu.VMEM)


def far(array):
    return pltpu.with_memory_space_constraint(array, pltpu.HBM)


def mm(a, b):
    return jnp.dot(a, b, preferred_element_type=f32)


def mm_nt(a, b):
    return lax.dot_general(a, b, (((1,), (1,)), ((), ())), preferred_element_type=f32)


def iota(shape, axis):
    return lax.broadcasted_iota(i32, shape, axis)


def to_column(row):
    n = row.shape[1]
    eye = iota((n, n), 0) == iota((n, n), 1)
    return jnp.sum(jnp.where(eye, row, 0.0), axis=1, keepdims=True)


def to_row(column):
    n = column.shape[0]
    eye = iota((n, n), 0) == iota((n, n), 1)
    return jnp.sum(jnp.where(eye, column, 0.0), axis=0, keepdims=True)


def id_digits(ids_row):
    low = (ids_row & 255).astype(f32)
    mid = ((ids_row >> 8) & 255).astype(f32)
    high = (ids_row >> 16).astype(f32)
    return low, mid, high


def lane_columns(columns, rows):
    lane = iota((rows, LANES), 1)
    out = jnp.zeros((rows, LANES), f32)
    for at, column in enumerate(columns):
        out = jnp.where(lane == at, column, out)
    return out


def shift_of(size):
    assert size & (size - 1) == 0
    return size.bit_length() - 1


def renumber(slot, cap, user_size, pool_size):
    block = slot >> shift_of(cap)
    place = ((block & (pool_size - 1)) << shift_of(user_size)) + (block >> shift_of(pool_size))
    return (place << shift_of(cap)) + (slot & (cap - 1))


class Copies:
    def __init__(self, source, target, sems, first, count):
        size = source.shape[0] // count
        self.copies = [
            pltpu.make_async_copy(
                source.at[pl.ds(at * size, size)],
                target.at[pl.ds(at * size, size)],
                sems.at[first + at],
            )
            for at in range(count)
        ]
        for copy in self.copies:
            copy.start()

    def wait(self):
        for copy in self.copies:
            copy.wait()


def select_kernel(
    user_size,
    pool_size,
    fetch,
    rows,
    negs,
    ids,
    counts,
    out,
    packed,
    fetch_ref,
    rows_ref,
    out_ref,
    extra_ref,
    ids_ref,
    counts_ref,
    sems,
):
    table = Copies(fetch, fetch_ref, sems, 0, 1)
    small = [Copies(ids, ids_ref, sems, 1, 1), Copies(counts, counts_ref, sems, 2, 1)]
    copy = Copies(rows, rows_ref, sems, 5, SPLIT)
    kept = negs.shape[0]
    body = pltpu.make_async_copy(negs, packed.at[pl.ds(0, kept)], sems.at[3])
    body.start()
    _, cap, blocks = fetch_ref.shape
    count = blocks * cap
    row = iota((count, blocks), 0)
    start = renumber(iota((1, blocks), 1) * cap, cap, user_size, pool_size)
    pick = jnp.where((row >= start) & (row < start + cap), 1.0, 0.0).astype(bf16)
    place = iota((count, cap), 1) == (iota((count, cap), 0) & (cap - 1))
    table.wait()
    picked = fetch_ref[0]
    high = mm_nt(pick, (picked >> 7).astype(f32).astype(bf16))
    low = mm_nt(pick, (picked & 127).astype(f32).astype(bf16))
    column = jnp.sum(jnp.where(place, high * 128.0 + low, 0.0), axis=1, keepdims=True)
    item = iota((count, rows_ref.shape[0]), 1).astype(f32)
    chosen = jnp.where(item == column, 1.0, 0.0).astype(bf16)
    for one in small:
        one.wait()
    numbers = id_digits(ids_ref[...]) + (counts_ref[...].astype(f32),)
    at = iota((EXTRA, kept), 0)
    extra = jnp.zeros((EXTRA, kept), f32)
    for line, one in enumerate(numbers):
        extra = jnp.where(at == line, one, extra)
    extra_ref[...] = jnp.zeros(extra_ref.shape, bf16)
    extra_ref[:, :kept] = extra.astype(bf16)
    tail = pltpu.make_async_copy(extra_ref, packed.at[pl.ds(kept, EXTRA)], sems.at[4])
    tail.start()
    copy.wait()
    size = count // SPLIT
    for part in range(SPLIT):
        cut = slice(part * size, (part + 1) * size)
        out_ref[cut, :] = mm(chosen[cut], rows_ref[...]).astype(bf16)
        Copies(out_ref.at[pl.ds(part * size, size)], out.at[pl.ds(part * size, size)], sems, 5 + SPLIT + part, 1)
    body.wait()
    tail.wait()
    for part in range(SPLIT):
        there = pl.ds(part * size, size)
        pltpu.make_async_copy(out_ref.at[there], out.at[there], sems.at[5 + SPLIT + part]).wait()


def select_rows(user_size, pool_size, fetch, rows, negs, ids, counts):
    blocks, _, cap = fetch.shape
    packed = (negs.shape[0] + EXTRA, negs.shape[1])
    chosen = (blocks * cap, rows.shape[1])
    return pl.pallas_call(
        functools.partial(select_kernel, user_size, pool_size),
        in_specs=[OUTSIDE] * 5,
        out_specs=[OUTSIDE, OUTSIDE],
        out_shape=[jax.ShapeDtypeStruct(chosen, bf16), jax.ShapeDtypeStruct(packed, bf16)],
        scratch_shapes=[
            pltpu.VMEM((1, cap, blocks), i32),
            pltpu.VMEM(rows.shape, bf16),
            pltpu.VMEM(chosen, bf16),
            pltpu.VMEM((EXTRA, negs.shape[1]), bf16),
            pltpu.VMEM(ids.shape, i32),
            pltpu.VMEM(counts.shape, i32),
            pltpu.SemaphoreType.DMA((5 + 2 * SPLIT,)),
        ],
        compiler_params=PARAMS,
        name="select_rows",
    )(*[far(one) for one in (fetch.transpose(1, 2, 0), rows, negs, ids, counts)])


def tower(rows_ref, w_in_ref, bias, w_out, bias_ref, out_ref, sems):
    small = Copies(bias, bias_ref, sems, 0, 1)
    large = Copies(w_out, out_ref, sems, 1, SPLIT)
    small.wait()
    total_units = w_in_ref.shape[1]
    chunk = total_units // SPLIT
    hidden = []
    for at in range(0, total_units, chunk):
        piece = mm(rows_ref[...], w_in_ref[:, at : at + chunk]) + bias_ref[:, at : at + chunk]
        hidden.append(jnp.maximum(piece, 0.0).astype(bf16))
    hidden = jnp.concatenate(hidden, axis=1)
    large.wait()
    embedding = mm(hidden, out_ref[...])
    total = jnp.sum(embedding * embedding, axis=1, keepdims=True)
    return embedding * lax.rsqrt(total + norm_epsilon)


def neg_kernel(
    own_ref, apart_ref, w_in_ref, bias, w_out, out_ref, rows_ref, bias_ref, w_out_ref, sems
):
    count = rows_ref.shape[0] // 2
    rows_ref[:count, :] = own_ref[:count, :]
    rows_ref[count:, :] = apart_ref[:count, :]
    unit = tower(rows_ref, w_in_ref, bias, w_out, bias_ref, w_out_ref, sems)
    width = unit.shape[1]
    out_ref[:width, :] = unit.T.astype(bf16)
    out_ref[width:, :count] = own_ref[count:, :count]
    out_ref[width:, count:] = apart_ref[count:, :count]


def neg_tower(own, apart, w_in, bias, w_out):
    count = own.shape[0] - EXTRA
    width = own.shape[1]
    return pl.pallas_call(
        neg_kernel,
        in_specs=[INSIDE, INSIDE, INSIDE, OUTSIDE, OUTSIDE],
        out_shape=pltpu.HBM((width + EXTRA, 2 * count), bf16),
        scratch_shapes=[
            pltpu.VMEM((2 * count, width), bf16),
            pltpu.VMEM(bias.shape, f32),
            pltpu.VMEM(w_out.shape, bf16),
            pltpu.SemaphoreType.DMA((1 + SPLIT,)),
        ],
        compiler_params=PARAMS,
        name="neg_tower",
    )(near(own), near(apart), near(w_in), far(bias), far(w_out))


def event_weights(logits, live):
    raised = [jnp.exp(one) for one in logits]
    total = functools.reduce(jnp.add, raised)
    return [(one / total * live).astype(bf16).astype(f32) for one in raised]


def scatter_weights(weights, upper, onehot_ref, slot_ref):
    users = weights[0].shape[0]
    pages = slot_ref.shape[1] // LANES
    count = pages * INTERESTS * SUB
    for group in range(users // GROUP_USERS):
        at = slice(group * GROUP_USERS, (group + 1) * GROUP_USERS)
        base = jnp.concatenate(
            [
                jnp.where(upper[at] == page, weights[k][at], 0.0)
                for page in range(pages)
                for k in range(INTERESTS)
            ],
            axis=0,
        )
        user = iota((count, 1), 0) & (GROUP_USERS - 1)
        left = jnp.concatenate(
            [
                jnp.where((user >> 1) == pair, base, 0.0).astype(bf16)
                for pair in range(GROUP_USERS // 2)
            ],
            axis=1,
        )
        both = mm(left, onehot_ref[group])
        own = jnp.where((user & 1) == 0, both[:, :LANES], both[:, LANES:])
        for page in range(pages):
            for k in range(INTERESTS):
                source = (page * INTERESTS + k) * SUB
                target = k * users + group * GROUP_USERS
                slot_ref[target : target + SUB, page * LANES : (page + 1) * LANES] = own[
                    source : source + SUB
                ]


def live_mask(length_ref, shape):
    length = to_column(length_ref[...].astype(f32))
    return jnp.where(iota(shape, 1).astype(f32) < length, 1.0, 0.0)


def prepare_kernel(
    renumbered,
    index,
    length,
    init,
    w_in,
    onehot,
    slots,
    moved,
    w_in_ref,
    index_ref,
    length_ref,
    init_ref,
    onehot_ref,
    slot_ref,
    moved_ref,
    sems,
):
    pairs = ((index, index_ref), (length, length_ref), (init, init_ref))
    copies = [Copies(*pair, sems, at, 1) for at, pair in enumerate(pairs)]
    users, events = index_ref.shape
    groups = users // GROUP_USERS
    weight = Copies(w_in, w_in_ref, sems, 5 + groups, SPLIT)
    copies[0].wait()
    index = renumbered(index_ref[...])
    moved_ref[...] = index
    back = [Copies(moved_ref, moved, sems, 3, 1)]
    upper = index >> 7
    lower = (index & (LANES - 1)).astype(f32).T
    lane_id = iota((events, LANES), 1).astype(f32)
    for group in range(groups):
        for within in range(GROUP_USERS):
            user = group * GROUP_USERS + within
            pair, side = divmod(within, 2)
            hit = jnp.where(lane_id == lower[:, user : user + 1], 1.0, 0.0).astype(bf16)
            onehot_ref[
                group, pair * events : (pair + 1) * events, side * LANES : (side + 1) * LANES
            ] = hit
        there = pl.ds(group, 1)
        back.append(Copies(onehot_ref.at[there], onehot.at[there], sems, 5 + group, 1))
    for one in copies[1:]:
        one.wait()
    live = live_mask(length_ref, index.shape)
    weights = event_weights([init_ref[:, k, :] for k in range(INTERESTS)], live)
    scatter_weights(weights, upper, onehot_ref, slot_ref)
    back.append(Copies(slot_ref, slots, sems, 4, 1))
    back.append(weight)
    for one in back:
        one.wait()


def prepare(renumbered, index, length, init, w_in, slots):
    users, events = index.shape
    groups = users // GROUP_USERS
    onehot = (groups, GROUP_USERS // 2 * events, 2 * LANES)
    first = (INTERESTS * users, slots)
    return pl.pallas_call(
        functools.partial(prepare_kernel, renumbered),
        in_specs=[OUTSIDE] * 4,
        out_specs=[OUTSIDE] * 3 + [INSIDE],
        out_shape=[
            pltpu.HBM(onehot, bf16),
            pltpu.HBM(first, f32),
            pltpu.HBM(index.shape, i32),
            pltpu.VMEM(w_in.shape, bf16),
        ],
        scratch_shapes=[
            pltpu.VMEM(index.shape, i32),
            pltpu.VMEM(length.shape, i32),
            pltpu.VMEM(init.shape, f32),
            pltpu.VMEM(onehot, bf16),
            pltpu.VMEM(first, f32),
            pltpu.VMEM(index.shape, i32),
            pltpu.SemaphoreType.DMA((5 + groups + SPLIT,)),
        ],
        compiler_params=PARAMS,
        name="prepare",
    )(far(index), far(length), far(init), far(w_in))


def route_kernel(
    renumbered,
    rows_ref,
    w_in_ref,
    bias,
    w_out,
    bilinear,
    onehot,
    first,
    index,
    length,
    init,
    label,
    ids,
    counts,
    interests_ref,
    vec_ref,
    positive_ref,
    bias_ref,
    out_ref,
    map_ref,
    onehot_ref,
    first_ref,
    index_ref,
    length_ref,
    init_ref,
    label_ref,
    ids_ref,
    counts_ref,
    slot_ref,
    sems,
):
    pairs = (
        (bilinear, map_ref),
        (first, first_ref),
        (index, index_ref),
        (length, length_ref),
        (init, init_ref),
        (label, label_ref),
        (ids, ids_ref),
        (counts, counts_ref),
    )
    start = 1 + SPLIT
    others = [Copies(*pair, sems, start + at, 1) for at, pair in enumerate(pairs)]
    unit = tower(rows_ref, w_in_ref, bias, w_out, bias_ref, out_ref, sems).astype(bf16)
    fetch = Copies(onehot, onehot_ref, sems, start + len(pairs), onehot.shape[0])
    for other in others:
        other.wait()
    mapped = mm(unit, map_ref[...]).astype(bf16)
    users, events = index_ref.shape
    slots, width = mapped.shape
    index = index_ref[...]
    upper = index >> 7
    lower = index & (LANES - 1)
    live = live_mask(length_ref, index.shape)
    logits = [init_ref[:, k, :] for k in range(INTERESTS)]
    capsules = None
    for iteration in range(ITERS):
        if iteration == 1:
            fetch.wait()
        if iteration:
            scatter_weights(event_weights(logits, live), upper, onehot_ref, slot_ref)
        slot_weights = first_ref[...] if iteration == 0 else slot_ref[...]
        coarse = slot_weights.astype(bf16)
        rest = (slot_weights - coarse.astype(f32)).astype(bf16)
        sums = mm(coarse, mapped) + mm(rest, mapped)
        norm_sq = jnp.sum(sums * sums, axis=1, keepdims=True)
        capsules = sums * (jnp.sqrt(norm_sq) / (1.0 + norm_sq))
        if iteration + 1 < ITERS:
            scores = mm_nt(capsules.astype(bf16), mapped)
            found = [[None] * (events // LANES) for _ in range(INTERESTS)]
            for part in range(events // LANES):
                rows = [[] for _ in range(INTERESTS)]
                for user in range(0, users, SUB):
                    low = lower[user : user + SUB, part * LANES : (part + 1) * LANES]
                    high = upper[user : user + SUB, part * LANES : (part + 1) * LANES]
                    for k in range(INTERESTS):
                        one = None
                        for page in range(slots // LANES):
                            piece = scores[
                                k * users + user : k * users + user + SUB,
                                page * LANES : (page + 1) * LANES,
                            ]
                            taken = jnp.take_along_axis(
                                piece, low, axis=1, mode="promise_in_bounds"
                            )
                            one = taken if one is None else jnp.where(high == page, taken, one)
                        rows[k].append(one)
                for k in range(INTERESTS):
                    found[k][part] = jnp.concatenate(rows[k], axis=0)
            for k in range(INTERESTS):
                logits[k] = logits[k] + jnp.concatenate(found[k], axis=1)
    each = [capsules[k * users : (k + 1) * users] for k in range(INTERESTS)]
    for k in range(INTERESTS):
        interests_ref[:, k * width : (k + 1) * width] = each[k]
    label = to_column(renumbered(label_ref[...]).astype(f32))
    chosen = jnp.where(iota((users, slots), 1).astype(f32) == label, 1.0, 0.0).astype(bf16)
    label_rows = mm(chosen, unit)
    raised = [
        jnp.exp(attend_scale * jnp.sum(one * label_rows, axis=1, keepdims=True)) for one in each
    ]
    total = functools.reduce(jnp.add, raised)
    user_vec = functools.reduce(jnp.add, [(r / total) * one for r, one in zip(raised, each)])
    user_vec = user_vec.astype(bf16)
    vec_ref[:, :width] = user_vec
    vec_ref[:, width:] = lane_columns([to_column(one) for one in id_digits(ids_ref[...])], users).astype(bf16)
    match = jnp.sum(user_vec.astype(f32) * label_rows, axis=1, keepdims=True)
    positive_ref[...] = logit_scale * to_row(match) - jnp.log(counts_ref[...].astype(f32))


def route(renumbered, rows, w_in, *others):
    _, _, bilinear, onehot, first, index, _, _, _, _, _ = others
    users = index.shape[0]
    width = bilinear.shape[1]
    return pl.pallas_call(
        functools.partial(route_kernel, renumbered),
        in_specs=[INSIDE] * 2 + [OUTSIDE] * len(others),
        out_shape=[
            pltpu.VMEM((users, INTERESTS * width), f32),
            pltpu.VMEM((users, width + LANES), bf16),
            pltpu.VMEM((1, users), f32),
        ],
        scratch_shapes=[pltpu.VMEM(one.shape, one.dtype) for one in others]
        + [
            pltpu.VMEM(first.shape, f32),
            pltpu.SemaphoreType.DMA((SPLIT + len(others) - 1 + onehot.shape[0],)),
        ],
        compiler_params=PARAMS,
        name="route",
    )(near(rows), near(w_in), *[far(one) for one in others])


def sums_kernel(parts, pieces, *refs):
    vec_refs = refs[:parts]
    neg_refs = refs[parts : parts + pieces]
    out_refs = refs[parts + pieces :]
    vec = jnp.concatenate([ref[...] for ref in vec_refs], axis=0)
    users = vec_refs[0].shape[0]
    width = vec.shape[1] - LANES
    digits = vec[:, width:].astype(f32)
    label_ids = digits[:, 0:1] + 256.0 * digits[:, 1:2] + 65536.0 * digits[:, 2:3]
    vec = vec[:, :width]
    total = None
    for ref in neg_refs:
        extra = ref[width:, :].astype(f32)
        ids = extra[0:1] + 256.0 * extra[1:2] + 65536.0 * extra[2:3]
        terms = jnp.exp(logit_scale * mm(vec, ref[:width, :])) * (1.0 / extra[3:4])
        terms = jnp.where(ids != label_ids, terms, 0.0)
        total = terms if total is None else total + terms
    total = to_row(jnp.sum(total, axis=1, keepdims=True))
    for part, ref in enumerate(out_refs):
        ref[...] = total[:, part * users : (part + 1) * users]


def negative_sums(vecs, negs):
    users = vecs[0].shape[0]
    return pl.pallas_call(
        functools.partial(sums_kernel, len(vecs), len(negs)),
        out_shape=[pltpu.VMEM((1, users), f32) for _ in vecs],
        compiler_params=PARAMS,
        name="negative_sums",
    )(*[near(one) for one in [*vecs, *negs]])


def swap_pool(array, size, bit):
    return lax.ppermute(array, "pool", [(at, at ^ bit) for at in range(size)])


def late_masks(pool_size):
    return range(2, pool_size // 2, 2)


def swap_user(array, size, mask):
    return lax.ppermute(array, "user", [(at, at ^ mask) for at in range(size)])


def swap_both(array, user_size, pool_size, user_mask, pool_mask):
    perm = [
        (user * pool_size + pool, (user ^ user_mask) * pool_size + (pool ^ pool_mask))
        for user in range(user_size)
        for pool in range(pool_size)
    ]
    return lax.ppermute(array, ("user", "pool"), perm)


def piece_masks(user_size):
    masks = [(user, pool) for user in range(0, user_size, 2) for pool in (0, 1)]
    return masks[:0:-1]


def gather_negatives(own, user_size, pool_size):
    pieces = [own]
    for user, pool in piece_masks(user_size):
        pieces.append(swap_both(own, user_size, pool_size, user, pool))
    others = []
    for piece in pieces:
        others.append(swap_user(piece, user_size, 1))
    return pieces + others


def on_device(
    user_size,
    pool_size,
    item_feats,
    w_in,
    bias_in,
    w_out,
    bilinear,
    fetch_table,
    hist_index,
    hist_len,
    route_init,
    label_index,
    label_ids,
    label_counts,
    neg_feats,
    neg_ids,
    neg_counts,
):
    outgoing, packed = select_rows(
        user_size, pool_size, fetch_table, item_feats, neg_feats, neg_ids.reshape(1, -1), neg_counts.reshape(1, -1)
    )
    apart = swap_pool(packed, pool_size, pool_size // 2)
    arrived = lax.all_to_all(
        outgoing.reshape(fetch_table.shape[0], fetch_table.shape[2], -1),
        ("pool", "user"),
        split_axis=0,
        concat_axis=0,
        tiled=True,
    )
    arrived = arrived.reshape(outgoing.shape)

    length = hist_len.reshape(1, -1)
    renumbered = functools.partial(
        renumber, cap=fetch_table.shape[2], user_size=user_size, pool_size=pool_size
    )
    onehot, first, moved, w_in = prepare(
        renumbered, hist_index, length, route_init, w_in, outgoing.shape[0]
    )
    own_neg = neg_tower(packed, apart, w_in, bias_in.reshape(1, -1), w_out)
    negs = gather_negatives(own_neg, user_size, pool_size)

    interests, vec, positive = route(
        renumbered,
        arrived,
        w_in,
        bias_in.reshape(1, -1),
        w_out,
        bilinear,
        onehot,
        first,
        moved,
        length,
        route_init,
        label_index.reshape(1, -1),
        label_ids.reshape(1, -1),
        label_counts.reshape(1, -1),
    )
    away = late_masks(pool_size)
    vecs = [vec]
    for mask in away:
        vecs.append(swap_pool(vec, pool_size, mask))
    sums = negative_sums(vecs, negs)
    partition = jnp.exp(positive) + sums[0]
    for mask, one in zip(away, sums[1:]):
        partition += swap_pool(one, pool_size, mask)
    user_loss = jnp.log(partition) - positive
    return (interests, user_loss.reshape(-1))


def solution(mesh):
    both = ("user", "pool")
    in_specs = (
        P(both, None),
        P(),
        P(),
        P(),
        P(),
        P(None, both, None),
        P(both, None),
        P(both),
        P(both, None, None),
        P(both),
        P(both),
        P(both),
        P(both, None),
        P(both),
        P(both),
    )
    out_specs = (P(both, None), P(both))

    def body(*args):
        return on_device(mesh.shape["user"], mesh.shape["pool"], *args)

    return jax.shard_map(body, mesh=mesh, in_specs=in_specs, out_specs=out_specs, check_vma=False)
```

```python
import functools

import jax
import jax.numpy as jnp
from jax import lax
from jax.experimental import pallas as pl
from jax.experimental.pallas import tpu as pltpu
from jax.sharding import PartitionSpec as P


INTERESTS = 4
ITERS = 3
LANES = 128
SUB = 8
EXTRA = 16
SPLIT = 4
GROUP_USERS = 8

norm_epsilon = 1e-06
attend_scale = 8.0
logit_scale = 20.0

f32 = jnp.float32
bf16 = jnp.bfloat16
i32 = jnp.int32


INSIDE = pl.BlockSpec(memory_space=pltpu.VMEM)
OUTSIDE = pl.BlockSpec(memory_space=pltpu.HBM)
PARAMS = pltpu.CompilerParams(vmem_limit_bytes=20 << 20)


def near(array):
    return pltpu.with_memory_space_constraint(array, pltpu.VMEM)


def far(array):
    return pltpu.with_memory_space_constraint(array, pltpu.HBM)


def mm(a, b):
    return jnp.dot(a, b, preferred_element_type=f32)


def mm_nt(a, b):
    return lax.dot_general(a, b, (((1,), (1,)), ((), ())), preferred_element_type=f32)


def iota(shape, axis):
    return lax.broadcasted_iota(i32, shape, axis)


def to_column(row):
    n = row.shape[1]
    eye = iota((n, n), 0) == iota((n, n), 1)
    return jnp.sum(jnp.where(eye, row, 0.0), axis=1, keepdims=True)


def to_row(column):
    n = column.shape[0]
    eye = iota((n, n), 0) == iota((n, n), 1)
    return jnp.sum(jnp.where(eye, column, 0.0), axis=0, keepdims=True)


def id_digits(ids_row):
    low = (ids_row & 255).astype(f32)
    mid = ((ids_row >> 8) & 255).astype(f32)
    high = (ids_row >> 16).astype(f32)
    return low, mid, high


def lane_columns(columns, rows):
    lane = iota((rows, LANES), 1)
    out = jnp.zeros((rows, LANES), f32)
    for at, column in enumerate(columns):
        out = jnp.where(lane == at, column, out)
    return out


def shift_of(size):
    assert size & (size - 1) == 0
    return size.bit_length() - 1


def renumber(slot, cap, user_size, pool_size):
    block = slot >> shift_of(cap)
    place = ((block & (pool_size - 1)) << shift_of(user_size)) + (block >> shift_of(pool_size))
    return (place << shift_of(cap)) + (slot & (cap - 1))


class Copies:
    def __init__(self, source, target, sems, first, count):
        size = source.shape[0] // count
        self.copies = [
            pltpu.make_async_copy(
                source.at[pl.ds(at * size, size)],
                target.at[pl.ds(at * size, size)],
                sems.at[first + at],
            )
            for at in range(count)
        ]
        for copy in self.copies:
            copy.start()

    def wait(self):
        for copy in self.copies:
            copy.wait()


def select_kernel(
    user_size,
    pool_size,
    fetch,
    rows,
    negs,
    ids,
    counts,
    out,
    packed,
    fetch_ref,
    rows_ref,
    out_ref,
    extra_ref,
    ids_ref,
    counts_ref,
    sems,
):
    table = Copies(fetch, fetch_ref, sems, 0, 1)
    small = [Copies(ids, ids_ref, sems, 1, 1), Copies(counts, counts_ref, sems, 2, 1)]
    copy = Copies(rows, rows_ref, sems, 5, SPLIT)
    kept = negs.shape[0]
    body = pltpu.make_async_copy(negs, packed.at[pl.ds(0, kept)], sems.at[3])
    body.start()
    _, cap, blocks = fetch_ref.shape
    count = blocks * cap
    row = iota((count, blocks), 0)
    start = renumber(iota((1, blocks), 1) * cap, cap, user_size, pool_size)
    pick = jnp.where((row >= start) & (row < start + cap), 1.0, 0.0).astype(bf16)
    place = iota((count, cap), 1) == (iota((count, cap), 0) & (cap - 1))
    table.wait()
    picked = fetch_ref[0]
    high = mm_nt(pick, (picked >> 7).astype(f32).astype(bf16))
    low = mm_nt(pick, (picked & 127).astype(f32).astype(bf16))
    column = jnp.sum(jnp.where(place, high * 128.0 + low, 0.0), axis=1, keepdims=True)
    item = iota((count, rows_ref.shape[0]), 1).astype(f32)
    chosen = jnp.where(item == column, 1.0, 0.0).astype(bf16)
    for one in small:
        one.wait()
    numbers = id_digits(ids_ref[...]) + (counts_ref[...].astype(f32),)
    at = iota((EXTRA, kept), 0)
    extra = jnp.zeros((EXTRA, kept), f32)
    for line, one in enumerate(numbers):
        extra = jnp.where(at == line, one, extra)
    extra_ref[...] = jnp.zeros(extra_ref.shape, bf16)
    extra_ref[:, :kept] = extra.astype(bf16)
    tail = pltpu.make_async_copy(extra_ref, packed.at[pl.ds(kept, EXTRA)], sems.at[4])
    tail.start()
    copy.wait()
    size = count // SPLIT
    for part in range(SPLIT):
        cut = slice(part * size, (part + 1) * size)
        out_ref[cut, :] = mm(chosen[cut], rows_ref[...]).astype(bf16)
        Copies(out_ref.at[pl.ds(part * size, size)], out.at[pl.ds(part * size, size)], sems, 5 + SPLIT + part, 1)
    body.wait()
    tail.wait()
    for part in range(SPLIT):
        there = pl.ds(part * size, size)
        pltpu.make_async_copy(out_ref.at[there], out.at[there], sems.at[5 + SPLIT + part]).wait()


def select_rows(user_size, pool_size, fetch, rows, negs, ids, counts):
    blocks, _, cap = fetch.shape
    packed = (negs.shape[0] + EXTRA, negs.shape[1])
    chosen = (blocks * cap, rows.shape[1])
    return pl.pallas_call(
        functools.partial(select_kernel, user_size, pool_size),
        in_specs=[OUTSIDE] * 5,
        out_specs=[OUTSIDE, OUTSIDE],
        out_shape=[jax.ShapeDtypeStruct(chosen, bf16), jax.ShapeDtypeStruct(packed, bf16)],
        scratch_shapes=[
            pltpu.VMEM((1, cap, blocks), i32),
            pltpu.VMEM(rows.shape, bf16),
            pltpu.VMEM(chosen, bf16),
            pltpu.VMEM((EXTRA, negs.shape[1]), bf16),
            pltpu.VMEM(ids.shape, i32),
            pltpu.VMEM(counts.shape, i32),
            pltpu.SemaphoreType.DMA((5 + 2 * SPLIT,)),
        ],
        compiler_params=PARAMS,
        name="select_rows",
    )(*[far(one) for one in (fetch.transpose(1, 2, 0), rows, negs, ids, counts)])


def tower(rows_ref, w_in_ref, bias, w_out, bias_ref, out_ref, sems):
    small = Copies(bias, bias_ref, sems, 0, 1)
    large = Copies(w_out, out_ref, sems, 1, SPLIT)
    small.wait()
    total_units = w_in_ref.shape[1]
    chunk = total_units // SPLIT
    hidden = []
    for at in range(0, total_units, chunk):
        piece = mm(rows_ref[...], w_in_ref[:, at : at + chunk]) + bias_ref[:, at : at + chunk]
        hidden.append(jnp.maximum(piece, 0.0).astype(bf16))
    hidden = jnp.concatenate(hidden, axis=1)
    large.wait()
    embedding = mm(hidden, out_ref[...])
    total = jnp.sum(embedding * embedding, axis=1, keepdims=True)
    return embedding * lax.rsqrt(total + norm_epsilon)


def neg_kernel(
    own_ref, apart_ref, w_in_ref, bias, w_out, out_ref, rows_ref, bias_ref, w_out_ref, sems
):
    count = rows_ref.shape[0] // 2
    rows_ref[:count, :] = own_ref[:count, :]
    rows_ref[count:, :] = apart_ref[:count, :]
    unit = tower(rows_ref, w_in_ref, bias, w_out, bias_ref, w_out_ref, sems)
    width = unit.shape[1]
    out_ref[:width, :] = unit.T.astype(bf16)
    out_ref[width:, :count] = own_ref[count:, :count]
    out_ref[width:, count:] = apart_ref[count:, :count]


def neg_tower(own, apart, w_in, bias, w_out):
    count = own.shape[0] - EXTRA
    width = own.shape[1]
    return pl.pallas_call(
        neg_kernel,
        in_specs=[INSIDE, INSIDE, INSIDE, OUTSIDE, OUTSIDE],
        out_shape=pltpu.HBM((width + EXTRA, 2 * count), bf16),
        scratch_shapes=[
            pltpu.VMEM((2 * count, width), bf16),
            pltpu.VMEM(bias.shape, f32),
            pltpu.VMEM(w_out.shape, bf16),
            pltpu.SemaphoreType.DMA((1 + SPLIT,)),
        ],
        compiler_params=PARAMS,
        name="neg_tower",
    )(near(own), near(apart), near(w_in), far(bias), far(w_out))


def event_weights(logits, live):
    raised = [jnp.exp(one) for one in logits]
    total = functools.reduce(jnp.add, raised)
    return [(one / total * live).astype(bf16).astype(f32) for one in raised]


def scatter_weights(weights, upper, onehot_ref, slot_ref):
    users = weights[0].shape[0]
    pages = slot_ref.shape[1] // LANES
    count = pages * INTERESTS * SUB
    for group in range(users // GROUP_USERS):
        at = slice(group * GROUP_USERS, (group + 1) * GROUP_USERS)
        base = jnp.concatenate(
            [
                jnp.where(upper[at] == page, weights[k][at], 0.0)
                for page in range(pages)
                for k in range(INTERESTS)
            ],
            axis=0,
        )
        user = iota((count, 1), 0) & (GROUP_USERS - 1)
        left = jnp.concatenate(
            [
                jnp.where((user >> 1) == pair, base, 0.0).astype(bf16)
                for pair in range(GROUP_USERS // 2)
            ],
            axis=1,
        )
        both = mm(left, onehot_ref[group])
        own = jnp.where((user & 1) == 0, both[:, :LANES], both[:, LANES:])
        for page in range(pages):
            for k in range(INTERESTS):
                source = (page * INTERESTS + k) * SUB
                target = k * users + group * GROUP_USERS
                slot_ref[target : target + SUB, page * LANES : (page + 1) * LANES] = own[
                    source : source + SUB
                ]


def live_mask(length_ref, shape):
    length = to_column(length_ref[...].astype(f32))
    return jnp.where(iota(shape, 1).astype(f32) < length, 1.0, 0.0)


def prepare_kernel(
    renumbered,
    index,
    length,
    init,
    w_in,
    onehot,
    slots,
    moved,
    w_in_ref,
    index_ref,
    length_ref,
    init_ref,
    onehot_ref,
    slot_ref,
    moved_ref,
    sems,
):
    pairs = ((index, index_ref), (length, length_ref), (init, init_ref))
    copies = [Copies(*pair, sems, at, 1) for at, pair in enumerate(pairs)]
    users, events = index_ref.shape
    groups = users // GROUP_USERS
    weight = Copies(w_in, w_in_ref, sems, 5 + groups, SPLIT)
    copies[0].wait()
    index = renumbered(index_ref[...])
    moved_ref[...] = index
    back = [Copies(moved_ref, moved, sems, 3, 1)]
    upper = index >> 7
    lower = (index & (LANES - 1)).astype(f32).T
    lane_id = iota((events, LANES), 1).astype(f32)
    for group in range(groups):
        for within in range(GROUP_USERS):
            user = group * GROUP_USERS + within
            pair, side = divmod(within, 2)
            hit = jnp.where(lane_id == lower[:, user : user + 1], 1.0, 0.0).astype(bf16)
            onehot_ref[
                group, pair * events : (pair + 1) * events, side * LANES : (side + 1) * LANES
            ] = hit
        there = pl.ds(group, 1)
        back.append(Copies(onehot_ref.at[there], onehot.at[there], sems, 5 + group, 1))
    for one in copies[1:]:
        one.wait()
    live = live_mask(length_ref, index.shape)
    weights = event_weights([init_ref[:, k, :] for k in range(INTERESTS)], live)
    scatter_weights(weights, upper, onehot_ref, slot_ref)
    back.append(Copies(slot_ref, slots, sems, 4, 1))
    back.append(weight)
    for one in back:
        one.wait()


def prepare(renumbered, index, length, init, w_in, slots):
    users, events = index.shape
    groups = users // GROUP_USERS
    onehot = (groups, GROUP_USERS // 2 * events, 2 * LANES)
    first = (INTERESTS * users, slots)
    return pl.pallas_call(
        functools.partial(prepare_kernel, renumbered),
        in_specs=[OUTSIDE] * 4,
        out_specs=[OUTSIDE] * 3 + [INSIDE],
        out_shape=[
            pltpu.HBM(onehot, bf16),
            pltpu.HBM(first, f32),
            pltpu.HBM(index.shape, i32),
            pltpu.VMEM(w_in.shape, bf16),
        ],
        scratch_shapes=[
            pltpu.VMEM(index.shape, i32),
            pltpu.VMEM(length.shape, i32),
            pltpu.VMEM(init.shape, f32),
            pltpu.VMEM(onehot, bf16),
            pltpu.VMEM(first, f32),
            pltpu.VMEM(index.shape, i32),
            pltpu.SemaphoreType.DMA((5 + groups + SPLIT,)),
        ],
        compiler_params=PARAMS,
        name="prepare",
    )(far(index), far(length), far(init), far(w_in))


def route_kernel(
    renumbered,
    rows_ref,
    w_in_ref,
    bias,
    w_out,
    bilinear,
    onehot,
    first,
    index,
    length,
    init,
    label,
    ids,
    counts,
    held,
    interests_ref,
    vec_ref,
    positive_ref,
    held_ref,
    bias_ref,
    out_ref,
    map_ref,
    onehot_ref,
    first_ref,
    index_ref,
    length_ref,
    init_ref,
    label_ref,
    ids_ref,
    counts_ref,
    slot_ref,
    sems,
):
    pairs = (
        (bilinear, map_ref),
        (first, first_ref),
        (index, index_ref),
        (length, length_ref),
        (init, init_ref),
        (label, label_ref),
        (ids, ids_ref),
        (counts, counts_ref),
    )
    start = 1 + SPLIT
    others = [Copies(*pair, sems, start + at, 1) for at, pair in enumerate(pairs)]
    unit = tower(rows_ref, w_in_ref, bias, w_out, bias_ref, out_ref, sems).astype(bf16)
    fetch = Copies(onehot, onehot_ref, sems, start + len(pairs), onehot.shape[0])
    keep = Copies(held, held_ref, sems, start + len(pairs) + onehot.shape[0], 1)
    for other in others:
        other.wait()
    mapped = mm(unit, map_ref[...]).astype(bf16)
    users, events = index_ref.shape
    slots, width = mapped.shape
    index = index_ref[...]
    upper = index >> 7
    lower = index & (LANES - 1)
    live = live_mask(length_ref, index.shape)
    logits = [init_ref[:, k, :] for k in range(INTERESTS)]
    capsules = None
    for iteration in range(ITERS):
        if iteration == 1:
            fetch.wait()
        if iteration:
            scatter_weights(event_weights(logits, live), upper, onehot_ref, slot_ref)
        slot_weights = first_ref[...] if iteration == 0 else slot_ref[...]
        coarse = slot_weights.astype(bf16)
        rest = (slot_weights - coarse.astype(f32)).astype(bf16)
        sums = mm(coarse, mapped) + mm(rest, mapped)
        norm_sq = jnp.sum(sums * sums, axis=1, keepdims=True)
        capsules = sums * (jnp.sqrt(norm_sq) / (1.0 + norm_sq))
        if iteration + 1 < ITERS:
            scores = mm_nt(capsules.astype(bf16), mapped)
            found = [[None] * (events // LANES) for _ in range(INTERESTS)]
            for part in range(events // LANES):
                rows = [[] for _ in range(INTERESTS)]
                for user in range(0, users, SUB):
                    low = lower[user : user + SUB, part * LANES : (part + 1) * LANES]
                    high = upper[user : user + SUB, part * LANES : (part + 1) * LANES]
                    for k in range(INTERESTS):
                        one = None
                        for page in range(slots // LANES):
                            piece = scores[
                                k * users + user : k * users + user + SUB,
                                page * LANES : (page + 1) * LANES,
                            ]
                            taken = jnp.take_along_axis(
                                piece, low, axis=1, mode="promise_in_bounds"
                            )
                            one = taken if one is None else jnp.where(high == page, taken, one)
                        rows[k].append(one)
                for k in range(INTERESTS):
                    found[k][part] = jnp.concatenate(rows[k], axis=0)
            for k in range(INTERESTS):
                logits[k] = logits[k] + jnp.concatenate(found[k], axis=1)
    each = [capsules[k * users : (k + 1) * users] for k in range(INTERESTS)]
    for k in range(INTERESTS):
        interests_ref[:, k * width : (k + 1) * width] = each[k]
    label = to_column(renumbered(label_ref[...]).astype(f32))
    chosen = jnp.where(iota((users, slots), 1).astype(f32) == label, 1.0, 0.0).astype(bf16)
    label_rows = mm(chosen, unit)
    raised = [
        jnp.exp(attend_scale * jnp.sum(one * label_rows, axis=1, keepdims=True)) for one in each
    ]
    total = functools.reduce(jnp.add, raised)
    user_vec = functools.reduce(jnp.add, [(r / total) * one for r, one in zip(raised, each)])
    user_vec = user_vec.astype(bf16)
    vec_ref[:, :width] = user_vec
    vec_ref[:, width:] = lane_columns([to_column(one) for one in id_digits(ids_ref[...])], users).astype(bf16)
    match = jnp.sum(user_vec.astype(f32) * label_rows, axis=1, keepdims=True)
    positive_ref[...] = logit_scale * to_row(match) - jnp.log(counts_ref[...].astype(f32))
    keep.wait()


def route(renumbered, rows, w_in, *others):
    bias, w_out, bilinear, onehot, first, index, *_, held = others
    users = index.shape[0]
    width = bilinear.shape[1]
    return pl.pallas_call(
        functools.partial(route_kernel, renumbered),
        in_specs=[INSIDE] * 2 + [OUTSIDE] * len(others),
        out_shape=[
            pltpu.VMEM((users, INTERESTS * width), f32),
            pltpu.VMEM((users, width + LANES), bf16),
            pltpu.VMEM((1, users), f32),
            pltpu.VMEM(held.shape, held.dtype),
        ],
        scratch_shapes=[pltpu.VMEM(one.shape, one.dtype) for one in others[:-1]]
        + [
            pltpu.VMEM(first.shape, f32),
            pltpu.SemaphoreType.DMA((SPLIT + len(others) - 1 + onehot.shape[0],)),
        ],
        compiler_params=PARAMS,
        name="route",
    )(near(rows), near(w_in), *[far(one) for one in others])


def sums_kernel(parts, pieces, *refs):
    vec_refs = refs[:parts]
    neg_refs = refs[parts : parts + pieces]
    out_refs = refs[parts + pieces :]
    vec = jnp.concatenate([ref[...] for ref in vec_refs], axis=0)
    users = vec_refs[0].shape[0]
    width = vec.shape[1] - LANES
    digits = vec[:, width:].astype(f32)
    label_ids = digits[:, 0:1] + 256.0 * digits[:, 1:2] + 65536.0 * digits[:, 2:3]
    vec = vec[:, :width]
    total = None
    for ref in neg_refs:
        extra = ref[width:, :].astype(f32)
        ids = extra[0:1] + 256.0 * extra[1:2] + 65536.0 * extra[2:3]
        terms = jnp.exp(logit_scale * mm(vec, ref[:width, :])) * (1.0 / extra[3:4])
        terms = jnp.where(ids != label_ids, terms, 0.0)
        total = terms if total is None else total + terms
    total = to_row(jnp.sum(total, axis=1, keepdims=True))
    for part, ref in enumerate(out_refs):
        ref[...] = total[:, part * users : (part + 1) * users]


def negative_sums(vecs, negs):
    users = vecs[0].shape[0]
    return pl.pallas_call(
        functools.partial(sums_kernel, len(vecs), len(negs)),
        out_shape=[pltpu.VMEM((1, users), f32) for _ in vecs],
        compiler_params=PARAMS,
        name="negative_sums",
    )(*[near(one) for one in [*vecs, *negs]])


def swap_pool(array, size, bit):
    return lax.ppermute(array, "pool", [(at, at ^ bit) for at in range(size)])


def late_masks(pool_size):
    return range(2, pool_size // 2, 2)


def swap_user(array, size, mask):
    return lax.ppermute(array, "user", [(at, at ^ mask) for at in range(size)])


def swap_both(array, user_size, pool_size, user_mask, pool_mask):
    perm = [
        (user * pool_size + pool, (user ^ user_mask) * pool_size + (pool ^ pool_mask))
        for user in range(user_size)
        for pool in range(pool_size)
    ]
    return lax.ppermute(array, ("user", "pool"), perm)


def piece_masks(user_size):
    masks = [(user, pool) for user in range(0, user_size, 2) for pool in (0, 1)]
    return masks[:0:-1]


def gather_negatives(own, user_size, pool_size):
    pieces = [own]
    for user, pool in piece_masks(user_size):
        pieces.append(swap_both(own, user_size, pool_size, user, pool))
    others = []
    for piece in pieces:
        others.append(swap_user(piece, user_size, 1))
    return pieces + others


def on_device(
    user_size,
    pool_size,
    item_feats,
    w_in,
    bias_in,
    w_out,
    bilinear,
    fetch_table,
    hist_index,
    hist_len,
    route_init,
    label_index,
    label_ids,
    label_counts,
    neg_feats,
    neg_ids,
    neg_counts,
):
    outgoing, packed = select_rows(
        user_size, pool_size, fetch_table, item_feats, neg_feats, neg_ids.reshape(1, -1), neg_counts.reshape(1, -1)
    )
    apart = swap_pool(packed, pool_size, pool_size // 2)
    arrived = lax.all_to_all(
        outgoing.reshape(fetch_table.shape[0], fetch_table.shape[2], -1),
        ("pool", "user"),
        split_axis=0,
        concat_axis=0,
        tiled=True,
    )
    arrived = arrived.reshape(outgoing.shape)

    length = hist_len.reshape(1, -1)
    renumbered = functools.partial(
        renumber, cap=fetch_table.shape[2], user_size=user_size, pool_size=pool_size
    )
    onehot, first, moved, w_in = prepare(
        renumbered, hist_index, length, route_init, w_in, outgoing.shape[0]
    )
    own_neg = neg_tower(packed, apart, w_in, bias_in.reshape(1, -1), w_out)
    negs = gather_negatives(own_neg, user_size, pool_size)

    interests, vec, positive, negs[len(negs) // 2] = route(
        renumbered,
        arrived,
        w_in,
        bias_in.reshape(1, -1),
        w_out,
        bilinear,
        onehot,
        first,
        moved,
        length,
        route_init,
        label_index.reshape(1, -1),
        label_ids.reshape(1, -1),
        label_counts.reshape(1, -1),
        negs[len(negs) // 2],
    )
    away = late_masks(pool_size)
    vecs = [vec]
    for mask in away:
        vecs.append(swap_pool(vec, pool_size, mask))
    sums = negative_sums(vecs, negs)
    partition = jnp.exp(positive) + sums[0]
    for mask, one in zip(away, sums[1:]):
        partition += swap_pool(one, pool_size, mask)
    user_loss = jnp.log(partition) - positive
    return (interests, user_loss.reshape(-1))


def solution(mesh):
    both = ("user", "pool")
    in_specs = (
        P(both, None),
        P(),
        P(),
        P(),
        P(),
        P(None, both, None),
        P(both, None),
        P(both),
        P(both, None, None),
        P(both),
        P(both),
        P(both),
        P(both, None),
        P(both),
        P(both),
    )
    out_specs = (P(both, None), P(both))

    def body(*args):
        return on_device(mesh.shape["user"], mesh.shape["pool"], *args)

    return jax.shard_map(body, mesh=mesh, in_specs=in_specs, out_specs=out_specs, check_vma=False)
```
